32 devices in a mesh: dp: 8 (over z, x), fsdp: 4 (over y, core).
Axes of the slice: x: 2, y: 2, z: 4, core: 2. Of those that a mesh axis runs over, the one named last changes fastest.
Arguments:
- frames: bfloat16 [32768, 1024], P(('dp', 'fsdp')), may hold values from -6 to 6
- segment_ids: int32 [32, 1024], P(('dp', 'fsdp')), may hold values from 0 to 3, as said below
- positions: int32 [32, 1024], P(('dp', 'fsdp')), may hold values from 0 to 1023, as said below
- cotangent: bfloat16 [32768, 1024], P(('dp', 'fsdp')), may hold values from -6 to 6
- norm1_gain: bfloat16 [1024], P(('dp', 'fsdp')), may hold values from 0.099609375 to 1.8984375
- norm1_shift: bfloat16 [1024], P(('dp', 'fsdp')), may hold values from -3 to 3
- qkv_weight: bfloat16 [1024, 3072], P('dp', 'fsdp'), may hold values from -0.1875 to 0.1875
- query_bias: bfloat16 [1024], P(('dp', 'fsdp')), may hold values from -3 to 3
- value_bias: bfloat16 [1024], P(('dp', 'fsdp')), may hold values from -3 to 3
- out_weight: bfloat16 [1024, 1024], P('dp', 'fsdp'), may hold values from -0.75 to 0.75
- out_bias: bfloat16 [1024], P(('dp', 'fsdp')), may hold values from -3 to 3
- norm2_gain: bfloat16 [1024], P(('dp', 'fsdp')), may hold values from 0.099609375 to 1.8984375
- norm2_shift: bfloat16 [1024], P(('dp', 'fsdp')), may hold values from -3 to 3
- up_weight: bfloat16 [1024, 4096], P('dp', 'fsdp'), may hold values from -0.1875 to 0.1875
- up_bias: bfloat16 [4096], P(('dp', 'fsdp')), may hold values from -3 to 3
- down_weight: bfloat16 [4096, 1024], P('dp', 'fsdp'), may hold values from -0.09375 to 0.09375
- down_bias: bfloat16 [1024], P(('dp', 'fsdp')), may hold values from -3 to 3
Outputs:
- output: bfloat16 [32768, 1024], P(('dp', 'fsdp'))
- frames_grad: bfloat16 [32768, 1024], P(('dp', 'fsdp'))
- norm1_gain_grad: float32 [1024], P(('dp', 'fsdp'))
- norm1_shift_grad: float32 [1024], P(('dp', 'fsdp'))
- qkv_weight_grad: float32 [1024, 3072], P('dp', 'fsdp')
- query_bias_grad: float32 [1024], P(('dp', 'fsdp'))
- value_bias_grad: float32 [1024], P(('dp', 'fsdp'))
- out_weight_grad: float32 [1024, 1024], P('dp', 'fsdp')
- out_bias_grad: float32 [1024], P(('dp', 'fsdp'))
- norm2_gain_grad: float32 [1024], P(('dp', 'fsdp'))
- norm2_shift_grad: float32 [1024], P(('dp', 'fsdp'))
- up_weight_grad: float32 [1024, 4096], P('dp', 'fsdp')
- up_bias_grad: float32 [4096], P(('dp', 'fsdp'))
- down_weight_grad: float32 [4096, 1024], P('dp', 'fsdp')
- down_bias_grad: float32 [1024], P(('dp', 'fsdp'))
The draws below stay inside these ranges and needn't reach their ends.
Inputs may be any that keep to these rules, and one draw needn't show every extreme that they name: `segment_ids`: within each packed row the utterance numbers start at 0 and rise by one at each utterance's start; the first packed row holds one utterance, every other row exactly four. `positions`: A position is 0 where a row or an utterance begins and one more than the position before it otherwise.
All inputs are finite; a program needn't handle non-finite values.
Results may differ from the reference program's by a relative error of at most 0.02.
Values may be sent and summed in bfloat16 or wider, within the bound.
A program may use at most 320 MiB of HBM per device.

```python
import math
import jax
import jax.numpy as jnp
from jax import lax

D = 1024
HEADS = 16
HEAD_DIM = 64
FF = 4096
ROW_LEN = 1024
ROWS = 32
TOKENS = 32768


def packed_layout(key):
    sub_key = jax.random.fold_in(key, 7)
    index = jnp.arange(ROW_LEN, dtype=jnp.int32)[None, :]
    drawn = jax.random.randint(sub_key, (ROWS, ROW_LEN), 0, 1048576)
    scores = drawn * ROW_LEN + index
    scores = jnp.where(index == 0, 2147483647, scores)
    third = -lax.top_k(-scores, 3)[0][:, 2:3]
    row_index = jnp.arange(ROWS, dtype=jnp.int32)[:, None]
    cuts = (scores <= third) & (row_index > 0)
    starts = cuts | (index == 0)
    segment = jnp.cumsum(starts.astype(jnp.int32), axis=1) - 1
    begins = lax.cummax(jnp.where(starts, index, 0), axis=1)
    return (segment.astype(jnp.int32), (index - begins).astype(jnp.int32))


def draw_segment_ids(key, part):
    return packed_layout(key)[0]


def draw_positions(key, part):
    return packed_layout(key)[1]


def spiked(array, own_key, source, target, parts, factor):
    owner, partner = [(jnp.arange(array.shape[axis_at]) // (array.shape[axis_at] // parts)).reshape([-1 if axis == axis_at else 1 for axis in range(array.ndim)]) for axis_at in (source, target)]
    chosen = jax.random.permutation(own_key, parts)[partner]
    strong = (owner == chosen) | (owner == (partner + parts // 2) % parts)
    return jnp.where(strong, factor * array, array)


def level_of(rng, dims, split, least, largest):
    loudness = 1.0
    for position, blocks in split:
        steps = jax.random.uniform(jax.random.fold_in(jax.random.fold_in(rng, 6), position), (blocks,), jnp.float32, least / len(split), largest / len(split))
        loudness = loudness * jnp.repeat(jnp.exp(steps), dims[position] // blocks).reshape((-1,) + (1,) * (len(dims) - 1 - position))
    return loudness


def centred(stream_key, dims, scale, most, cuts=(), kind=jnp.bfloat16):
    level = level_of(stream_key, dims, cuts, -0.22, 0.18) if cuts else 1.0
    values = jax.random.normal(stream_key, dims, jnp.float32) * scale * level
    return jnp.minimum(jnp.maximum(values, -most), most).astype(kind)


def noise_with(rng, shape, deviation, limit, split, heavy, kind=jnp.bfloat16):
    values = deviation * jax.random.normal(rng, shape, jnp.float32)
    if split:
        values = values * level_of(rng, shape, split, -0.22, 0.18)
    return jnp.clip(spiked(values, jax.random.fold_in(rng, 3), *heavy), -limit, limit).astype(kind)


def setup_inputs(seed: int = 0) -> dict:
    streams_of = jax.random.split(jax.random.key(seed), 18)
    return {
        "frames": centred(streams_of[0], (TOKENS, D), 1.0, 6.0, ((0, 32),)),
        "segment_ids": draw_segment_ids(jax.random.fold_in(streams_of[17], 71), 0),
        "positions": draw_positions(jax.random.fold_in(streams_of[17], 71), 0),
        "cotangent": noise_with(streams_of[3], (TOKENS, D), 1.0, 6.0, ((0, 32),), (0, 1, 32, 2.75)),
        "norm1_gain": jnp.clip(1.0 + 0.18 * jax.random.normal(streams_of[4], (D,), jnp.float32), 0.099609375, 1.8984375).astype(jnp.bfloat16),
        "norm1_shift": centred(streams_of[5], (D,), 0.5, 3.0, ((0, 32),)),
        "qkv_weight": centred(streams_of[6], (D, 3 * D), D ** -0.5, 0.1875, ((0, 8), (1, 4))),
        "query_bias": centred(streams_of[7], (D,), 0.5, 3.0, ((0, 32),)),
        "value_bias": centred(streams_of[8], (D,), 0.5, 3.0, ((0, 32),)),
        "out_weight": centred(streams_of[9], (D, D), (D // 16) ** -0.5, 0.75, ((0, 8), (1, 4))),
        "out_bias": centred(streams_of[10], (D,), 0.5, 3.0, ((0, 32),)),
        "norm2_gain": jnp.clip(1.0 + 0.18 * jax.random.normal(streams_of[11], (D,), jnp.float32), 0.099609375, 1.8984375).astype(jnp.bfloat16),
        "norm2_shift": centred(streams_of[12], (D,), 0.5, 3.0, ((0, 32),)),
        "up_weight": centred(streams_of[13], (D, FF), D ** -0.5, 0.1875, ((0, 8), (1, 4))),
        "up_bias": centred(streams_of[14], (FF,), 0.5, 3.0, ((0, 32),)),
        "down_weight": centred(streams_of[15], (FF, D), FF ** -0.5, 0.09375, ((0, 8), (1, 4))),
        "down_bias": centred(streams_of[16], (D,), 0.5, 3.0, ((0, 32),)),
    }


@jax.custom_vjp
def low(v):
    return lax.optimization_barrier(v.astype(jnp.bfloat16)).astype(jnp.float32)

@jax.custom_vjp
def low_back(v):
    return v

def low_keep(v):
    return (low(v), None)

def low_pass(kept, grad):
    return (grad,)

def back_keep(v):
    return (v, None)

def back_low(kept, grad):
    return (low(grad),)
low.defvjp(low_keep, low_pass)
low_back.defvjp(back_keep, back_low)
eps = 1e-05

def sinusoid(places, width):
    halves = jnp.arange(width // 2, dtype=jnp.float32)
    rates = jnp.exp(halves * (-2.0 * math.log(10000.0) / width))
    angles = places.astype(jnp.float32)[..., None] * rates
    return jnp.stack([jnp.sin(angles), jnp.cos(angles)], axis=-1).reshape(places.shape + (width,))

def layer_norm(values, gain, shift):
    centered = values - lax.optimization_barrier(jnp.mean(values, axis=-1, keepdims=True))
    spread = lax.optimization_barrier(jnp.mean(centered * centered, axis=-1, keepdims=True))
    return centered * lax.rsqrt(spread + eps) * gain + shift

def project(values, matrix):
    return jnp.einsum('gtd,de->gte', values, matrix, precision=lax.Precision.HIGHEST)

def forward(inputs, params, segments, places):
    gain_first, shift_first, weight_in, bias_query, bias_value, weight_out, bias_out, gain_second, shift_second, weight_up, bias_up, weight_down, bias_down = params
    count, length, width = inputs.shape
    normed_one = low(layer_norm(inputs, gain_first, shift_first))
    bias_all = jnp.concatenate([bias_query, jnp.zeros_like(bias_query), bias_value])
    projected = low(low_back(project(normed_one, weight_in) + bias_all))
    query = projected[..., :width].reshape(count, length, HEADS, HEAD_DIM)
    keys = projected[..., width:2 * width].reshape(count, length, HEADS, HEAD_DIM)
    values = projected[..., 2 * width:].reshape(count, length, HEADS, HEAD_DIM)
    scale = 1.0 / math.sqrt(HEAD_DIM)
    scores = jnp.einsum('gqhd,gkhd->ghqk', query, keys, precision=lax.Precision.HIGHEST) * scale
    scores = low_back(scores)
    allowed = (segments[:, :, None] == segments[:, None, :]) & (places[:, None, :] <= places[:, :, None])
    scores = jnp.where(allowed[:, None], scores, -1e+30)
    probs = low(jax.nn.softmax(scores, axis=-1))
    mixed = jnp.einsum('ghqk,gkhd->gqhd', probs, values, precision=lax.Precision.HIGHEST)
    mixed = low(low_back(mixed.reshape(count, length, width)))
    resid_two = inputs + low_back(project(mixed, weight_out) + bias_out)
    normed_two = low(layer_norm(resid_two, gain_second, shift_second))
    hidden = low_back(project(normed_two, weight_up) + bias_up)
    activated = low(jax.nn.gelu(hidden, approximate=False))
    return resid_two + low_back(project(activated, weight_down) + bias_down)

def reference(frames, segment_ids, positions, cotangent, norm1_gain, norm1_shift, qkv_weight, query_bias, value_bias, out_weight, out_bias, norm2_gain, norm2_shift, up_weight, up_bias, down_weight, down_bias):
    params = tuple((item.astype(jnp.float32) for item in (norm1_gain, norm1_shift, qkv_weight, query_bias, value_bias, out_weight, out_bias, norm2_gain, norm2_shift, up_weight, up_bias, down_weight, down_bias)))
    group_rows = max(1, min(ROWS, 4096 // ROW_LEN))
    count = ROWS // group_rows
    inputs = frames.astype(jnp.float32).reshape(ROWS, ROW_LEN, D) + sinusoid(positions, D)
    inputs = inputs.reshape(count, group_rows, ROW_LEN, D)
    incoming = cotangent.astype(jnp.float32).reshape(count, group_rows, ROW_LEN, D)
    segment_groups = segment_ids.reshape(count, group_rows, ROW_LEN)
    place_groups = positions.reshape(count, group_rows, ROW_LEN)

    def one_group(totals, pieces):
        group_inputs, group_cot, group_segments, group_places = pieces

        def apply(inputs_here, params_here):
            return forward(inputs_here, params_here, group_segments, group_places)
        result, pullback = jax.vjp(apply, group_inputs, params)
        input_grad, param_grads = pullback(group_cot)
        totals = jax.tree.map(jnp.add, totals, param_grads)
        return (totals, (result, input_grad))
    zeros = tuple((jnp.zeros_like(item) for item in params))
    totals, (result, input_grad) = lax.scan(one_group, zeros, (inputs, incoming, segment_groups, place_groups))
    return (result.reshape(TOKENS, D).astype(jnp.bfloat16), input_grad.reshape(TOKENS, D).astype(jnp.bfloat16), totals[0], totals[1], totals[2], totals[3], totals[4], totals[5], totals[6], totals[7], totals[8], totals[9], totals[10], totals[11], totals[12])
```

```python
from functools import partial
import math

import jax
import jax.numpy as jnp
from jax import lax
from jax.experimental import pallas as pl
from jax.experimental.pallas import tpu as pltpu
from jax.sharding import PartitionSpec as P

MESH = pl.DeviceIdType.MESH

HEADS = 16
HEAD_DIM = 64


eps = 1e-05


def sinusoid(places, width):
    halves = jnp.arange(width // 2, dtype=jnp.float32)
    rates = jnp.exp(halves * (-2.0 * math.log(10000.0) / width))
    angles = places.astype(jnp.float32)[..., None] * rates
    return jnp.stack([jnp.sin(angles), jnp.cos(angles)], axis=-1).reshape(places.shape + (width,))


def affine_norm(values, gain, shift):
    centered = values - jnp.mean(values, axis=-1, keepdims=True)
    spread = jnp.mean(centered * centered, axis=-1, keepdims=True)
    return centered * lax.rsqrt(spread + eps) * gain + shift


def grid_of(dp_count, fsdp_count):
    across = 1
    while across * across * 2 <= dp_count:
        across *= 2
    while dp_count % across:
        across //= 2
    cores = 2 if fsdp_count % 2 == 0 else 1
    return dp_count // across, across, fsdp_count // cores, cores


def gather_kernel(plan, *refs):
    dims, chunks, offsets = plan
    deep, across, down, cores = dims
    count = len(chunks)
    names = len(refs) - 9
    shards = refs[: names // 2]
    wholes = refs[names // 2 : names]
    local, z_send, z_recv, a_send, a_recv, b_send, b_recv, s_send, s_recv = refs[names:]
    outer = lax.axis_index("dp")
    inner = lax.axis_index("fsdp")
    z, x, y, c = outer // across, outer % across, inner // cores, inner % cores

    def device(zz, xx, yy, cc):
        return (zz * across + xx, yy * cores + cc)

    along_z = [device((z + k) % deep, x, y, c) for k in range(1, deep)]
    along_x = [device(z, (x + k) % across, y, c) for k in range(1, across)]
    along_y = [device(z, x, (y + k) % down, c) for k in range(1, down)]
    twin = [device(z, x, y, 1 - c)] if cores == 2 else []
    barrier = pltpu.get_barrier_semaphore()
    everyone = along_z + along_x + along_y + twin
    for peer in everyone:
        pl.semaphore_signal(barrier, inc=1, device_id=peer, device_id_type=MESH)
    pl.semaphore_wait(barrier, len(everyone))

    def block(i, zz, xx, yy, cc):
        which, rows, cols, start, size = chunks[i]
        return wholes[which].at[
            pl.ds(pl.multiple_of((zz * across + xx) * rows, 16), rows),
            pl.ds(pl.multiple_of((yy * cores + cc) * cols + start, 128), size),
        ]

    def strip(i, yy, cc):
        which, rows, cols, start, size = chunks[i]
        return wholes[which].at[
            :, pl.ds(pl.multiple_of((yy * cores + cc) * cols + start, 128), size)
        ]

    def own(i):
        which, rows, cols, start, size = chunks[i]
        return shards[which].at[:, pl.ds(start, size)]

    def copy(source, target, send, recv, peer):
        return pltpu.make_async_remote_copy(
            src_ref=source,
            dst_ref=target,
            send_sem=send,
            recv_sem=recv,
            device_id=peer,
            device_id_type=MESH,
        )

    def first(i):
        pltpu.make_async_copy(own(i), block(i, z, x, y, c), local.at[i]).start()
        for k, peer in enumerate(along_z):
            copy(own(i), block(i, z, x, y, c), z_send.at[i, k], z_recv.at[i, k], peer).start()

    def second(i):
        pltpu.make_async_copy(own(i), block(i, z, x, y, c), local.at[i]).wait()
        for k, peer in enumerate(along_z):
            landed = block(i, (z + deep - k - 1) % deep, x, y, c)
            copy(own(i), landed, z_send.at[i, k], z_recv.at[i, k], peer).wait()

        @pl.when(c == 0)
        def _():
            for k, peer in enumerate(along_x):
                for zz in range(deep):
                    piece = block(i, zz, x, y, c)
                    at = k * deep + zz
                    copy(piece, piece, a_send.at[i, at], a_recv.at[i, at], peer).start()

        @pl.when(c == 1)
        def _():
            for k, peer in enumerate(along_y):
                for zz in range(deep):
                    piece = block(i, zz, x, y, c)
                    at = k * deep + zz
                    copy(piece, piece, a_send.at[i, at], a_recv.at[i, at], peer).start()

    def third(i):
        @pl.when(c == 0)
        def _():
            for k, peer in enumerate(along_x):
                for zz in range(deep):
                    piece = block(i, zz, (x + across - k - 1) % across, y, c)
                    at = k * deep + zz
                    copy(piece, piece, a_send.at[i, at], a_recv.at[i, at], peer).wait()
            mine = strip(i, y, c)
            for k, peer in enumerate(along_y):
                copy(mine, mine, b_send.at[i, k], b_recv.at[i, k], peer).start()
            for peer in twin:
                copy(mine, mine, s_send.at[i, 0], s_recv.at[i, 0], peer).start()

        @pl.when(c == 1)
        def _():
            for k, peer in enumerate(along_y):
                for zz in range(deep):
                    piece = block(i, zz, x, (y + down - k - 1) % down, c)
                    at = k * deep + zz
                    copy(piece, piece, a_send.at[i, at], a_recv.at[i, at], peer).wait()
            for k, peer in enumerate(along_x):
                for zz in range(deep):
                    for yy in range(down):
                        piece = block(i, zz, x, yy, c)
                        at = (k * deep + zz) * down + yy
                        copy(piece, piece, b_send.at[i, at], b_recv.at[i, at], peer).start()

    def fourth(i):
        @pl.when(c == 0)
        def _():
            for k, peer in enumerate(along_y):
                landed = strip(i, (y + down - k - 1) % down, c)
                copy(landed, landed, b_send.at[i, k], b_recv.at[i, k], peer).wait()
                for other in twin:
                    copy(
                        landed, landed, s_send.at[i, k + 1], s_recv.at[i, k + 1], other
                    ).start()

        @pl.when(c == 1)
        def _():
            for k, peer in enumerate(along_x):
                for zz in range(deep):
                    for yy in range(down):
                        piece = block(i, zz, (x + across - k - 1) % across, yy, c)
                        at = (k * deep + zz) * down + yy
                        copy(piece, piece, b_send.at[i, at], b_recv.at[i, at], peer).wait()
            for k in range(down):
                piece = strip(i, (y + down - k) % down, c)
                for other in twin:
                    copy(piece, piece, s_send.at[i, k], s_recv.at[i, k], other).start()

    def fifth(i):
        for k in range(down):
            landed = strip(i, (y + down - k) % down, 1 - c)
            for other in twin:
                copy(landed, landed, s_send.at[i, k], s_recv.at[i, k], other).wait()

    stages = (first, second, third, fourth, fifth)
    for step in range(count + offsets[-1]):
        for at in reversed(range(5)):
            i = step - offsets[at]
            if 0 <= i < count:
                stages[at](i)


def gather_weights(shards):
    dp_count, fsdp_count = lax.axis_size("dp"), lax.axis_size("fsdp")
    dims = grid_of(dp_count, fsdp_count)
    deep, across, down, cores = dims
    chunks = []
    for which, shard in enumerate(shards):
        rows, cols = shard.shape
        size = cols
        if cols % 256 == 0 and rows * cols > 32768:
            size = 256 if cols > 256 else 128
        for start in range(0, cols, size):
            chunks.append((which, rows, cols, start, size))
    count = len(chunks)
    flat = max(deep * max(across, down), 1)
    return pl.pallas_call(
        partial(gather_kernel, (dims, tuple(chunks), (0, 2, 4, 6, 8))),
        out_shape=[
            jax.ShapeDtypeStruct((s.shape[0] * dp_count, s.shape[1] * fsdp_count), s.dtype)
            for s in shards
        ],
        in_specs=[pl.BlockSpec(memory_space=pl.ANY)] * len(shards),
        out_specs=[pl.BlockSpec(memory_space=pl.ANY)] * len(shards),
        scratch_shapes=[
            pltpu.SemaphoreType.DMA((count,)),
            pltpu.SemaphoreType.DMA((count, deep)),
            pltpu.SemaphoreType.DMA((count, deep)),
            pltpu.SemaphoreType.DMA((count, flat)),
            pltpu.SemaphoreType.DMA((count, flat)),
            pltpu.SemaphoreType.DMA((count, deep * across * down)),
            pltpu.SemaphoreType.DMA((count, deep * across * down)),
            pltpu.SemaphoreType.DMA((count, down)),
            pltpu.SemaphoreType.DMA((count, down)),
        ],
        compiler_params=pltpu.CompilerParams(collective_id=0, has_side_effects=True),
    )(*shards)


def collect(params):
    vectors = [item for item in params if item.ndim == 1]
    packed = jnp.concatenate(vectors)
    spread = lax.all_gather(packed, ("dp", "fsdp"), axis=0, tiled=False)
    wholes = gather_weights([params[2], params[5], params[9], params[11]])
    found = []
    start = 0
    matrices = iter(wholes)
    for item in params:
        if item.ndim == 2:
            found.append(next(matrices))
        else:
            found.append(spread[:, start : start + item.shape[0]].reshape(-1))
            start += item.shape[0]
    return tuple(found)


def spread_grads(grads):
    dp_count, fsdp_count = lax.axis_size("dp"), lax.axis_size("fsdp")
    devices = dp_count * fsdp_count
    vectors = [item.reshape(devices, -1) for item in grads if item.ndim == 1]
    widths = [item.shape[1] for item in vectors]
    packed = jnp.concatenate(vectors, axis=1)
    summed = lax.psum_scatter(packed, ("dp", "fsdp"), scatter_dimension=0, tiled=False)
    found = []
    start = 0
    for item in grads:
        if item.ndim == 2:
            rows, cols = item.shape[0] // dp_count, item.shape[1] // fsdp_count
            pieces = item.astype(jnp.bfloat16).reshape(dp_count, rows, fsdp_count, cols)
            pieces = pieces.transpose(0, 2, 1, 3).reshape(devices, rows, cols)
            owned = lax.psum_scatter(
                pieces, ("dp", "fsdp"), scatter_dimension=0, tiled=False
            )
            found.append(owned.astype(jnp.float32))
        else:
            width = item.shape[0] // devices
            found.append(summed[start : start + width])
            start += width
    return tuple(found)


def block_scores(query_part, key_part, segment_query, segment_key, place_query, place_key):
    scale = 1.0 / math.sqrt(HEAD_DIM)
    raw = (
        jnp.einsum("qhd,khd->hqk", query_part, key_part, preferred_element_type=jnp.float32) * scale
    )
    allowed = (segment_query[:, None] == segment_key[None, :]) & (
        place_key[None, :] <= place_query[:, None]
    )
    return jnp.where(allowed[None], raw, -1e30)


def body(
    frames,
    segment_ids,
    positions,
    cotangent,
    norm1_gain,
    norm1_shift,
    qkv_weight,
    query_bias,
    value_bias,
    out_weight,
    out_bias,
    norm2_gain,
    norm2_shift,
    up_weight,
    up_bias,
    down_weight,
    down_bias,
):
    params = (
        norm1_gain,
        norm1_shift,
        qkv_weight,
        query_bias,
        value_bias,
        out_weight,
        out_bias,
        norm2_gain,
        norm2_shift,
        up_weight,
        up_bias,
        down_weight,
        down_bias,
    )
    length, width = frames.shape
    heads = HEADS
    scale = 1.0 / math.sqrt(HEAD_DIM)
    block = min(512, length)
    blocks = length // block
    segment_row = segment_ids[0]
    place_row = positions[0]
    (
        gain_first,
        shift_first,
        weight_in,
        bias_query,
        bias_value,
        weight_out,
        bias_out,
        gain_second,
        shift_second,
        weight_up,
        bias_up,
        weight_down,
        bias_down,
    ) = collect(params)
    gain_one = gain_first.astype(jnp.float32)
    shift_one = shift_first.astype(jnp.float32)
    gain_two = gain_second.astype(jnp.float32)
    shift_two = shift_second.astype(jnp.float32)
    inputs = frames.astype(jnp.float32) + sinusoid(place_row, width)
    normed_one = affine_norm(inputs, gain_one, shift_one).astype(jnp.bfloat16)
    projected = jnp.dot(normed_one, weight_in, preferred_element_type=jnp.float32)
    query = (
        (projected[:, :width] + bias_query.astype(jnp.float32))
        .astype(jnp.bfloat16)
        .reshape(length, heads, HEAD_DIM)
    )
    keys = projected[:, width : 2 * width].astype(jnp.bfloat16).reshape(length, heads, HEAD_DIM)
    values = (
        (projected[:, 2 * width :] + bias_value.astype(jnp.float32))
        .astype(jnp.bfloat16)
        .reshape(length, heads, HEAD_DIM)
    )

    def rows_of(index):
        return slice(index * block, (index + 1) * block)

    def scores_for(row_block, col_block):
        rows = rows_of(row_block)
        cols = rows_of(col_block)
        return block_scores(
            query[rows],
            keys[cols],
            segment_row[rows],
            segment_row[cols],
            place_row[rows],
            place_row[cols],
        )

    log_totals = []
    attended_all = []
    for row_block in range(blocks):
        peak = jnp.full((heads, block), -1e30, jnp.float32)
        total = jnp.zeros((heads, block), jnp.float32)
        for col_block in range(row_block + 1):
            scores = scores_for(row_block, col_block)
            new_peak = jnp.maximum(peak, jnp.max(scores, axis=-1))
            total = total * jnp.exp(peak - new_peak) + jnp.sum(
                jnp.exp(scores - new_peak[..., None]), axis=-1
            )
            peak = new_peak
        log_total = peak + jnp.log(total)
        attended = jnp.zeros((block, heads, HEAD_DIM), jnp.float32)
        for col_block in range(row_block + 1):
            probs = jnp.exp(scores_for(row_block, col_block) - log_total[..., None]).astype(
                jnp.bfloat16
            )
            attended = attended + jnp.einsum(
                "hqk,khd->qhd",
                probs,
                values[rows_of(col_block)],
                preferred_element_type=jnp.float32,
            )
        log_totals.append(log_total)
        attended_all.append(attended)
    mixed = jnp.concatenate(attended_all, axis=0).reshape(length, width).astype(jnp.bfloat16)
    resid_two = (
        inputs
        + jnp.dot(mixed, weight_out, preferred_element_type=jnp.float32)
        + bias_out.astype(jnp.float32)
    )
    normed_two = affine_norm(resid_two, gain_two, shift_two).astype(jnp.bfloat16)
    hidden = jnp.dot(normed_two, weight_up, preferred_element_type=jnp.float32) + bias_up.astype(
        jnp.float32
    )
    activated = jax.nn.gelu(hidden, approximate=False).astype(jnp.bfloat16)
    result = (
        resid_two
        + jnp.dot(activated, weight_down, preferred_element_type=jnp.float32)
        + bias_down.astype(jnp.float32)
    )
    output = result.astype(jnp.bfloat16)
    grad_out = cotangent.astype(jnp.float32)
    down_grad = jnp.einsum("tf,td->fd", activated, cotangent, preferred_element_type=jnp.float32)
    down_bias_grad = jnp.sum(cotangent.astype(jnp.float32), axis=0)
    grad_act = jnp.einsum("td,fd->tf", cotangent, weight_down, preferred_element_type=jnp.float32)
    _, gelu_back = jax.vjp(partial(jax.nn.gelu, approximate=False), hidden)
    grad_hidden = gelu_back(grad_act)[0].astype(jnp.bfloat16)
    up_grad = jnp.einsum("td,tf->df", normed_two, grad_hidden, preferred_element_type=jnp.float32)
    up_bias_grad = jnp.sum(grad_hidden.astype(jnp.float32), axis=0)
    grad_normed_two = jnp.einsum(
        "tf,df->td", grad_hidden, weight_up, preferred_element_type=jnp.float32
    )
    _, norm_back_two = jax.vjp(affine_norm, resid_two, gain_two, shift_two)
    grad_resid_two, gain_two_grad, shift_two_grad = norm_back_two(grad_normed_two)
    grad_two = grad_out + grad_resid_two
    grad_branch = grad_two.astype(jnp.bfloat16)
    out_grad = jnp.einsum("to,td->od", mixed, grad_branch, preferred_element_type=jnp.float32)
    out_bias_grad = jnp.sum(grad_branch.astype(jnp.float32), axis=0)
    grad_mixed = jnp.einsum(
        "td,od->to", grad_branch, weight_out, preferred_element_type=jnp.float32
    )
    grad_mixed = grad_mixed.astype(jnp.bfloat16).reshape(length, heads, HEAD_DIM)
    grad_query = jnp.zeros((length, heads, HEAD_DIM), jnp.float32)
    grad_keys = jnp.zeros((length, heads, HEAD_DIM), jnp.float32)
    grad_values = jnp.zeros((length, heads, HEAD_DIM), jnp.float32)
    for row_block in range(blocks):
        rows = rows_of(row_block)
        grad_part = grad_mixed[rows]
        log_total = log_totals[row_block]
        delta = jnp.zeros((heads, block), jnp.float32)
        for col_block in range(row_block + 1):
            probs = jnp.exp(scores_for(row_block, col_block) - log_total[..., None])
            grad_probs = jnp.einsum(
                "qhd,khd->hqk",
                grad_part,
                values[rows_of(col_block)],
                preferred_element_type=jnp.float32,
            )
            delta = delta + jnp.sum(probs * grad_probs, axis=-1)
        for col_block in range(row_block + 1):
            cols = rows_of(col_block)
            probs = jnp.exp(scores_for(row_block, col_block) - log_total[..., None])
            grad_probs = jnp.einsum(
                "qhd,khd->hqk", grad_part, values[cols], preferred_element_type=jnp.float32
            )
            grad_scores = (probs * (grad_probs - delta[..., None])).astype(jnp.bfloat16)
            grad_values = grad_values.at[cols].add(
                jnp.einsum(
                    "hqk,qhd->khd",
                    probs.astype(jnp.bfloat16),
                    grad_part,
                    preferred_element_type=jnp.float32,
                )
            )
            grad_query = grad_query.at[rows].add(
                jnp.einsum(
                    "hqk,khd->qhd", grad_scores, keys[cols], preferred_element_type=jnp.float32
                )
                * scale
            )
            grad_keys = grad_keys.at[cols].add(
                jnp.einsum(
                    "hqk,qhd->khd", grad_scores, query[rows], preferred_element_type=jnp.float32
                )
                * scale
            )
    grad_projected = jnp.concatenate(
        [
            grad_query.reshape(length, width).astype(jnp.bfloat16),
            grad_keys.reshape(length, width).astype(jnp.bfloat16),
            grad_values.reshape(length, width).astype(jnp.bfloat16),
        ],
        axis=1,
    )
    qkv_grad = jnp.einsum(
        "td,te->de", normed_one, grad_projected, preferred_element_type=jnp.float32
    )
    query_bias_grad = jnp.sum(grad_projected[:, :width].astype(jnp.float32), axis=0)
    value_bias_grad = jnp.sum(grad_projected[:, 2 * width :].astype(jnp.float32), axis=0)
    grad_normed_one = jnp.einsum(
        "te,de->td", grad_projected, weight_in, preferred_element_type=jnp.float32
    )
    _, norm_back_one = jax.vjp(affine_norm, inputs, gain_one, shift_one)
    grad_resid_one, gain_one_grad, shift_one_grad = norm_back_one(grad_normed_one)
    frames_grad = (grad_two + grad_resid_one).astype(jnp.bfloat16)
    owned = spread_grads(
        (
            gain_one_grad,
            shift_one_grad,
            qkv_grad,
            query_bias_grad,
            value_bias_grad,
            out_grad,
            out_bias_grad,
            gain_two_grad,
            shift_two_grad,
            up_grad,
            up_bias_grad,
            down_grad,
            down_bias_grad,
        )
    )
    return (output, frames_grad) + owned


def solution(mesh):
    placed = (
        P(("dp", "fsdp"), None),
        P(("dp", "fsdp"), None),
        P(("dp", "fsdp"), None),
        P(("dp", "fsdp"), None),
        P(("dp", "fsdp")),
        P(("dp", "fsdp")),
        P("dp", "fsdp"),
        P(("dp", "fsdp")),
        P(("dp", "fsdp")),
        P("dp", "fsdp"),
        P(("dp", "fsdp")),
        P(("dp", "fsdp")),
        P(("dp", "fsdp")),
        P("dp", "fsdp"),
        P(("dp", "fsdp")),
        P("dp", "fsdp"),
        P(("dp", "fsdp")),
    )
    return jax.shard_map(
        body,
        mesh=mesh,
        in_specs=placed,
        out_specs=(
            P(("dp", "fsdp"), None),
            P(("dp", "fsdp"), None),
            P(("dp", "fsdp")),
            P(("dp", "fsdp")),
            P("dp", "fsdp"),
            P(("dp", "fsdp")),
            P(("dp", "fsdp")),
            P("dp", "fsdp"),
            P(("dp", "fsdp")),
            P(("dp", "fsdp")),
            P(("dp", "fsdp")),
            P("dp", "fsdp"),
            P(("dp", "fsdp")),
            P("dp", "fsdp"),
            P(("dp", "fsdp")),
        ),
        check_vma=False,
    )
```

```python
from functools import partial
import math

import jax
import jax.numpy as jnp
from jax import lax
from jax.experimental import pallas as pl
from jax.experimental.pallas import tpu as pltpu
from jax.sharding import PartitionSpec as P

MESH = pl.DeviceIdType.MESH

HEAD_DIM = 64


eps = 1e-05


def sinusoid(places, width):
    halves = jnp.arange(width // 2, dtype=jnp.float32)
    rates = jnp.exp(halves * (-2.0 * math.log(10000.0) / width))
    angles = places.astype(jnp.float32)[..., None] * rates
    return jnp.stack([jnp.sin(angles), jnp.cos(angles)], axis=-1).reshape(places.shape + (width,))


def standardize(values):
    centered = values - jnp.mean(values, axis=-1, keepdims=True)
    spread = jnp.mean(centered * centered, axis=-1, keepdims=True)
    rate = lax.rsqrt(spread + eps)
    return centered * rate, rate


def grid_of(dp_count, fsdp_count):
    across = 1
    while across * across * 8 <= dp_count:
        across *= 2
    while dp_count % across:
        across //= 2
    cores = 2 if fsdp_count % 2 == 0 else 1
    return dp_count // across, across, fsdp_count // cores, cores


def gather_kernel(plan, *refs):
    dims, chunks, offsets = plan
    deep, across, down, cores = dims
    count = len(chunks)
    names = len(refs) - 9
    shards = refs[: names // 2]
    wholes = refs[names // 2 : names]
    local, z_send, z_recv, a_send, a_recv, b_send, b_recv, s_send, s_recv = refs[names:]
    outer = lax.axis_index("dp")
    inner = lax.axis_index("fsdp")
    z, x, y, c = outer // across, outer % across, inner // cores, inner % cores

    def device(zz, xx, yy, cc):
        return (zz * across + xx, yy * cores + cc)

    along_z = [device((z + k) % deep, x, y, c) for k in range(1, deep)]
    along_x = [device(z, (x + k) % across, y, c) for k in range(1, across)]
    along_y = [device(z, x, (y + k) % down, c) for k in range(1, down)]
    twin = [device(z, x, y, 1 - c)] if cores == 2 else []
    barrier = pltpu.get_barrier_semaphore()
    everyone = along_z + along_x + along_y + twin
    for peer in everyone:
        pl.semaphore_signal(barrier, inc=1, device_id=peer, device_id_type=MESH)
    pl.semaphore_wait(barrier, len(everyone))

    def block(i, zz, xx, yy, cc):
        which, rows, cols, start, size = chunks[i]
        return wholes[which].at[
            pl.ds(pl.multiple_of((zz * across + xx) * rows, 16), rows),
            pl.ds(pl.multiple_of((yy * cores + cc) * cols + start, 128), size),
        ]

    def strip(i, yy, cc):
        which, rows, cols, start, size = chunks[i]
        return wholes[which].at[
            :, pl.ds(pl.multiple_of((yy * cores + cc) * cols + start, 128), size)
        ]

    def own(i):
        which, rows, cols, start, size = chunks[i]
        return shards[which].at[:, pl.ds(start, size)]

    def copy(source, target, send, recv, peer):
        return pltpu.make_async_remote_copy(
            src_ref=source,
            dst_ref=target,
            send_sem=send,
            recv_sem=recv,
            device_id=peer,
            device_id_type=MESH,
        )

    def first(i):
        pltpu.make_async_copy(own(i), block(i, z, x, y, c), local.at[i]).start()
        for k, peer in enumerate(along_z):
            copy(own(i), block(i, z, x, y, c), z_send.at[i, k], z_recv.at[i, k], peer).start()

    def second(i):
        pltpu.make_async_copy(own(i), block(i, z, x, y, c), local.at[i]).wait()
        for k, peer in enumerate(along_z):
            landed = block(i, (z + deep - k - 1) % deep, x, y, c)
            copy(own(i), landed, z_send.at[i, k], z_recv.at[i, k], peer).wait()

        @pl.when(c == 0)
        def _():
            for k, peer in enumerate(along_x):
                for zz in range(deep):
                    piece = block(i, zz, x, y, c)
                    at = k * deep + zz
                    copy(piece, piece, a_send.at[i, at], a_recv.at[i, at], peer).start()

        @pl.when(c == 1)
        def _():
            for k, peer in enumerate(along_y):
                for zz in range(deep):
                    piece = block(i, zz, x, y, c)
                    at = k * deep + zz
                    copy(piece, piece, a_send.at[i, at], a_recv.at[i, at], peer).start()

    def third(i):
        @pl.when(c == 0)
        def _():
            for k, peer in enumerate(along_x):
                for zz in range(deep):
                    piece = block(i, zz, (x + across - k - 1) % across, y, c)
                    at = k * deep + zz
                    copy(piece, piece, a_send.at[i, at], a_recv.at[i, at], peer).wait()
            mine = strip(i, y, c)
            for k, peer in enumerate(along_y):
                copy(mine, mine, b_send.at[i, k], b_recv.at[i, k], peer).start()
            for peer in twin:
                copy(mine, mine, s_send.at[i, 0], s_recv.at[i, 0], peer).start()

        @pl.when(c == 1)
        def _():
            for k, peer in enumerate(along_y):
                for zz in range(deep):
                    piece = block(i, zz, x, (y + down - k - 1) % down, c)
                    at = k * deep + zz
                    copy(piece, piece, a_send.at[i, at], a_recv.at[i, at], peer).wait()
            for k, peer in enumerate(along_x):
                for zz in range(deep):
                    for yy in range(down):
                        piece = block(i, zz, x, yy, c)
                        at = (k * deep + zz) * down + yy
                        copy(piece, piece, b_send.at[i, at], b_recv.at[i, at], peer).start()

    def fourth(i):
        @pl.when(c == 0)
        def _():
            for k, peer in enumerate(along_y):
                landed = strip(i, (y + down - k - 1) % down, c)
                copy(landed, landed, b_send.at[i, k], b_recv.at[i, k], peer).wait()
                for other in twin:
                    copy(
                        landed, landed, s_send.at[i, k + 1], s_recv.at[i, k + 1], other
                    ).start()

        @pl.when(c == 1)
        def _():
            for k, peer in enumerate(along_x):
                for zz in range(deep):
                    for yy in range(down):
                        piece = block(i, zz, (x + across - k - 1) % across, yy, c)
                        at = (k * deep + zz) * down + yy
                        copy(piece, piece, b_send.at[i, at], b_recv.at[i, at], peer).wait()
            for k in range(down):
                piece = strip(i, (y + down - k) % down, c)
                for other in twin:
                    copy(piece, piece, s_send.at[i, k], s_recv.at[i, k], other).start()

    def fifth(i):
        for k in range(down):
            landed = strip(i, (y + down - k) % down, 1 - c)
            for other in twin:
                copy(landed, landed, s_send.at[i, k], s_recv.at[i, k], other).wait()

    stages = (first, second, third, fourth, fifth)
    for step in range(count + offsets[-1]):
        for at in reversed(range(5)):
            i = step - offsets[at]
            if 0 <= i < count:
                stages[at](i)


def gather_weights(shards):
    dp_count, fsdp_count = lax.axis_size("dp"), lax.axis_size("fsdp")
    dims = grid_of(dp_count, fsdp_count)
    deep, across, down, cores = dims
    chunks = []
    for which, shard in enumerate(shards):
        rows, cols = shard.shape
        size = cols
        if cols % 256 == 0 and rows * cols > 32768:
            size = 256 if cols > 256 else 128
        for start in range(0, cols, size):
            chunks.append((which, rows, cols, start, size))
    count = len(chunks)
    flat = max(deep * max(across, down), 1)
    return pl.pallas_call(
        partial(gather_kernel, (dims, tuple(chunks), (0, 2, 4, 6, 8))),
        out_shape=[
            jax.ShapeDtypeStruct((s.shape[0] * dp_count, s.shape[1] * fsdp_count), s.dtype)
            for s in shards
        ],
        in_specs=[pl.BlockSpec(memory_space=pl.ANY)] * len(shards),
        out_specs=[pl.BlockSpec(memory_space=pl.ANY)] * len(shards),
        scratch_shapes=[
            pltpu.SemaphoreType.DMA((count,)),
            pltpu.SemaphoreType.DMA((count, deep)),
            pltpu.SemaphoreType.DMA((count, deep)),
            pltpu.SemaphoreType.DMA((count, flat)),
            pltpu.SemaphoreType.DMA((count, flat)),
            pltpu.SemaphoreType.DMA((count, deep * across * down)),
            pltpu.SemaphoreType.DMA((count, deep * across * down)),
            pltpu.SemaphoreType.DMA((count, down)),
            pltpu.SemaphoreType.DMA((count, down)),
        ],
        compiler_params=pltpu.CompilerParams(collective_id=0, has_side_effects=True),
    )(*shards)


def collect(params):
    vectors = [item for item in params if item.ndim == 1]
    packed = jnp.concatenate(vectors)
    spread = lax.all_gather(packed, ("dp", "fsdp"), axis=0, tiled=False)
    wholes = gather_weights([params[2], params[5], params[9], params[11]])
    found = []
    start = 0
    matrices = iter(wholes)
    for item in params:
        if item.ndim == 2:
            found.append(next(matrices))
        else:
            found.append(spread[:, start : start + item.shape[0]].reshape(-1))
            start += item.shape[0]
    return tuple(found)


def attend(query, keys, values, start):
    length = query.shape[0]
    block = min(256, length)
    lane = lax.broadcasted_iota(jnp.int32, (block, 2 * HEAD_DIM), 1)
    factor = math.log2(math.e) / math.sqrt(HEAD_DIM)
    parts = []
    for at in range(length // block):
        rows = slice(at * block, (at + 1) * block)
        span = (at + 1) * block
        asked = query[rows, :]
        seen = keys[:span, :]
        held = values[:span, :]
        row = at * block + lax.broadcasted_iota(jnp.int32, (block, span), 0)
        col = lax.broadcasted_iota(jnp.int32, (block, span), 1)
        allowed = (col <= row) & (col >= start[rows, :])
        found = []
        for side in range(2):
            mine = jnp.where((lane // HEAD_DIM) == side, asked, jnp.zeros_like(asked))
            scores = lax.dot_general(
                mine, seen, (((1,), (1,)), ((), ())), preferred_element_type=jnp.float32
            )
            scores = jnp.where(allowed, scores * factor, -1e30)
            weight = jnp.exp2(scores - jnp.max(scores, axis=1, keepdims=True))
            total = jnp.sum(weight, axis=1, keepdims=True)
            mixed = jnp.dot(
                weight.astype(jnp.bfloat16), held, preferred_element_type=jnp.float32
            )
            found.append(mixed / total)
        parts.append(jnp.where(lane < HEAD_DIM, found[0], found[1]).astype(jnp.bfloat16))
    return parts


def attention_kernel(query, keys, values, start, mixed):
    block = min(256, query.shape[0])
    for at, part in enumerate(attend(query, keys, values, start)):
        mixed[at * block : (at + 1) * block, :] = part


def attention(projected, start):
    length, triple = projected.shape
    width = triple // 3
    pairs = width // (2 * HEAD_DIM)
    return pl.pallas_call(
        attention_kernel,
        grid=(pairs,),
        out_shape=jax.ShapeDtypeStruct((length, width), jnp.bfloat16),
        in_specs=[
            pl.BlockSpec((length, 2 * HEAD_DIM), lambda h: (0, h)),
            pl.BlockSpec((length, 2 * HEAD_DIM), lambda h: (0, pairs + h)),
            pl.BlockSpec((length, 2 * HEAD_DIM), lambda h: (0, 2 * pairs + h)),
            pl.BlockSpec((length, 1), lambda h: (0, 0)),
        ],
        out_specs=pl.BlockSpec((length, 2 * HEAD_DIM), lambda h: (0, h)),
        name="attention",
    )(projected, projected, projected, start)


def matmul(left, right, contract):
    return lax.dot_general(
        left, right, ((contract[:1], contract[1:]), ((), ())), preferred_element_type=jnp.float32
    )


def backward_kernel(dims, *refs):
    (
        place, cot_hbm, act_hbm, slope_hbm, two_hbm, unit_two, rate_two, mixed_hbm, qkv_hbm,
        one_hbm, unit_one, rate_one, gains, in_hbm, out_hbm, up_hbm, down_hbm,
        result, owned, sums,
        grads, twin_in, a_in, b_in, z_in,
        v_own, v_hold, v_twin, v_a, v_b, v_z,
        cot, left, right, unit, wide, total, second, branch,
        load, t_send, t_recv, a_send, a_recv, b_send, b_recv, z_send, z_recv,
        v_send, v_recv,
    ) = refs
    deep, across, down, cores = dims
    side = across
    length, width = cot.shape
    hidden = wide.shape[1]
    piece, gw = owned.shape[1], owned.shape[2]
    fsdp = down * cores
    rows_each = 2 * piece
    outer = lax.axis_index("dp")
    inner = lax.axis_index("fsdp")
    z, x, y, c = outer // across, outer % across, inner // cores, inner % cores
    a = (1 - c) * x + c * y
    b = (1 - c) * y + c * x
    block = min(256, length)
    steps = length // block

    def device(zz, xx, yy, cc):
        return (zz * across + xx, yy * cores + cc)

    twin = device(z, x, y, 1 - c)

    def a_peer(k):
        to = (a + k) % side
        return device(z, (1 - c) * to + c * x, (1 - c) * y + c * to, c)

    def b_peer(k):
        to = (b + k) % side
        return device(z, (1 - c) * x + c * to, (1 - c) * to + c * y, c)

    def z_peer(k):
        return device((z + k) % deep, x, y, c)

    barrier = pltpu.get_barrier_semaphore()
    everyone = [twin]
    everyone += [a_peer(k) for k in range(1, side)] + [b_peer(k) for k in range(1, side)]
    everyone += [z_peer(k) for k in range(1, deep)]
    for peer in everyone:
        pl.semaphore_signal(barrier, inc=1, device_id=peer, device_id_type=MESH)
    pl.semaphore_wait(barrier, len(everyone))

    def copy(source, target, send, recv, peer):
        return pltpu.make_async_remote_copy(
            src_ref=source, dst_ref=target, send_sem=send, recv_sem=recv,
            device_id=peer, device_id_type=MESH,
        )

    def t_copy(i):
        return copy(
            grads.at[(i // 2) % 2, i % 2, 1 - c], twin_in.at[i], t_send.at[i], t_recv.at[i], twin
        )

    def a_copy(i, k):
        return copy(
            twin_in.at[i, (a + k) % side], a_in.at[i, k - 1],
            a_send.at[i, k - 1], a_recv.at[i, k - 1], a_peer(k),
        )

    def b_copy(i, k):
        return copy(
            a_in.at[i, 0, (b + k) % side], b_in.at[i, k - 1],
            b_send.at[i, k - 1], b_recv.at[i, k - 1], b_peer(k),
        )

    def z_copy(i, k):
        return copy(
            b_in.at[i, 0, (z + k) % deep], z_in.at[i, k - 1],
            z_send.at[i, k - 1], z_recv.at[i, k - 1], z_peer(k),
        )

    def first(i):
        t_copy(i).start()

    def second_stage(i):
        t_copy(i).wait()
        twin_in[i] = twin_in[i] + grads[(i // 2) % 2, i % 2, c]
        for k in range(1, side):
            a_copy(i, k).start()

    def third(i):
        for k in range(1, side):
            a_copy(i, k).wait()
        found = twin_in[i, a]
        for k in range(1, side):
            found = found + a_in[i, k - 1]
        a_in[i, 0] = found
        for k in range(1, side):
            b_copy(i, k).start()

    def fourth(i):
        for k in range(1, side):
            b_copy(i, k).wait()
        found = a_in[i, 0, b]
        for k in range(1, side):
            found = found + b_in[i, k - 1]
        b_in[i, 0] = found
        for k in range(1, deep):
            z_copy(i, k).start()

    def fifth(i):
        for k in range(1, deep):
            z_copy(i, k).wait()
        found = b_in[i, 0, z].astype(jnp.float32)
        for k in range(1, deep):
            found = found + z_in[i, k - 1].astype(jnp.float32)
        owned[i] = found

    stages = (first, second_stage, third, fourth, fifth)

    def advance(step, low, high):
        for at in reversed(range(5)):
            i = step - at
            if isinstance(step, int):
                if low <= i < high:
                    stages[at](i)
            else:
                @pl.when((i >= low) & (i < high))
                def _(i=i, at=at):
                    stages[at](i)

    def fetch(source, target, at):
        return pltpu.make_async_copy(source, target, load.at[at])

    def tile(ref, j):
        return ref.at[:, pl.ds(pl.multiple_of(j * width, width), width)]

    def band(ref, j):
        return ref.at[pl.ds(pl.multiple_of(j * width, width), width), :]

    def rows_at(m):
        return pl.ds(pl.multiple_of(m * block, block), block)

    def make_unit(slot, source, strip):
        @pl.loop(0, width // block)
        def _(m):
            lhs = left[rows_at(m), :]
            for f in range(fsdp):
                yy, cc = f // cores, f % cores
                found = matmul(lhs, source[:, pl.ds(strip(f), gw)], (1, 0)).astype(jnp.bfloat16)
                for q in range(block // piece):
                    owner = m * (block // rows_each) + q // 2
                    zz, xx = owner // across, owner % across
                    part = found[q * piece : (q + 1) * piece, :]
                    if cc == 0:
                        grads[slot, q % 2, 0, xx, yy, zz] = part
                    else:
                        grads[slot, q % 2, 1, yy, xx, zz] = part

    def columns(value):
        return jnp.sum(value, axis=0, keepdims=True)

    fetch(cot_hbm, cot, 0).start()
    fetch(band(act_hbm, 0), left, 1).start()
    fetch(band(down_hbm, 0), right, 2).start()
    fetch(slope_hbm, wide, 3).start()
    fetch(unit_two, unit, 4).start()
    v_own[...] = jnp.zeros_like(v_own)
    total[...] = jnp.zeros_like(total)
    fetch(cot_hbm, cot, 0).wait()

    @pl.loop(0, 4)
    def _(j):
        fetch(band(act_hbm, j), left, 1).wait()
        make_unit(j % 2, cot, lambda f: f * gw)

        @pl.when(j < 3)
        def _():
            fetch(band(act_hbm, (j + 1) % 4), left, 1).start()

        @pl.when(j == 3)
        def _():
            fetch(two_hbm, left, 1).start()

        advance(2 * j, 0, 18)
        fetch(band(down_hbm, j), right, 2).wait()

        @pl.when(j == 0)
        def _():
            fetch(slope_hbm, wide, 3).wait()

        span = pl.ds(pl.multiple_of(j * width, width), width)

        @pl.loop(0, steps)
        def _(m):
            found = matmul(cot[rows_at(m), :], right[...], (1, 1))
            found = (found * wide[rows_at(m), span].astype(jnp.float32)).astype(jnp.bfloat16)
            wide[rows_at(m), span] = found
            v_own[pl.ds(8 + j, 1), :] += columns(found.astype(jnp.float32))

        @pl.when(j < 3)
        def _():
            fetch(band(down_hbm, (j + 1) % 4), right, 2).start()

        @pl.when(j == 3)
        def _():
            fetch(tile(up_hbm, 0), right, 2).start()

        advance(2 * j + 1, 0, 18)

    fetch(two_hbm, left, 1).wait()
    each_up = hidden // fsdp

    @pl.loop(0, 4)
    def _(j):
        make_unit(j % 2, wide, lambda f: pl.multiple_of(f * each_up + j * gw, 128))
        advance(8 + 2 * j, 0, 18)
        fetch(tile(up_hbm, j), right, 2).wait()
        span = pl.ds(pl.multiple_of(j * width, width), width)

        @pl.loop(0, steps)
        def _(m):
            total[rows_at(m), :] += matmul(wide[rows_at(m), span], right[...], (1, 1))

        @pl.when(j < 3)
        def _():
            fetch(tile(up_hbm, (j + 1) % 4), right, 2).start()

        @pl.when(j == 3)
        def _():
            fetch(out_hbm, right, 2).start()

        advance(9 + 2 * j, 0, 18)

    triple = qkv_hbm.shape[1]
    packed = wide.at[:, pl.ds(0, triple)]
    fetch(mixed_hbm, left, 1).start()
    fetch(qkv_hbm, packed, 3).start()
    fetch(unit_two, unit, 4).wait()

    def norm_back(rate, gain, finish):
        @pl.loop(0, steps)
        def _(m):
            grad = total[rows_at(m), :]
            normal = unit[rows_at(m), :].astype(jnp.float32)
            scaled = grad * gain
            mean = jnp.mean(scaled, axis=1, keepdims=True)
            tilt = jnp.mean(scaled * normal, axis=1, keepdims=True)
            finish(m, grad, normal, rate[rows_at(m), :] * (scaled - mean - normal * tilt))

    def finish_two(m, grad, normal, moved):
        incoming = cot[rows_at(m), :].astype(jnp.float32)
        found = incoming + moved
        second[rows_at(m), :] = found
        low = found.astype(jnp.bfloat16)
        branch[rows_at(m), :] = low
        v_own[4:5, :] += columns(low.astype(jnp.float32))
        v_own[5:6, :] += columns(grad * normal)
        v_own[6:7, :] += columns(grad)
        v_own[7:8, :] += columns(incoming)

    norm_back(rate_two, gains[1:2, :], finish_two)
    fetch(unit_one, unit, 4).start()
    fetch(mixed_hbm, left, 1).wait()
    make_unit(0, branch, lambda f: f * gw)
    fetch(one_hbm, left, 1).start()
    advance(16, 0, 18)
    fetch(out_hbm, right, 2).wait()

    @pl.loop(0, steps)
    def _(m):
        found = matmul(branch[rows_at(m), :], right[...], (1, 1))
        branch[rows_at(m), :] = found.astype(jnp.bfloat16)

    fetch(tile(in_hbm, 0), right, 2).start()
    advance(17, 0, 18)
    fetch(qkv_hbm, packed, 3).wait()
    pairs = width // (2 * HEAD_DIM)
    scale = 1.0 / math.sqrt(HEAD_DIM)
    factor = scale * math.log2(math.e)
    lane = lax.broadcasted_iota(jnp.int32, (block, 2 * HEAD_DIM), 1)

    @pl.loop(0, pairs)
    def _(j):
        pair = 2 * HEAD_DIM
        at_q = pl.ds(pl.multiple_of(j * pair, pair), pair)
        at_k = pl.ds(pl.multiple_of(width + j * pair, pair), pair)
        at_v = pl.ds(pl.multiple_of(2 * width + j * pair, pair), pair)
        sum_q = jnp.zeros((1, pair), jnp.float32)
        for at in range(steps):
            rows = pl.ds(at * block, block)
            span = (at + 1) * block
            asked = wide[rows, at_q]
            given = branch[rows, at_q]
            seen = wide[pl.ds(0, span), at_k]
            held = wide[pl.ds(0, span), at_v]
            col = at * block + lax.broadcasted_iota(jnp.int32, (span, block), 1)
            row = lax.broadcasted_iota(jnp.int32, (span, block), 0)
            begin = at * block + lax.broadcasted_iota(jnp.int32, (1, block), 1)
            begin = begin - place[:, pl.ds(at * block, block)]
            allowed = (row <= col) & (row >= begin)
            grad_q = []
            grad_k = None
            grad_v = None
            for half in range(2):
                keep = (lane // HEAD_DIM) == half
                mine = jnp.where(keep, asked, jnp.zeros_like(asked))
                ours = jnp.where(keep, given, jnp.zeros_like(given))
                scores = matmul(seen, mine, (1, 1))
                scores = jnp.where(allowed, scores * factor, -1e30)
                probs = jnp.exp2(scores - jnp.max(scores, axis=0, keepdims=True))
                probs = probs * (1.0 / columns(probs))
                grad_p = matmul(held, ours, (1, 1))
                delta = columns(probs * grad_p)
                grad_s = (probs * (grad_p - delta)).astype(jnp.bfloat16)
                part_v = matmul(probs.astype(jnp.bfloat16), ours, (1, 0))
                part_k = matmul(grad_s, mine, (1, 0))
                grad_q.append(matmul(grad_s, seen, (0, 0)))
                grad_v = part_v if grad_v is None else grad_v + part_v
                grad_k = part_k if grad_k is None else grad_k + part_k
            found = jnp.where(lane < HEAD_DIM, grad_q[0], grad_q[1]) * scale
            found = found.astype(jnp.bfloat16)
            wide[rows, at_q] = found
            sum_q = sum_q + columns(found.astype(jnp.float32))
            if at:
                old = pl.ds(0, at * block)
                total[old, 0:pair] += grad_k[: at * block, :]
                total[old, pair : 2 * pair] += grad_v[: at * block, :]
            total[rows, 0:pair] = grad_k[at * block :, :]
            total[rows, pair : 2 * pair] = grad_v[at * block :, :]
        wide[:, at_k] = (total[:, 0:pair] * scale).astype(jnp.bfloat16)
        low = total[:, pair : 2 * pair].astype(jnp.bfloat16)
        wide[:, at_v] = low
        v_own[2:3, at_q] = sum_q
        v_own[3:4, at_q] = columns(low.astype(jnp.float32))
        advance(18 + j, 0, 18)

    total[...] = jnp.zeros_like(total)
    each_in = triple // fsdp
    fetch(one_hbm, left, 1).wait()
    for j in range(3):
        make_unit((9 + j) % 2, wide, lambda f: f * each_in + j * gw)
        advance(18 + 2 * j, 18, 24)
        if j:
            advance(18 + 2 * j + 1, 18, 24)
        else:
            advance(19, 18, 24)
    fetch(unit_one, unit, 4).wait()
    for j in range(3):
        fetch(tile(in_hbm, j), right, 2).wait()
        span = pl.ds(j * width, width)

        @pl.loop(0, steps)
        def _(m):
            total[rows_at(m), :] += matmul(wide[rows_at(m), span], right[...], (1, 1))

        if j < 2:
            fetch(tile(in_hbm, j + 1), right, 2).start()
        advance(24 + j, 18, 24)

    def finish_one(m, grad, normal, moved):
        branch[rows_at(m), :] = (second[rows_at(m), :] + moved).astype(jnp.bfloat16)
        v_own[0:1, :] += columns(grad * normal)
        v_own[1:2, :] += columns(grad)

    norm_back(rate_one, gains[0:1, :], finish_one)
    fetch(branch, result, 0).start()

    def small(source, target, at, peer):
        return copy(source, target, v_send.at[at], v_recv.at[at], peer)

    hops = [
        [(v_own, v_twin, 0, twin)],
        [(v_hold.at[0], v_a.at[k - 1], k, a_peer(k)) for k in range(1, side)],
        [(v_hold.at[1], v_b.at[k - 1], side + k - 1, b_peer(k)) for k in range(1, side)],
        [(v_hold.at[2], v_z.at[k - 1], 2 * side + k - 2, z_peer(k)) for k in range(1, deep)],
    ]
    lands = [
        lambda: [v_own[...], v_twin[...]],
        lambda: [v_hold[0]] + [v_a[k] for k in range(side - 1)],
        lambda: [v_hold[1]] + [v_b[k] for k in range(side - 1)],
        lambda: [v_hold[2]] + [v_z[k] for k in range(deep - 1)],
    ]
    for at in range(4):
        for hop in hops[at]:
            small(*hop).start()
        if at < 1:
            advance(27, 18, 24)
        for hop in hops[at]:
            small(*hop).wait()
        found = lands[at]()
        whole = found[0]
        for item in found[1:]:
            whole = whole + item
        if at < 3:
            v_hold[at] = whole
        else:
            sums[...] = whole
    fetch(branch, result, 0).wait()


def backward(place, cot, act, slope, two, unit_two, rate_two, mixed, qkv, one, unit_one,
             rate_one, gains, weights):
    dp_count, fsdp_count = lax.axis_size("dp"), lax.axis_size("fsdp")
    dims = grid_of(dp_count, fsdp_count)
    deep, across, down, cores = dims
    assert across == down and cores == 2
    length, width = cot.shape
    hidden = slope.shape[1]
    piece = width // dp_count // 2
    gw = width // fsdp_count
    count = 2 * (2 * (hidden // width) + 1 + qkv.shape[1] // width)
    any_ = pl.BlockSpec(memory_space=pl.ANY)
    vmem = pl.BlockSpec(memory_space=pltpu.VMEM)
    bf16, f32 = jnp.bfloat16, jnp.float32
    hops = 2 * side_of(dims) + deep
    return pl.pallas_call(
        partial(backward_kernel, dims),
        out_shape=[
            jax.ShapeDtypeStruct((length, width), bf16),
            jax.ShapeDtypeStruct((count, piece, gw), f32),
            jax.ShapeDtypeStruct((16, width), f32),
        ],
        in_specs=[vmem, any_, any_, any_, any_, any_, vmem, any_, any_, any_, any_, vmem, vmem]
        + [any_] * 4,
        out_specs=[any_, vmem, vmem],
        scratch_shapes=[
            pltpu.VMEM((2, 2, 2, across, down, deep, piece, gw), bf16),
            pltpu.VMEM((count, across, down, deep, piece, gw), bf16),
            pltpu.VMEM((count, across - 1, down, deep, piece, gw), bf16),
            pltpu.VMEM((count, down - 1, deep, piece, gw), bf16),
            pltpu.VMEM((count, deep - 1, piece, gw), bf16),
            pltpu.VMEM((16, width), f32),
            pltpu.VMEM((3, 16, width), f32),
            pltpu.VMEM((16, width), f32),
            pltpu.VMEM((across - 1, 16, width), f32),
            pltpu.VMEM((down - 1, 16, width), f32),
            pltpu.VMEM((deep - 1, 16, width), f32),
            pltpu.VMEM((length, width), bf16),
            pltpu.VMEM((width, width), bf16),
            pltpu.VMEM((width, width), bf16),
            pltpu.VMEM((length, width), bf16),
            pltpu.VMEM((length, hidden), bf16),
            pltpu.VMEM((length, width), f32),
            pltpu.VMEM((length, width), f32),
            pltpu.VMEM((length, width), bf16),
            pltpu.SemaphoreType.DMA((5,)),
            pltpu.SemaphoreType.DMA((count,)),
            pltpu.SemaphoreType.DMA((count,)),
            pltpu.SemaphoreType.DMA((count, across - 1)),
            pltpu.SemaphoreType.DMA((count, across - 1)),
            pltpu.SemaphoreType.DMA((count, down - 1)),
            pltpu.SemaphoreType.DMA((count, down - 1)),
            pltpu.SemaphoreType.DMA((count, deep - 1)),
            pltpu.SemaphoreType.DMA((count, deep - 1)),
            pltpu.SemaphoreType.DMA((hops,)),
            pltpu.SemaphoreType.DMA((hops,)),
        ],
        compiler_params=pltpu.CompilerParams(
            collective_id=1, has_side_effects=True, vmem_limit_bytes=67043328
        ),
        name="backward",
    )(place, cot, act, slope, two, unit_two, rate_two, mixed, qkv, one, unit_one, rate_one, gains,
      *weights)


def side_of(dims):
    return dims[1]


def pick_grads(owned, sums, width, hidden):
    dp_count, fsdp_count = lax.axis_size("dp"), lax.axis_size("fsdp")
    devices = dp_count * fsdp_count
    at = lax.axis_index("dp") * fsdp_count + lax.axis_index("fsdp")
    count, piece, gw = owned.shape
    bands = hidden // width

    def beside(part):
        groups = part.shape[0] // 2
        part = part.reshape(groups, 2 * piece, gw).transpose(1, 0, 2)
        return part.reshape(2 * piece, groups * gw)

    down = owned[: 2 * bands].reshape(bands * 2 * piece, gw)
    up = beside(owned[2 * bands : 4 * bands])
    out = owned[4 * bands : 4 * bands + 2].reshape(2 * piece, gw)
    qkv = beside(owned[4 * bands + 2 :])
    each = width // devices
    small = lax.dynamic_slice(sums[:8], (0, at * each), (8, each))
    tall = sums[8 : 8 + bands].reshape(hidden)
    tall = lax.dynamic_slice(tall, (at * (hidden // devices),), (hidden // devices,))
    return small, tall, qkv, out, up, down


def body(
    frames,
    segment_ids,
    positions,
    cotangent,
    norm1_gain,
    norm1_shift,
    qkv_weight,
    query_bias,
    value_bias,
    out_weight,
    out_bias,
    norm2_gain,
    norm2_shift,
    up_weight,
    up_bias,
    down_weight,
    down_bias,
):
    params = (
        norm1_gain,
        norm1_shift,
        qkv_weight,
        query_bias,
        value_bias,
        out_weight,
        out_bias,
        norm2_gain,
        norm2_shift,
        up_weight,
        up_bias,
        down_weight,
        down_bias,
    )
    length, width = frames.shape
    place_row = positions[0]
    (
        gain_first,
        shift_first,
        weight_in,
        bias_query,
        bias_value,
        weight_out,
        bias_out,
        gain_second,
        shift_second,
        weight_up,
        bias_up,
        weight_down,
        bias_down,
    ) = collect(params)
    gain_one = gain_first.astype(jnp.float32)
    shift_one = shift_first.astype(jnp.float32)
    gain_two = gain_second.astype(jnp.float32)
    shift_two = shift_second.astype(jnp.float32)
    inputs = frames.astype(jnp.float32) + sinusoid(place_row, width)
    unit_one, rate_one = standardize(inputs)
    normed_one = (unit_one * gain_one + shift_one).astype(jnp.bfloat16)
    projected = jnp.dot(normed_one, weight_in, preferred_element_type=jnp.float32)
    bias_all = jnp.concatenate([bias_query, jnp.zeros_like(bias_query), bias_value])
    projected = (projected + bias_all.astype(jnp.float32)).astype(jnp.bfloat16)

    start = jnp.arange(length, dtype=jnp.int32) - place_row
    mixed = attention(projected, start[:, None])
    resid_two = (
        inputs
        + jnp.dot(mixed, weight_out, preferred_element_type=jnp.float32)
        + bias_out.astype(jnp.float32)
    )
    unit_two, rate_two = standardize(resid_two)
    normed_two = (unit_two * gain_two + shift_two).astype(jnp.bfloat16)
    hidden = jnp.dot(normed_two, weight_up, preferred_element_type=jnp.float32) + bias_up.astype(
        jnp.float32
    )
    half = 0.5 + 0.5 * lax.erf(hidden * math.sqrt(0.5))
    activated = (hidden * half).astype(jnp.bfloat16)
    slope = half + hidden * jnp.exp(-0.5 * hidden * hidden) * (1.0 / math.sqrt(2.0 * math.pi))
    slope = slope.astype(jnp.bfloat16)
    result = (
        resid_two
        + jnp.dot(activated, weight_down, preferred_element_type=jnp.float32)
        + bias_down.astype(jnp.float32)
    )
    output = result.astype(jnp.bfloat16)
    many = hidden.shape[1]
    dp_count = lax.axis_size("dp")
    act = activated.T.reshape(dp_count, many // width, width // dp_count, length)
    act = act.transpose(1, 0, 2, 3).reshape(many, length)
    frames_grad, owned, sums = backward(
        positions,
        cotangent,
        act,
        slope,
        normed_two.T,
        unit_two.astype(jnp.bfloat16),
        rate_two,
        mixed.T,
        projected,
        normed_one.T,
        unit_one.astype(jnp.bfloat16),
        rate_one,
        jnp.stack([gain_one, gain_two]),
        (weight_in, weight_out, weight_up, weight_down),
    )
    small, tall, qkv_grad, out_grad, up_grad, down_grad = pick_grads(owned, sums, width, many)
    return (
        output,
        frames_grad,
        small[0],
        small[1],
        qkv_grad,
        small[2],
        small[3],
        out_grad,
        small[4],
        small[5],
        small[6],
        up_grad,
        tall,
        down_grad,
        small[7],
    )


def solution(mesh):
    placed = (
        P(("dp", "fsdp"), None),
        P(("dp", "fsdp"), None),
        P(("dp", "fsdp"), None),
        P(("dp", "fsdp"), None),
        P(("dp", "fsdp")),
        P(("dp", "fsdp")),
        P("dp", "fsdp"),
        P(("dp", "fsdp")),
        P(("dp", "fsdp")),
        P("dp", "fsdp"),
        P(("dp", "fsdp")),
        P(("dp", "fsdp")),
        P(("dp", "fsdp")),
        P("dp", "fsdp"),
        P(("dp", "fsdp")),
        P("dp", "fsdp"),
        P(("dp", "fsdp")),
    )
    return jax.shard_map(
        body,
        mesh=mesh,
        in_specs=placed,
        out_specs=(
            P(("dp", "fsdp"), None),
            P(("dp", "fsdp"), None),
            P(("dp", "fsdp")),
            P(("dp", "fsdp")),
            P("dp", "fsdp"),
            P(("dp", "fsdp")),
            P(("dp", "fsdp")),
            P("dp", "fsdp"),
            P(("dp", "fsdp")),
            P(("dp", "fsdp")),
            P(("dp", "fsdp")),
            P("dp", "fsdp"),
            P(("dp", "fsdp")),
            P("dp", "fsdp"),
            P(("dp", "fsdp")),
        ),
        check_vma=False,
    )
```

```python
from functools import partial
import math

import jax
import jax.numpy as jnp
from jax import lax
from jax.experimental import pallas as pl
from jax.experimental.pallas import tpu as pltpu
from jax.sharding import PartitionSpec as P

MESH = pl.DeviceIdType.MESH

HEAD_DIM = 64


eps = 1e-05


def grid_of(dp_count, fsdp_count):
    across = 1
    while across * across * 8 <= dp_count:
        across *= 2
    while dp_count % across:
        across //= 2
    cores = 2 if fsdp_count % 2 == 0 else 1
    return dp_count // across, across, fsdp_count // cores, cores


def forward_kernel(dims, *refs):
    (
        place, frames, vector_shard, in_shard, out_shard, up_shard, down_shard,
        result, weights, act_hbm, slope_hbm, two_hbm, unit_two, rate_two, mixed_hbm, qkv_hbm,
        one_hbm, unit_one, rate_one, vectors,
        spread, tall, stream, normed, unit, qkv, mixed, act, slope, turned, loaded,
        load, save, local, z_send, z_recv, a_send, a_recv, b_send, b_recv, s_send, s_recv,
    ) = refs
    deep, across, down, cores = dims
    side = across
    fsdp = down * cores
    dp_count = deep * across
    devices = dp_count * fsdp
    length, width = stream.shape
    hidden = act.shape[1]
    triple = qkv.shape[1]
    piece = weights.shape[4]
    rows_each = 2 * piece
    gw = width // fsdp
    each_in, each_up = triple // fsdp, hidden // fsdp
    groups_in, groups_up = triple // width, hidden // width
    units = weights.shape[0]
    count = 2 * units
    extra = count
    first_up = groups_in + 1
    first_down = first_up + groups_up
    block = min(256, length)
    steps = length // block
    outer = lax.axis_index("dp")
    inner = lax.axis_index("fsdp")
    z, x, y, c = outer // across, outer % across, inner // cores, inner % cores
    a = (1 - c) * x + c * y
    b = (1 - c) * y + c * x

    def device(zz, xx, yy, cc):
        return (zz * across + xx, yy * cores + cc)

    twin = device(z, x, y, 1 - c)

    def a_peer(k):
        to = (a + k) % side
        return device(z, (1 - c) * to + c * x, (1 - c) * y + c * to, c)

    def b_peer(k):
        to = (b + k) % side
        return device(z, (1 - c) * x + c * to, (1 - c) * to + c * y, c)

    def z_peer(k):
        return device((z + k) % deep, x, y, c)

    barrier = pltpu.get_barrier_semaphore()
    everyone = [twin]
    everyone += [a_peer(k) for k in range(1, side)] + [b_peer(k) for k in range(1, side)]
    everyone += [z_peer(k) for k in range(1, deep)]
    for peer in everyone:
        pl.semaphore_signal(barrier, inc=1, device_id=peer, device_id_type=MESH)
    pl.semaphore_wait(barrier, len(everyone))

    def copy(source, target, send, recv, peer):
        return pltpu.make_async_remote_copy(
            src_ref=source, dst_ref=target, send_sem=send, recv_sem=recv,
            device_id=peer, device_id_type=MESH,
        )

    every = slice(None)

    def view(i, zz, xx, yy, cc):
        lane = yy * cores + cc
        if isinstance(i, int) and i == extra:
            return spread.at[zz, xx, :, pl.ds(pl.multiple_of(lane * 128, 128), 128)]
        return weights.at[
            i // 2, zz, xx, i % 2, :, pl.ds(pl.multiple_of(lane * gw, 128), gw)
        ]

    def own(i):
        if i == extra:
            return vector_shard
        unit_at, half = i // 2, i % 2
        rows = pl.ds(half * piece, piece)
        if unit_at < groups_in:
            return in_shard.at[rows, pl.ds(unit_at * gw, gw)]
        if unit_at < first_up:
            return out_shard.at[rows, :]
        if unit_at < first_down:
            return up_shard.at[rows, pl.ds((unit_at - first_up) * gw, gw)]
        return down_shard.at[pl.ds((unit_at - first_down) * rows_each + half * piece, piece), :]

    def begin(i):
        mine = view(i, z, x, y, c)
        pltpu.make_async_copy(own(i), mine, local.at[i]).start()
        for k in range(1, deep):
            copy(own(i), mine, z_send.at[i, k - 1], z_recv.at[i, k - 1], z_peer(k)).start()

    def first(i):
        mine = view(i, z, x, y, c)
        pltpu.make_async_copy(mine, mine, local.at[i]).wait()
        for k in range(1, deep):
            landed = view(i, (z + deep - k) % deep, x, y, c)
            copy(mine, landed, z_send.at[i, k - 1], z_recv.at[i, k - 1], z_peer(k)).wait()
        line = view(i, every, x, y, c)
        for k in range(1, side):
            copy(line, line, a_send.at[i, k - 1], a_recv.at[i, k - 1], a_peer(k)).start()

    def second(i):
        for k in range(1, side):
            xs = (1 - c) * ((x + side - k) % side) + c * x
            ys = (1 - c) * y + c * ((y + side - k) % side)
            landed = view(i, every, xs, ys, c)
            copy(landed, landed, a_send.at[i, k - 1], a_recv.at[i, k - 1], a_peer(k)).wait()
        for k in range(1, side):
            for s in range(side):
                line = view(i, every, (1 - c) * s + c * x, (1 - c) * y + c * s, c)
                at = (k - 1) * side + s
                copy(line, line, b_send.at[i, at], b_recv.at[i, at], b_peer(k)).start()

    def third(i):
        for k in range(1, side):
            for s in range(side):
                xs = (1 - c) * s + c * ((x + side - k) % side)
                ys = (1 - c) * ((y + side - k) % side) + c * s
                landed = view(i, every, xs, ys, c)
                at = (k - 1) * side + s
                copy(landed, landed, b_send.at[i, at], b_recv.at[i, at], b_peer(k)).wait()
        for s in range(side):
            sheet = view(i, every, every, s, c)
            copy(sheet, sheet, s_send.at[i, s], s_recv.at[i, s], twin).start()

    def fourth(i):
        for s in range(side):
            sheet = view(i, every, every, s, 1 - c)
            copy(sheet, sheet, s_send.at[i, s], s_recv.at[i, s], twin).wait()

    stages = (first, second, third, fourth)

    def advance(step):
        for at in reversed(range(4)):
            i = step - at
            if isinstance(step, int):
                if 0 <= i < count:
                    stages[at](i)
            else:
                @pl.when((i >= 0) & (i < count))
                def _(i=i, at=at):
                    stages[at](i)

    def rows_at(m):
        return pl.ds(pl.multiple_of(m * block, block), block)

    def lanes(start, size):
        return pl.ds(start if isinstance(start, int) else pl.multiple_of(start, 128), size)

    def unit_load(at, slot):
        return pltpu.make_async_copy(weights.at[at], loaded.at[slot], load.at[slot])

    def matrix(slot):
        return loaded[slot].reshape(width, width)

    begin(extra)
    for i in range(count):
        begin(i)

    even = lax.broadcasted_iota(jnp.int32, (1, width), 1)
    speed = jnp.exp((even // 2).astype(jnp.float32) * (-2.0 * math.log(10000.0) / width))
    phase = (even % 2).astype(jnp.float32) * (0.5 * math.pi)
    small = min(64, block)
    for at in range(4):
        @pl.loop(0, length // 4 // small)
        def _(s):
            rows = pl.ds(pl.multiple_of(at * (length // 4) + s * small, small), small)
            angle = place[rows, :].astype(jnp.float32) * speed + phase
            stream[rows, :] = frames[rows, :].astype(jnp.float32) + jnp.sin(angle)

        stages[at](extra)
        advance(at)

    group = 128 // (width // devices)
    for tile in range(width // 128):
        found = None
        for owner in range(tile * group, (tile + 1) * group):
            dp_at, f = owner // fsdp, owner % fsdp
            part = spread[dp_at // across, dp_at % across, 0:8, f * 128 : (f + 1) * 128]
            found = part if found is None else found + part
        vectors[:, tile * 128 : (tile + 1) * 128] = found
    group = 128 // (hidden // devices)
    for tile in range(hidden // 128):
        found = None
        for owner in range(tile * group, (tile + 1) * group):
            dp_at, f = owner // fsdp, owner % fsdp
            part = spread[dp_at // across, dp_at % across, 8:16, f * 128 : (f + 1) * 128]
            found = part if found is None else found + part
        tall[:, tile * 128 : (tile + 1) * 128] = found

    def normalize(m, value, row, rate_ref):
        mean = jnp.mean(value, axis=1, keepdims=True)
        centered = value - mean
        rate = lax.rsqrt(jnp.mean(centered * centered, axis=1, keepdims=True) + eps)
        normal = centered * rate
        rate_ref[rows_at(m), :] = jnp.broadcast_to(rate, (block, 128))
        unit[rows_at(m), :] = normal.astype(jnp.bfloat16)
        found = (normal * vectors[row : row + 1, :] + vectors[row + 1 : row + 2, :])
        found = found.astype(jnp.bfloat16)
        normed[rows_at(m), :] = found
        return found

    @pl.loop(0, steps)
    def _(m):
        found = normalize(m, stream[rows_at(m), :], 0, rate_one)
        turned[0, :, rows_at(m)] = found.T

    def keep(source, target, at):
        return pltpu.make_async_copy(source, target, save.at[at])

    keep(unit, unit_one, 0).start()
    keep(turned.at[0], one_hbm, 1).start()
    advance(4)
    for g in range(groups_in):
        if g:
            advance(3 + 2 * g)
            advance(4 + 2 * g)
        unit_load(g, g % 2).start()
        unit_load(g, g % 2).wait()

        @pl.loop(0, steps)
        def _(m):
            found = jnp.dot(
                normed[rows_at(m), :], matrix(g % 2), preferred_element_type=jnp.float32
            )
            for f in range(fsdp):
                start = f * each_in + g * gw
                part = found[:, f * gw : (f + 1) * gw]
                if start < width:
                    part = part + vectors[2:3, start : start + gw]
                elif start >= 2 * width:
                    at = start - 2 * width
                    part = part + vectors[3:4, at : at + gw]
                qkv[rows_at(m), start : start + gw] = part.astype(jnp.bfloat16)

    keep(qkv, qkv_hbm, 2).start()
    pairs = width // (2 * HEAD_DIM)
    base = 2 * (groups_in - 1) + 5
    factor = math.log2(math.e) / math.sqrt(HEAD_DIM)
    lane = lax.broadcasted_iota(jnp.int32, (block, 2 * HEAD_DIM), 1)

    @pl.loop(0, pairs)
    def _(j):
        pair = 2 * HEAD_DIM
        at_q = lanes(j * pair, pair)
        at_k = lanes(width + j * pair, pair)
        at_v = lanes(2 * width + j * pair, pair)
        for at in range(steps):
            rows = pl.ds(at * block, block)
            span = (at + 1) * block
            asked = qkv[rows, at_q]
            seen = qkv[pl.ds(0, span), at_k]
            held = qkv[pl.ds(0, span), at_v]
            row = at * block + lax.broadcasted_iota(jnp.int32, (block, span), 0)
            col = lax.broadcasted_iota(jnp.int32, (block, span), 1)
            start = at * block + lax.broadcasted_iota(jnp.int32, (block, 1), 0) - place[rows, :]
            allowed = (col <= row) & (col >= start)
            found = []
            for half in range(2):
                mine = jnp.where((lane // HEAD_DIM) == half, asked, jnp.zeros_like(asked))
                scores = matmul(mine, seen, (1, 1))
                scores = jnp.where(allowed, scores * factor, -1e30)
                weight = jnp.exp2(scores - jnp.max(scores, axis=1, keepdims=True))
                whole = jnp.sum(weight, axis=1, keepdims=True)
                found.append(matmul(weight.astype(jnp.bfloat16), held, (1, 0)) / whole)
            part = jnp.where(lane < HEAD_DIM, found[0], found[1]).astype(jnp.bfloat16)
            mixed[rows, at_q] = part
            turned[1, lanes(j * pair, pair), rows] = part.T
        advance(base + j)

    keep(turned.at[1], mixed_hbm, 3).start()
    unit_load(groups_in, 0).start()
    base = base + pairs
    advance(base)
    keep(unit, unit_one, 0).wait()
    keep(turned.at[0], one_hbm, 1).wait()
    unit_load(groups_in, 0).wait()

    @pl.loop(0, steps)
    def _(m):
        found = jnp.dot(mixed[rows_at(m), :], matrix(0), preferred_element_type=jnp.float32)
        found = stream[rows_at(m), :] + found + vectors[4:5, :]
        stream[rows_at(m), :] = found
        found = normalize(m, found, 5, rate_two)
        turned[0, :, rows_at(m)] = found.T

    keep(unit, unit_two, 0).start()
    keep(turned.at[0], two_hbm, 1).start()
    advance(base + 1)
    base = base + 2

    def turned_rows(slot, g):
        moves = []
        for q in range(width // rows_each):
            f, rest = q * rows_each // gw, q * rows_each % gw
            at = f * each_up + g * gw + rest
            owner, band = at // (groups_up * rows_each), (at // rows_each) % groups_up
            target = pl.multiple_of(band * width + owner * rows_each, 16)
            moves.append(
                pltpu.make_async_copy(
                    turned.at[slot, pl.ds(q * rows_each, rows_each), :],
                    act_hbm.at[pl.ds(target, rows_each), :],
                    save.at[4 + slot],
                )
            )
        return moves

    def turned_done(slot):
        return pltpu.make_async_copy(
            turned.at[slot], act_hbm.at[pl.ds(0, width), :], save.at[4 + slot]
        )

    unit_load(first_up, 0).start()

    @pl.loop(0, groups_up)
    def _(g):
        slot = g % 2
        unit_load(first_up + g, slot).wait()

        @pl.when(g < groups_up - 1)
        def _():
            unit_load(first_up + g + 1, 1 - slot).start()

        @pl.when(g == 0)
        def _():
            keep(turned.at[0], two_hbm, 1).wait()

        @pl.when(g == 1)
        def _():
            keep(turned.at[1], mixed_hbm, 3).wait()

        @pl.when(g >= 2)
        def _():
            turned_done(slot).wait()

        @pl.loop(0, steps)
        def _(m):
            found = jnp.dot(
                normed[rows_at(m), :], matrix(slot), preferred_element_type=jnp.float32
            )
            for f in range(fsdp):
                at = lanes(f * each_up + g * gw, gw)
                pre = found[:, f * gw : (f + 1) * gw] + tall[0:1, at]
                half = 0.5 + 0.5 * lax.erf(pre * math.sqrt(0.5))
                low = (pre * half).astype(jnp.bfloat16)
                act[rows_at(m), at] = low
                bend = half + pre * jnp.exp(-0.5 * pre * pre) * (1.0 / math.sqrt(2.0 * math.pi))
                slope[rows_at(m), at] = bend.astype(jnp.bfloat16)
                turned[slot, pl.ds(f * gw, gw), rows_at(m)] = low.T

        for move in turned_rows(slot, g):
            move.start()
        advance(base + 2 * g)
        advance(base + 1 + 2 * g)

    keep(slope, slope_hbm, 6).start()
    for step in range(base + 2 * groups_up, count + 3):
        advance(step)

    def band_load(k, slot):
        moves = []
        for q in range(dp_count):
            owner, at = k * (dp_count // groups_up) + q // groups_up, q % groups_up
            moves.append(
                pltpu.make_async_copy(
                    weights.at[first_down + at, owner // across, owner % across],
                    loaded.at[slot, q // across, q % across],
                    load.at[slot],
                )
            )
        return moves

    for move in band_load(0, 0):
        move.start()

    @pl.loop(0, groups_up)
    def _(k):
        slot = k % 2
        unit_load(0, slot).wait()

        @pl.when(k < groups_up - 1)
        def _():
            for move in band_load(k + 1, 1 - slot):
                move.start()

        @pl.loop(0, steps)
        def _(m):
            stream[rows_at(m), :] += jnp.dot(
                act[rows_at(m), lanes(k * width, width)], matrix(slot),
                preferred_element_type=jnp.float32,
            )

    @pl.loop(0, steps)
    def _(m):
        normed[rows_at(m), :] = (stream[rows_at(m), :] + vectors[7:8, :]).astype(jnp.bfloat16)

    keep(normed, result, 7).start()
    keep(unit, unit_two, 0).wait()
    keep(qkv, qkv_hbm, 2).wait()
    for slot in range(2):
        turned_done(slot).wait()
    keep(slope, slope_hbm, 6).wait()
    keep(normed, result, 7).wait()


def forward(place, frames, vectors, shards):
    dp_count, fsdp_count = lax.axis_size("dp"), lax.axis_size("fsdp")
    dims = grid_of(dp_count, fsdp_count)
    deep, across, down, cores = dims
    assert across == down and cores == 2
    length, width = frames.shape
    triple = shards[0].shape[1] * fsdp_count
    hidden = shards[2].shape[1] * fsdp_count
    piece = width // dp_count // 2
    units = 2 * (hidden // width) + 1 + triple // width
    count = 2 * units
    any_ = pl.BlockSpec(memory_space=pl.ANY)
    vmem = pl.BlockSpec(memory_space=pltpu.VMEM)
    bf16, f32 = jnp.bfloat16, jnp.float32

    def shape(*sizes, kind=bf16):
        return jax.ShapeDtypeStruct(sizes, kind)

    return pl.pallas_call(
        partial(forward_kernel, dims),
        out_shape=[
            shape(length, width),
            shape(units, deep, across, 2, piece, width),
            shape(hidden, length),
            shape(length, hidden),
            shape(width, length),
            shape(length, width),
            shape(length, 128, kind=f32),
            shape(width, length),
            shape(length, triple),
            shape(width, length),
            shape(length, width),
            shape(length, 128, kind=f32),
            shape(8, width, kind=f32),
        ],
        in_specs=[vmem] * 7,
        out_specs=[any_] * 6 + [vmem] + [any_] * 4 + [vmem] * 2,
        scratch_shapes=[
            pltpu.VMEM((deep, across, 16, fsdp_count * 128), f32),
            pltpu.VMEM((8, hidden), f32),
            pltpu.VMEM((length, width), f32),
            pltpu.VMEM((length, width), bf16),
            pltpu.VMEM((length, width), bf16),
            pltpu.VMEM((length, triple), bf16),
            pltpu.VMEM((length, width), bf16),
            pltpu.VMEM((length, hidden), bf16),
            pltpu.VMEM((length, hidden), bf16),
            pltpu.VMEM((2, width, length), bf16),
            pltpu.VMEM((2, deep, across, 2, piece, width), bf16),
            pltpu.SemaphoreType.DMA((2,)),
            pltpu.SemaphoreType.DMA((8,)),
            pltpu.SemaphoreType.DMA((count + 1,)),
            pltpu.SemaphoreType.DMA((count + 1, deep - 1)),
            pltpu.SemaphoreType.DMA((count + 1, deep - 1)),
            pltpu.SemaphoreType.DMA((count + 1, across - 1)),
            pltpu.SemaphoreType.DMA((count + 1, across - 1)),
            pltpu.SemaphoreType.DMA((count + 1, (across - 1) * across)),
            pltpu.SemaphoreType.DMA((count + 1, (across - 1) * across)),
            pltpu.SemaphoreType.DMA((count + 1, down)),
            pltpu.SemaphoreType.DMA((count + 1, down)),
        ],
        compiler_params=pltpu.CompilerParams(
            collective_id=0, has_side_effects=True, vmem_limit_bytes=67043328
        ),
        name="forward",
    )(place, frames, vectors, *shards)


def place_vectors(items, up_bias):
    devices = lax.axis_size("dp") * lax.axis_size("fsdp")
    at = lax.axis_index("dp") * lax.axis_size("fsdp") + lax.axis_index("fsdp")
    lane = jnp.arange(128)

    def placed(rows):
        size = rows.shape[1]
        repeated = jnp.tile(rows.astype(jnp.float32), (1, 128 // size))
        return jnp.where((lane // size == at % (128 // size))[None], repeated, 0.0)

    packed = jnp.stack(items)
    return jnp.concatenate(
        [placed(packed), placed(up_bias[None]), jnp.zeros((7, 128), jnp.float32)]
    )


def matmul(left, right, contract):
    return lax.dot_general(
        left, right, ((contract[:1], contract[1:]), ((), ())), preferred_element_type=jnp.float32
    )


def backward_kernel(dims, *refs):
    (
        place, cot_hbm, act_hbm, slope_hbm, two_hbm, unit_two, rate_two, mixed_hbm, qkv_hbm,
        one_hbm, unit_one, rate_one, gains, weights,
        result, owned, sums,
        grads, twin_in, a_in, b_in, z_in,
        v_own, v_hold, v_twin, v_a, v_b, v_z,
        cot, left, right, unit, wide, total, second, branch,
        load, t_send, t_recv, a_send, a_recv, b_send, b_recv, z_send, z_recv,
        v_send, v_recv,
    ) = refs
    deep, across, down, cores = dims
    side = across
    length, width = cot.shape
    hidden = wide.shape[1]
    piece, gw = owned.shape[1], owned.shape[2]
    fsdp = down * cores
    rows_each = 2 * piece
    outer = lax.axis_index("dp")
    inner = lax.axis_index("fsdp")
    z, x, y, c = outer // across, outer % across, inner // cores, inner % cores
    a = (1 - c) * x + c * y
    b = (1 - c) * y + c * x
    block = min(256, length)
    steps = length // block

    def device(zz, xx, yy, cc):
        return (zz * across + xx, yy * cores + cc)

    twin = device(z, x, y, 1 - c)

    def a_peer(k):
        to = (a + k) % side
        return device(z, (1 - c) * to + c * x, (1 - c) * y + c * to, c)

    def b_peer(k):
        to = (b + k) % side
        return device(z, (1 - c) * x + c * to, (1 - c) * to + c * y, c)

    def z_peer(k):
        return device((z + k) % deep, x, y, c)

    barrier = pltpu.get_barrier_semaphore()
    everyone = [twin]
    everyone += [a_peer(k) for k in range(1, side)] + [b_peer(k) for k in range(1, side)]
    everyone += [z_peer(k) for k in range(1, deep)]
    for peer in everyone:
        pl.semaphore_signal(barrier, inc=1, device_id=peer, device_id_type=MESH)
    pl.semaphore_wait(barrier, len(everyone))

    def copy(source, target, send, recv, peer):
        return pltpu.make_async_remote_copy(
            src_ref=source, dst_ref=target, send_sem=send, recv_sem=recv,
            device_id=peer, device_id_type=MESH,
        )

    def t_copy(i):
        return copy(
            grads.at[(i // 2) % 2, i % 2, 1 - c], twin_in.at[i], t_send.at[i], t_recv.at[i], twin
        )

    def a_copy(i, k):
        return copy(
            twin_in.at[i, (a + k) % side], a_in.at[i, k - 1],
            a_send.at[i, k - 1], a_recv.at[i, k - 1], a_peer(k),
        )

    def b_copy(i, k):
        return copy(
            a_in.at[i, 0, (b + k) % side], b_in.at[i, k - 1],
            b_send.at[i, k - 1], b_recv.at[i, k - 1], b_peer(k),
        )

    def z_copy(i, k):
        return copy(
            b_in.at[i, 0, (z + k) % deep], z_in.at[i, k - 1],
            z_send.at[i, k - 1], z_recv.at[i, k - 1], z_peer(k),
        )

    def first(i):
        t_copy(i).start()

    def second_stage(i):
        t_copy(i).wait()
        twin_in[i] = twin_in[i] + grads[(i // 2) % 2, i % 2, c]
        for k in range(1, side):
            a_copy(i, k).start()

    def third(i):
        for k in range(1, side):
            a_copy(i, k).wait()
        found = twin_in[i, a]
        for k in range(1, side):
            found = found + a_in[i, k - 1]
        a_in[i, 0] = found
        for k in range(1, side):
            b_copy(i, k).start()

    def fourth(i):
        for k in range(1, side):
            b_copy(i, k).wait()
        found = a_in[i, 0, b]
        for k in range(1, side):
            found = found + b_in[i, k - 1]
        b_in[i, 0] = found
        for k in range(1, deep):
            z_copy(i, k).start()

    def fifth(i):
        for k in range(1, deep):
            z_copy(i, k).wait()
        found = b_in[i, 0, z].astype(jnp.float32)
        for k in range(1, deep):
            found = found + z_in[i, k - 1].astype(jnp.float32)
        owned[i] = found

    stages = (first, second_stage, third, fourth, fifth)

    def advance(step, low, high):
        for at in reversed(range(5)):
            i = step - at
            if isinstance(step, int):
                if low <= i < high:
                    stages[at](i)
            else:
                @pl.when((i >= low) & (i < high))
                def _(i=i, at=at):
                    stages[at](i)

    def fetch(source, target, at):
        return pltpu.make_async_copy(source, target, load.at[at])

    groups_up = hidden // width
    groups_in = qkv_hbm.shape[1] // width
    first_up = groups_in + 1
    first_down = first_up + groups_up
    dp_count = deep * across

    def down_load(j):
        moves = []
        for q in range(dp_count):
            owner, at = j * (dp_count // groups_up) + q // groups_up, q % groups_up
            moves.append(
                fetch(weights.at[first_down + at, pl.ds(2 * owner, 2)], right.at[pl.ds(2 * q, 2)], 2)
            )
        return moves

    def matrix():
        return right[...].reshape(width, width)

    def strips(rows, each, g):
        parts = []
        for f in range(fsdp):
            start = f * each + g * gw
            if not isinstance(start, int):
                start = pl.multiple_of(start, 128)
            parts.append(wide[rows, pl.ds(start, gw)])
        return jnp.concatenate(parts, axis=1)

    def band(ref, j):
        return ref.at[pl.ds(pl.multiple_of(j * width, width), width), :]

    def rows_at(m):
        return pl.ds(pl.multiple_of(m * block, block), block)

    def make_unit(slot, source, strip):
        @pl.loop(0, width // block)
        def _(m):
            lhs = left[rows_at(m), :]
            for f in range(fsdp):
                yy, cc = f // cores, f % cores
                found = matmul(lhs, source[:, pl.ds(strip(f), gw)], (1, 0)).astype(jnp.bfloat16)
                for q in range(block // piece):
                    owner = m * (block // rows_each) + q // 2
                    zz, xx = owner // across, owner % across
                    part = found[q * piece : (q + 1) * piece, :]
                    if cc == 0:
                        grads[slot, q % 2, 0, xx, yy, zz] = part
                    else:
                        grads[slot, q % 2, 1, yy, xx, zz] = part

    def columns(value):
        return jnp.sum(value, axis=0, keepdims=True)

    fetch(cot_hbm, cot, 0).start()
    fetch(band(act_hbm, 0), left, 1).start()
    for move in down_load(0):
        move.start()
    fetch(slope_hbm, wide, 3).start()
    fetch(unit_two, unit, 4).start()
    v_own[...] = jnp.zeros_like(v_own)
    total[...] = jnp.zeros_like(total)
    fetch(cot_hbm, cot, 0).wait()

    @pl.loop(0, 4)
    def _(j):
        fetch(band(act_hbm, j), left, 1).wait()
        make_unit(j % 2, cot, lambda f: f * gw)

        @pl.when(j < 3)
        def _():
            fetch(band(act_hbm, (j + 1) % 4), left, 1).start()

        @pl.when(j == 3)
        def _():
            fetch(two_hbm, left, 1).start()

        advance(2 * j, 0, 18)
        fetch(weights.at[0], right, 2).wait()

        @pl.when(j == 0)
        def _():
            fetch(slope_hbm, wide, 3).wait()

        span = pl.ds(pl.multiple_of(j * width, width), width)

        @pl.loop(0, steps)
        def _(m):
            found = matmul(cot[rows_at(m), :], matrix(), (1, 1))
            found = (found * wide[rows_at(m), span].astype(jnp.float32)).astype(jnp.bfloat16)
            wide[rows_at(m), span] = found
            v_own[pl.ds(8 + j, 1), :] += columns(found.astype(jnp.float32))

        @pl.when(j < 3)
        def _():
            for move in down_load((j + 1) % 4):
                move.start()

        @pl.when(j == 3)
        def _():
            fetch(weights.at[first_up], right, 2).start()

        advance(2 * j + 1, 0, 18)

    fetch(two_hbm, left, 1).wait()
    each_up = hidden // fsdp

    @pl.loop(0, 4)
    def _(j):
        make_unit(j % 2, wide, lambda f: pl.multiple_of(f * each_up + j * gw, 128))
        advance(8 + 2 * j, 0, 18)
        fetch(weights.at[first_up + j], right, 2).wait()

        @pl.loop(0, steps)
        def _(m):
            total[rows_at(m), :] += matmul(strips(rows_at(m), each_up, j), matrix(), (1, 1))

        @pl.when(j < 3)
        def _():
            fetch(weights.at[first_up + (j + 1) % 4], right, 2).start()

        @pl.when(j == 3)
        def _():
            fetch(weights.at[groups_in], right, 2).start()

        advance(9 + 2 * j, 0, 18)

    triple = qkv_hbm.shape[1]
    packed = wide.at[:, pl.ds(0, triple)]
    fetch(mixed_hbm, left, 1).start()
    fetch(qkv_hbm, packed, 3).start()
    fetch(unit_two, unit, 4).wait()

    def norm_back(rate, gain, finish):
        @pl.loop(0, steps)
        def _(m):
            grad = total[rows_at(m), :]
            normal = unit[rows_at(m), :].astype(jnp.float32)
            scaled = grad * gain
            mean = jnp.mean(scaled, axis=1, keepdims=True)
            tilt = jnp.mean(scaled * normal, axis=1, keepdims=True)
            finish(m, grad, normal, rate[rows_at(m), 0:1] * (scaled - mean - normal * tilt))

    def finish_two(m, grad, normal, moved):
        incoming = cot[rows_at(m), :].astype(jnp.float32)
        found = incoming + moved
        second[rows_at(m), :] = found
        low = found.astype(jnp.bfloat16)
        branch[rows_at(m), :] = low
        v_own[4:5, :] += columns(low.astype(jnp.float32))
        v_own[5:6, :] += columns(grad * normal)
        v_own[6:7, :] += columns(grad)
        v_own[7:8, :] += columns(incoming)

    norm_back(rate_two, gains[5:6, :], finish_two)
    fetch(unit_one, unit, 4).start()
    fetch(mixed_hbm, left, 1).wait()
    make_unit(0, branch, lambda f: f * gw)
    fetch(one_hbm, left, 1).start()
    advance(16, 0, 18)
    fetch(weights.at[groups_in], right, 2).wait()

    @pl.loop(0, steps)
    def _(m):
        found = matmul(branch[rows_at(m), :], matrix(), (1, 1))
        branch[rows_at(m), :] = found.astype(jnp.bfloat16)

    fetch(weights.at[0], right, 2).start()
    advance(17, 0, 18)
    fetch(qkv_hbm, packed, 3).wait()
    pairs = width // (2 * HEAD_DIM)
    scale = 1.0 / math.sqrt(HEAD_DIM)
    factor = scale * math.log2(math.e)
    lane = lax.broadcasted_iota(jnp.int32, (block, 2 * HEAD_DIM), 1)

    @pl.loop(0, pairs)
    def _(j):
        pair = 2 * HEAD_DIM
        at_q = pl.ds(pl.multiple_of(j * pair, pair), pair)
        at_k = pl.ds(pl.multiple_of(width + j * pair, pair), pair)
        at_v = pl.ds(pl.multiple_of(2 * width + j * pair, pair), pair)
        sum_q = jnp.zeros((1, pair), jnp.float32)
        for at in range(steps):
            rows = pl.ds(at * block, block)
            span = (at + 1) * block
            asked = wide[rows, at_q]
            given = branch[rows, at_q]
            seen = wide[pl.ds(0, span), at_k]
            held = wide[pl.ds(0, span), at_v]
            col = at * block + lax.broadcasted_iota(jnp.int32, (span, block), 1)
            row = lax.broadcasted_iota(jnp.int32, (span, block), 0)
            begin = at * block + lax.broadcasted_iota(jnp.int32, (1, block), 1)
            begin = begin - place[:, pl.ds(at * block, block)]
            allowed = (row <= col) & (row >= begin)
            grad_q = []
            grad_k = None
            grad_v = None
            for half in range(2):
                keep = (lane // HEAD_DIM) == half
                mine = jnp.where(keep, asked, jnp.zeros_like(asked))
                ours = jnp.where(keep, given, jnp.zeros_like(given))
                scores = matmul(seen, mine, (1, 1))
                scores = jnp.where(allowed, scores * factor, -1e30)
                probs = jnp.exp2(scores - jnp.max(scores, axis=0, keepdims=True))
                probs = probs * (1.0 / columns(probs))
                grad_p = matmul(held, ours, (1, 1))
                delta = columns(probs * grad_p)
                grad_s = (probs * (grad_p - delta)).astype(jnp.bfloat16)
                part_v = matmul(probs.astype(jnp.bfloat16), ours, (1, 0))
                part_k = matmul(grad_s, mine, (1, 0))
                grad_q.append(matmul(grad_s, seen, (0, 0)))
                grad_v = part_v if grad_v is None else grad_v + part_v
                grad_k = part_k if grad_k is None else grad_k + part_k
            found = jnp.where(lane < HEAD_DIM, grad_q[0], grad_q[1]) * scale
            found = found.astype(jnp.bfloat16)
            wide[rows, at_q] = found
            sum_q = sum_q + columns(found.astype(jnp.float32))
            if at:
                old = pl.ds(0, at * block)
                total[old, 0:pair] += grad_k[: at * block, :]
                total[old, pair : 2 * pair] += grad_v[: at * block, :]
            total[rows, 0:pair] = grad_k[at * block :, :]
            total[rows, pair : 2 * pair] = grad_v[at * block :, :]
        wide[:, at_k] = (total[:, 0:pair] * scale).astype(jnp.bfloat16)
        low = total[:, pair : 2 * pair].astype(jnp.bfloat16)
        wide[:, at_v] = low
        v_own[2:3, at_q] = sum_q
        v_own[3:4, at_q] = columns(low.astype(jnp.float32))
        advance(18 + j, 0, 18)

    total[...] = jnp.zeros_like(total)
    each_in = triple // fsdp
    fetch(one_hbm, left, 1).wait()
    for j in range(3):
        make_unit((9 + j) % 2, wide, lambda f: f * each_in + j * gw)
        advance(18 + 2 * j, 18, 24)
        if j:
            advance(18 + 2 * j + 1, 18, 24)
        else:
            advance(19, 18, 24)
    fetch(unit_one, unit, 4).wait()
    for j in range(3):
        fetch(weights.at[j], right, 2).wait()

        @pl.loop(0, steps)
        def _(m):
            total[rows_at(m), :] += matmul(strips(rows_at(m), each_in, j), matrix(), (1, 1))

        if j < 2:
            fetch(weights.at[j + 1], right, 2).start()
        advance(24 + j, 18, 24)

    def finish_one(m, grad, normal, moved):
        branch[rows_at(m), :] = (second[rows_at(m), :] + moved).astype(jnp.bfloat16)
        v_own[0:1, :] += columns(grad * normal)
        v_own[1:2, :] += columns(grad)

    norm_back(rate_one, gains[0:1, :], finish_one)
    fetch(branch, result, 0).start()

    def small(source, target, at, peer):
        return copy(source, target, v_send.at[at], v_recv.at[at], peer)

    hops = [
        [(v_own, v_twin, 0, twin)],
        [(v_hold.at[0], v_a.at[k - 1], k, a_peer(k)) for k in range(1, side)],
        [(v_hold.at[1], v_b.at[k - 1], side + k - 1, b_peer(k)) for k in range(1, side)],
        [(v_hold.at[2], v_z.at[k - 1], 2 * side + k - 2, z_peer(k)) for k in range(1, deep)],
    ]
    lands = [
        lambda: [v_own[...], v_twin[...]],
        lambda: [v_hold[0]] + [v_a[k] for k in range(side - 1)],
        lambda: [v_hold[1]] + [v_b[k] for k in range(side - 1)],
        lambda: [v_hold[2]] + [v_z[k] for k in range(deep - 1)],
    ]
    for at in range(4):
        for hop in hops[at]:
            small(*hop).start()
        if at < 1:
            advance(27, 18, 24)
        for hop in hops[at]:
            small(*hop).wait()
        found = lands[at]()
        whole = found[0]
        for item in found[1:]:
            whole = whole + item
        if at < 3:
            v_hold[at] = whole
        else:
            sums[...] = whole
    fetch(branch, result, 0).wait()


def backward(place, cot, act, slope, two, unit_two, rate_two, mixed, qkv, one, unit_one,
             rate_one, gains, weights):
    dp_count, fsdp_count = lax.axis_size("dp"), lax.axis_size("fsdp")
    dims = grid_of(dp_count, fsdp_count)
    deep, across, down, cores = dims
    assert across == down and cores == 2
    length, width = cot.shape
    hidden = slope.shape[1]
    piece = width // dp_count // 2
    gw = width // fsdp_count
    count = 2 * (2 * (hidden // width) + 1 + qkv.shape[1] // width)
    any_ = pl.BlockSpec(memory_space=pl.ANY)
    vmem = pl.BlockSpec(memory_space=pltpu.VMEM)
    bf16, f32 = jnp.bfloat16, jnp.float32
    hops = 2 * side_of(dims) + deep
    return pl.pallas_call(
        partial(backward_kernel, dims),
        out_shape=[
            jax.ShapeDtypeStruct((length, width), bf16),
            jax.ShapeDtypeStruct((count, piece, gw), f32),
            jax.ShapeDtypeStruct((16, width), f32),
        ],
        in_specs=[vmem, any_, any_, any_, any_, any_, vmem, any_, any_, any_, any_, vmem, vmem]
        + [any_],
        out_specs=[any_, vmem, vmem],
        scratch_shapes=[
            pltpu.VMEM((2, 2, 2, across, down, deep, piece, gw), bf16),
            pltpu.VMEM((count, across, down, deep, piece, gw), bf16),
            pltpu.VMEM((count, across - 1, down, deep, piece, gw), bf16),
            pltpu.VMEM((count, down - 1, deep, piece, gw), bf16),
            pltpu.VMEM((count, deep - 1, piece, gw), bf16),
            pltpu.VMEM((16, width), f32),
            pltpu.VMEM((3, 16, width), f32),
            pltpu.VMEM((16, width), f32),
            pltpu.VMEM((across - 1, 16, width), f32),
            pltpu.VMEM((down - 1, 16, width), f32),
            pltpu.VMEM((deep - 1, 16, width), f32),
            pltpu.VMEM((length, width), bf16),
            pltpu.VMEM((width, width), bf16),
            pltpu.VMEM((2 * dp_count, piece, width), bf16),
            pltpu.VMEM((length, width), bf16),
            pltpu.VMEM((length, hidden), bf16),
            pltpu.VMEM((length, width), f32),
            pltpu.VMEM((length, width), f32),
            pltpu.VMEM((length, width), bf16),
            pltpu.SemaphoreType.DMA((5,)),
            pltpu.SemaphoreType.DMA((count,)),
            pltpu.SemaphoreType.DMA((count,)),
            pltpu.SemaphoreType.DMA((count, across - 1)),
            pltpu.SemaphoreType.DMA((count, across - 1)),
            pltpu.SemaphoreType.DMA((count, down - 1)),
            pltpu.SemaphoreType.DMA((count, down - 1)),
            pltpu.SemaphoreType.DMA((count, deep - 1)),
            pltpu.SemaphoreType.DMA((count, deep - 1)),
            pltpu.SemaphoreType.DMA((hops,)),
            pltpu.SemaphoreType.DMA((hops,)),
        ],
        compiler_params=pltpu.CompilerParams(
            collective_id=1, has_side_effects=True, vmem_limit_bytes=67043328
        ),
        name="backward",
    )(place, cot, act, slope, two, unit_two, rate_two, mixed, qkv, one, unit_one, rate_one, gains,
      weights)


def side_of(dims):
    return dims[1]


def pick_grads(owned, sums, width, hidden):
    dp_count, fsdp_count = lax.axis_size("dp"), lax.axis_size("fsdp")
    devices = dp_count * fsdp_count
    at = lax.axis_index("dp") * fsdp_count + lax.axis_index("fsdp")
    count, piece, gw = owned.shape
    bands = hidden // width

    def beside(part):
        groups = part.shape[0] // 2
        part = part.reshape(groups, 2 * piece, gw).transpose(1, 0, 2)
        return part.reshape(2 * piece, groups * gw)

    down = owned[: 2 * bands].reshape(bands * 2 * piece, gw)
    up = beside(owned[2 * bands : 4 * bands])
    out = owned[4 * bands : 4 * bands + 2].reshape(2 * piece, gw)
    qkv = beside(owned[4 * bands + 2 :])
    each = width // devices
    small = lax.dynamic_slice(sums[:8], (0, at * each), (8, each))
    tall = sums[8 : 8 + bands].reshape(hidden)
    tall = lax.dynamic_slice(tall, (at * (hidden // devices),), (hidden // devices,))
    return small, tall, qkv, out, up, down


def body(
    frames,
    segment_ids,
    positions,
    cotangent,
    norm1_gain,
    norm1_shift,
    qkv_weight,
    query_bias,
    value_bias,
    out_weight,
    out_bias,
    norm2_gain,
    norm2_shift,
    up_weight,
    up_bias,
    down_weight,
    down_bias,
):
    length, width = frames.shape
    many = up_weight.shape[1] * lax.axis_size("fsdp")
    vectors = place_vectors(
        [
            norm1_gain,
            norm1_shift,
            query_bias,
            value_bias,
            out_bias,
            norm2_gain,
            norm2_shift,
            down_bias,
        ],
        up_bias,
    )
    (
        output, weights, act, slope, two, unit_two, rate_two, mixed, qkv, one, unit_one, rate_one,
        gains,
    ) = forward(
        positions[0][:, None], frames, vectors, (qkv_weight, out_weight, up_weight, down_weight)
    )
    units, deep, across, halves, piece, _ = weights.shape
    weights = weights.reshape(units, deep * across * halves, piece, width)
    frames_grad, owned, sums = backward(
        positions, cotangent, act, slope, two, unit_two, rate_two, mixed, qkv, one, unit_one,
        rate_one, gains, weights,
    )
    small, tall, qkv_grad, out_grad, up_grad, down_grad = pick_grads(owned, sums, width, many)
    return (
        output,
        frames_grad,
        small[0],
        small[1],
        qkv_grad,
        small[2],
        small[3],
        out_grad,
        small[4],
        small[5],
        small[6],
        up_grad,
        tall,
        down_grad,
        small[7],
    )


def solution(mesh):
    placed = (
        P(("dp", "fsdp"), None),
        P(("dp", "fsdp"), None),
        P(("dp", "fsdp"), None),
        P(("dp", "fsdp"), None),
        P(("dp", "fsdp")),
        P(("dp", "fsdp")),
        P("dp", "fsdp"),
        P(("dp", "fsdp")),
        P(("dp", "fsdp")),
        P("dp", "fsdp"),
        P(("dp", "fsdp")),
        P(("dp", "fsdp")),
        P(("dp", "fsdp")),
        P("dp", "fsdp"),
        P(("dp", "fsdp")),
        P("dp", "fsdp"),
        P(("dp", "fsdp")),
    )
    return jax.shard_map(
        body,
        mesh=mesh,
        in_specs=placed,
        out_specs=(
            P(("dp", "fsdp"), None),
            P(("dp", "fsdp"), None),
            P(("dp", "fsdp")),
            P(("dp", "fsdp")),
            P("dp", "fsdp"),
            P(("dp", "fsdp")),
            P(("dp", "fsdp")),
            P("dp", "fsdp"),
            P(("dp", "fsdp")),
            P(("dp", "fsdp")),
            P(("dp", "fsdp")),
            P("dp", "fsdp"),
            P(("dp", "fsdp")),
            P("dp", "fsdp"),
            P(("dp", "fsdp")),
        ),
        check_vma=False,
    )
```

```python
from functools import partial
import math

import jax
import jax.numpy as jnp
from jax import lax
from jax.experimental import pallas as pl
from jax.experimental.pallas import tpu as pltpu
from jax.sharding import PartitionSpec as P

MESH = pl.DeviceIdType.MESH

HEAD_DIM = 64


eps = 1e-05


def grid_of(dp_count, fsdp_count):
    across = 1
    while across * across * 8 <= dp_count:
        across *= 2
    while dp_count % across:
        across //= 2
    cores = 2 if fsdp_count % 2 == 0 else 1
    return dp_count // across, across, fsdp_count // cores, cores


def forward_kernel(dims, *refs):
    (
        place, frames, vector_shard, in_shard, out_shard, up_shard, down_shard,
        result, weights, act_hbm, slope_hbm, two_hbm, unit_two, rate_two, mixed_hbm, qkv_hbm,
        one_hbm, unit_one, rate_one, vectors,
        spread, tall, stream, normed, unit, qkv, mixed, act, slope, turned, loaded,
        load, save, local, z_send, z_recv, a_send, a_recv, b_send, b_recv, s_send, s_recv,
    ) = refs
    deep, across, down, cores = dims
    side = across
    fsdp = down * cores
    dp_count = deep * across
    devices = dp_count * fsdp
    length, width = stream.shape
    hidden = act.shape[1]
    triple = qkv.shape[1]
    piece = weights.shape[4]
    rows_each = 2 * piece
    gw = width // fsdp
    each_in, each_up = triple // fsdp, hidden // fsdp
    groups_in, groups_up = triple // width, hidden // width
    units = weights.shape[0]
    count = 2 * units
    extra = count
    first_up = groups_in + 1
    first_down = first_up + groups_up
    block = min(256, length)
    steps = length // block
    outer = lax.axis_index("dp")
    inner = lax.axis_index("fsdp")
    z, x, y, c = outer // across, outer % across, inner // cores, inner % cores
    a = (1 - c) * x + c * y
    b = (1 - c) * y + c * x

    def device(zz, xx, yy, cc):
        return (zz * across + xx, yy * cores + cc)

    twin = device(z, x, y, 1 - c)

    def a_peer(k):
        to = (a + k) % side
        return device(z, (1 - c) * to + c * x, (1 - c) * y + c * to, c)

    def b_peer(k):
        to = (b + k) % side
        return device(z, (1 - c) * x + c * to, (1 - c) * to + c * y, c)

    def z_peer(k):
        return device((z + k) % deep, x, y, c)

    barrier = pltpu.get_barrier_semaphore()
    everyone = [twin]
    everyone += [a_peer(k) for k in range(1, side)] + [b_peer(k) for k in range(1, side)]
    everyone += [z_peer(k) for k in range(1, deep)]
    for peer in everyone:
        pl.semaphore_signal(barrier, inc=1, device_id=peer, device_id_type=MESH)
    pl.semaphore_wait(barrier, len(everyone))

    def copy(source, target, send, recv, peer):
        return pltpu.make_async_remote_copy(
            src_ref=source, dst_ref=target, send_sem=send, recv_sem=recv,
            device_id=peer, device_id_type=MESH,
        )

    every = slice(None)

    def view(i, zz, xx, yy, cc):
        lane = yy * cores + cc
        if isinstance(i, int) and i == extra:
            return spread.at[zz, xx, :, pl.ds(pl.multiple_of(lane * 128, 128), 128)]
        return weights.at[
            i // 2, zz, xx, i % 2, :, pl.ds(pl.multiple_of(lane * gw, 128), gw)
        ]

    def own(i):
        if i == extra:
            return vector_shard
        unit_at, half = i // 2, i % 2
        rows = pl.ds(half * piece, piece)
        if unit_at < groups_in:
            return in_shard.at[rows, pl.ds(unit_at * gw, gw)]
        if unit_at < first_up:
            return out_shard.at[rows, :]
        if unit_at < first_down:
            return up_shard.at[rows, pl.ds((unit_at - first_up) * gw, gw)]
        return down_shard.at[pl.ds((unit_at - first_down) * rows_each + half * piece, piece), :]

    def begin(i):
        mine = view(i, z, x, y, c)
        pltpu.make_async_copy(own(i), mine, local.at[i]).start()
        for k in range(1, deep):
            copy(own(i), mine, z_send.at[i, k - 1], z_recv.at[i, k - 1], z_peer(k)).start()

    def first(i):
        mine = view(i, z, x, y, c)
        pltpu.make_async_copy(mine, mine, local.at[i]).wait()
        for k in range(1, deep):
            landed = view(i, (z + deep - k) % deep, x, y, c)
            copy(mine, landed, z_send.at[i, k - 1], z_recv.at[i, k - 1], z_peer(k)).wait()
        line = view(i, every, x, y, c)
        for k in range(1, side):
            copy(line, line, a_send.at[i, k - 1], a_recv.at[i, k - 1], a_peer(k)).start()

    def second(i):
        for k in range(1, side):
            xs = (1 - c) * ((x + side - k) % side) + c * x
            ys = (1 - c) * y + c * ((y + side - k) % side)
            landed = view(i, every, xs, ys, c)
            copy(landed, landed, a_send.at[i, k - 1], a_recv.at[i, k - 1], a_peer(k)).wait()
        for k in range(1, side):
            for s in range(side):
                line = view(i, every, (1 - c) * s + c * x, (1 - c) * y + c * s, c)
                at = (k - 1) * side + s
                copy(line, line, b_send.at[i, at], b_recv.at[i, at], b_peer(k)).start()

    def third(i):
        for k in range(1, side):
            for s in range(side):
                xs = (1 - c) * s + c * ((x + side - k) % side)
                ys = (1 - c) * ((y + side - k) % side) + c * s
                landed = view(i, every, xs, ys, c)
                at = (k - 1) * side + s
                copy(landed, landed, b_send.at[i, at], b_recv.at[i, at], b_peer(k)).wait()
        for s in range(side):
            sheet = view(i, every, every, s, c)
            copy(sheet, sheet, s_send.at[i, s], s_recv.at[i, s], twin).start()

    def fourth(i):
        for s in range(side):
            sheet = view(i, every, every, s, 1 - c)
            copy(sheet, sheet, s_send.at[i, s], s_recv.at[i, s], twin).wait()

    stages = (first, second, third, fourth)
    lag = 2
    last = 3 * lag

    def advance(step):
        for at in reversed(range(4)):
            i = step - lag * at
            if isinstance(step, int):
                if 0 <= i < count:
                    stages[at](i)
            else:
                @pl.when((i >= 0) & (i < count))
                def _(i=i, at=at):
                    stages[at](i)

    def rows_at(m):
        return pl.ds(pl.multiple_of(m * block, block), block)

    def lanes(start, size):
        return pl.ds(start if isinstance(start, int) else pl.multiple_of(start, 128), size)

    def unit_load(at, slot):
        return pltpu.make_async_copy(weights.at[at], loaded.at[slot], load.at[slot])

    def matrix(slot):
        return loaded[slot].reshape(width, width)

    begin(extra)
    for i in range(count):
        begin(i)

    even = lax.broadcasted_iota(jnp.int32, (1, width), 1)
    speed = jnp.exp((even // 2).astype(jnp.float32) * (-2.0 * math.log(10000.0) / width))
    phase = (even % 2).astype(jnp.float32) * (0.5 * math.pi)
    small = min(64, block)
    for at in range(4):
        @pl.loop(0, length // 4 // small)
        def _(s):
            rows = pl.ds(pl.multiple_of(at * (length // 4) + s * small, small), small)
            angle = place[rows, :].astype(jnp.float32) * speed + phase
            stream[rows, :] = frames[rows, :].astype(jnp.float32) + jnp.sin(angle)

        stages[at](extra)
        advance(at)

    group = 128 // (width // devices)
    for tile in range(width // 128):
        found = None
        for owner in range(tile * group, (tile + 1) * group):
            dp_at, f = owner // fsdp, owner % fsdp
            part = spread[dp_at // across, dp_at % across, 0:8, f * 128 : (f + 1) * 128]
            found = part if found is None else found + part
        vectors[:, tile * 128 : (tile + 1) * 128] = found
    group = 128 // (hidden // devices)
    for tile in range(hidden // 128):
        found = None
        for owner in range(tile * group, (tile + 1) * group):
            dp_at, f = owner // fsdp, owner % fsdp
            part = spread[dp_at // across, dp_at % across, 8:16, f * 128 : (f + 1) * 128]
            found = part if found is None else found + part
        tall[:, tile * 128 : (tile + 1) * 128] = found

    def normalize(m, value, row, rate_ref):
        mean = jnp.mean(value, axis=1, keepdims=True)
        centered = value - mean
        rate = lax.rsqrt(jnp.mean(centered * centered, axis=1, keepdims=True) + eps)
        normal = centered * rate
        rate_ref[rows_at(m), :] = jnp.broadcast_to(rate, (block, 128))
        unit[rows_at(m), :] = normal.astype(jnp.bfloat16)
        found = (normal * vectors[row : row + 1, :] + vectors[row + 1 : row + 2, :])
        found = found.astype(jnp.bfloat16)
        normed[rows_at(m), :] = found
        return found

    @pl.loop(0, steps)
    def _(m):
        found = normalize(m, stream[rows_at(m), :], 0, rate_one)
        turned[0, :, rows_at(m)] = found.T

    def keep(source, target, at):
        return pltpu.make_async_copy(source, target, save.at[at])

    keep(unit, unit_one, 0).start()
    keep(turned.at[0], one_hbm, 1).start()
    done = 4
    for g in range(groups_in):
        while done < 2 * g + 2 + last:
            advance(done)
            done += 1
        unit_load(g, g % 2).start()
        unit_load(g, g % 2).wait()

        @pl.loop(0, steps)
        def _(m):
            found = jnp.dot(
                normed[rows_at(m), :], matrix(g % 2), preferred_element_type=jnp.float32
            )
            for f in range(fsdp):
                start = f * each_in + g * gw
                part = found[:, f * gw : (f + 1) * gw]
                if start < width:
                    part = part + vectors[2:3, start : start + gw]
                elif start >= 2 * width:
                    at = start - 2 * width
                    part = part + vectors[3:4, at : at + gw]
                qkv[rows_at(m), start : start + gw] = part.astype(jnp.bfloat16)

    keep(qkv, qkv_hbm, 2).start()
    pairs = width // (2 * HEAD_DIM)
    base = done
    factor = math.log2(math.e) / math.sqrt(HEAD_DIM)
    lane = lax.broadcasted_iota(jnp.int32, (block, 2 * HEAD_DIM), 1)

    @pl.loop(0, pairs)
    def _(j):
        pair = 2 * HEAD_DIM
        at_q = lanes(j * pair, pair)
        at_k = lanes(width + j * pair, pair)
        at_v = lanes(2 * width + j * pair, pair)
        for at in range(steps):
            rows = pl.ds(at * block, block)
            span = (at + 1) * block
            asked = qkv[rows, at_q]
            seen = qkv[pl.ds(0, span), at_k]
            held = qkv[pl.ds(0, span), at_v]
            row = at * block + lax.broadcasted_iota(jnp.int32, (block, span), 0)
            col = lax.broadcasted_iota(jnp.int32, (block, span), 1)
            start = at * block + lax.broadcasted_iota(jnp.int32, (block, 1), 0) - place[rows, :]
            allowed = (col <= row) & (col >= start)
            found = []
            for half in range(2):
                mine = jnp.where((lane // HEAD_DIM) == half, asked, jnp.zeros_like(asked))
                scores = matmul(mine, seen, (1, 1))
                scores = jnp.where(allowed, scores * factor, -1e30)
                weight = jnp.exp2(scores - jnp.max(scores, axis=1, keepdims=True))
                whole = jnp.sum(weight, axis=1, keepdims=True)
                found.append(matmul(weight.astype(jnp.bfloat16), held, (1, 0)) / whole)
            part = jnp.where(lane < HEAD_DIM, found[0], found[1]).astype(jnp.bfloat16)
            mixed[rows, at_q] = part
            turned[1, lanes(j * pair, pair), rows] = part.T
        advance(base + j)

    keep(turned.at[1], mixed_hbm, 3).start()
    unit_load(groups_in, 0).start()
    base = base + pairs
    advance(base)
    keep(unit, unit_one, 0).wait()
    keep(turned.at[0], one_hbm, 1).wait()
    unit_load(groups_in, 0).wait()

    @pl.loop(0, steps)
    def _(m):
        found = jnp.dot(mixed[rows_at(m), :], matrix(0), preferred_element_type=jnp.float32)
        found = stream[rows_at(m), :] + found + vectors[4:5, :]
        stream[rows_at(m), :] = found
        found = normalize(m, found, 5, rate_two)
        turned[0, :, rows_at(m)] = found.T

    keep(unit, unit_two, 0).start()
    keep(turned.at[0], two_hbm, 1).start()
    advance(base + 1)
    base = base + 2

    def turned_rows(slot, g):
        moves = []
        for q in range(width // rows_each):
            f, rest = q * rows_each // gw, q * rows_each % gw
            at = f * each_up + g * gw + rest
            owner, band = at // (groups_up * rows_each), (at // rows_each) % groups_up
            target = pl.multiple_of(band * width + owner * rows_each, 16)
            moves.append(
                pltpu.make_async_copy(
                    turned.at[slot, pl.ds(q * rows_each, rows_each), :],
                    act_hbm.at[pl.ds(target, rows_each), :],
                    save.at[4 + slot],
                )
            )
        return moves

    def turned_done(slot):
        return pltpu.make_async_copy(
            turned.at[slot], act_hbm.at[pl.ds(0, width), :], save.at[4 + slot]
        )

    unit_load(first_up, 0).start()

    @pl.loop(0, groups_up)
    def _(g):
        slot = g % 2
        unit_load(first_up + g, slot).wait()

        @pl.when(g < groups_up - 1)
        def _():
            unit_load(first_up + g + 1, 1 - slot).start()

        @pl.when(g == 0)
        def _():
            keep(turned.at[0], two_hbm, 1).wait()

        @pl.when(g == 1)
        def _():
            keep(turned.at[1], mixed_hbm, 3).wait()

        @pl.when(g >= 2)
        def _():
            turned_done(slot).wait()

        @pl.loop(0, steps)
        def _(m):
            found = jnp.dot(
                normed[rows_at(m), :], matrix(slot), preferred_element_type=jnp.float32
            )
            for f in range(fsdp):
                at = lanes(f * each_up + g * gw, gw)
                pre = found[:, f * gw : (f + 1) * gw] + tall[0:1, at]
                half = 0.5 + 0.5 * lax.erf(pre * math.sqrt(0.5))
                low = (pre * half).astype(jnp.bfloat16)
                act[rows_at(m), at] = low
                bend = half + pre * jnp.exp(-0.5 * pre * pre) * (1.0 / math.sqrt(2.0 * math.pi))
                slope[rows_at(m), at] = bend.astype(jnp.bfloat16)
                turned[slot, pl.ds(f * gw, gw), rows_at(m)] = low.T

        for move in turned_rows(slot, g):
            move.start()
        advance(base + 2 * g)
        advance(base + 1 + 2 * g)

    keep(slope, slope_hbm, 6).start()
    for step in range(base + 2 * groups_up, count + last):
        advance(step)

    def band_load(k, slot):
        moves = []
        for q in range(dp_count):
            owner, at = k * (dp_count // groups_up) + q // groups_up, q % groups_up
            moves.append(
                pltpu.make_async_copy(
                    weights.at[first_down + at, owner // across, owner % across],
                    loaded.at[slot, q // across, q % across],
                    load.at[slot],
                )
            )
        return moves

    for move in band_load(0, 0):
        move.start()

    @pl.loop(0, groups_up)
    def _(k):
        slot = k % 2
        unit_load(0, slot).wait()

        @pl.when(k < groups_up - 1)
        def _():
            for move in band_load(k + 1, 1 - slot):
                move.start()

        @pl.loop(0, steps)
        def _(m):
            stream[rows_at(m), :] += jnp.dot(
                act[rows_at(m), lanes(k * width, width)], matrix(slot),
                preferred_element_type=jnp.float32,
            )

    @pl.loop(0, steps)
    def _(m):
        normed[rows_at(m), :] = (stream[rows_at(m), :] + vectors[7:8, :]).astype(jnp.bfloat16)

    keep(normed, result, 7).start()
    keep(unit, unit_two, 0).wait()
    keep(qkv, qkv_hbm, 2).wait()
    for slot in range(2):
        turned_done(slot).wait()
    keep(slope, slope_hbm, 6).wait()
    keep(normed, result, 7).wait()


def forward(place, frames, vectors, shards):
    dp_count, fsdp_count = lax.axis_size("dp"), lax.axis_size("fsdp")
    dims = grid_of(dp_count, fsdp_count)
    deep, across, down, cores = dims
    assert across == down and cores == 2
    length, width = frames.shape
    triple = shards[0].shape[1] * fsdp_count
    hidden = shards[2].shape[1] * fsdp_count
    piece = width // dp_count // 2
    units = 2 * (hidden // width) + 1 + triple // width
    count = 2 * units
    any_ = pl.BlockSpec(memory_space=pl.ANY)
    vmem = pl.BlockSpec(memory_space=pltpu.VMEM)
    bf16, f32 = jnp.bfloat16, jnp.float32

    def shape(*sizes, kind=bf16):
        return jax.ShapeDtypeStruct(sizes, kind)

    return pl.pallas_call(
        partial(forward_kernel, dims),
        out_shape=[
            shape(length, width),
            shape(units, deep, across, 2, piece, width),
            shape(hidden, length),
            shape(length, hidden),
            shape(width, length),
            shape(length, width),
            shape(length, 128, kind=f32),
            shape(width, length),
            shape(length, triple),
            shape(width, length),
            shape(length, width),
            shape(length, 128, kind=f32),
            shape(8, width, kind=f32),
        ],
        in_specs=[vmem] * 7,
        out_specs=[any_] * 6 + [vmem] + [any_] * 4 + [vmem] * 2,
        scratch_shapes=[
            pltpu.VMEM((deep, across, 16, fsdp_count * 128), f32),
            pltpu.VMEM((8, hidden), f32),
            pltpu.VMEM((length, width), f32),
            pltpu.VMEM((length, width), bf16),
            pltpu.VMEM((length, width), bf16),
            pltpu.VMEM((length, triple), bf16),
            pltpu.VMEM((length, width), bf16),
            pltpu.VMEM((length, hidden), bf16),
            pltpu.VMEM((length, hidden), bf16),
            pltpu.VMEM((2, width, length), bf16),
            pltpu.VMEM((2, deep, across, 2, piece, width), bf16),
            pltpu.SemaphoreType.DMA((2,)),
            pltpu.SemaphoreType.DMA((8,)),
            pltpu.SemaphoreType.DMA((count + 1,)),
            pltpu.SemaphoreType.DMA((count + 1, deep - 1)),
            pltpu.SemaphoreType.DMA((count + 1, deep - 1)),
            pltpu.SemaphoreType.DMA((count + 1, across - 1)),
            pltpu.SemaphoreType.DMA((count + 1, across - 1)),
            pltpu.SemaphoreType.DMA((count + 1, (across - 1) * across)),
            pltpu.SemaphoreType.DMA((count + 1, (across - 1) * across)),
            pltpu.SemaphoreType.DMA((count + 1, down)),
            pltpu.SemaphoreType.DMA((count + 1, down)),
        ],
        compiler_params=pltpu.CompilerParams(
            collective_id=0, has_side_effects=True, vmem_limit_bytes=67043328
        ),
        name="forward",
    )(place, frames, vectors, *shards)


def place_vectors(items, up_bias):
    devices = lax.axis_size("dp") * lax.axis_size("fsdp")
    at = lax.axis_index("dp") * lax.axis_size("fsdp") + lax.axis_index("fsdp")
    lane = jnp.arange(128)

    def placed(rows):
        size = rows.shape[1]
        repeated = jnp.tile(rows.astype(jnp.float32), (1, 128 // size))
        return jnp.where((lane // size == at % (128 // size))[None], repeated, 0.0)

    packed = jnp.stack(items)
    return jnp.concatenate(
        [placed(packed), placed(up_bias[None]), jnp.zeros((7, 128), jnp.float32)]
    )


def matmul(left, right, contract):
    return lax.dot_general(
        left, right, ((contract[:1], contract[1:]), ((), ())), preferred_element_type=jnp.float32
    )


def backward_kernel(dims, *refs):
    (
        place, cot_hbm, act_hbm, slope_hbm, two_hbm, unit_two, rate_two, mixed_hbm, qkv_hbm,
        one_hbm, unit_one, rate_one, gains, weights,
        result, owned, sums,
        grads, twin_in, a_in, b_in, z_in,
        v_own, v_hold, v_twin, v_a, v_b, v_z,
        cot, left, right, unit, wide, total, second, branch,
        load, t_send, t_recv, a_send, a_recv, b_send, b_recv, z_send, z_recv,
        v_send, v_recv,
    ) = refs
    deep, across, down, cores = dims
    side = across
    length, width = cot.shape
    hidden = wide.shape[1]
    piece, gw = owned.shape[1], owned.shape[2]
    fsdp = down * cores
    rows_each = 2 * piece
    outer = lax.axis_index("dp")
    inner = lax.axis_index("fsdp")
    z, x, y, c = outer // across, outer % across, inner // cores, inner % cores
    a = (1 - c) * x + c * y
    b = (1 - c) * y + c * x
    block = min(256, length)
    steps = length // block

    def device(zz, xx, yy, cc):
        return (zz * across + xx, yy * cores + cc)

    twin = device(z, x, y, 1 - c)

    def a_peer(k):
        to = (a + k) % side
        return device(z, (1 - c) * to + c * x, (1 - c) * y + c * to, c)

    def b_peer(k):
        to = (b + k) % side
        return device(z, (1 - c) * x + c * to, (1 - c) * to + c * y, c)

    def z_peer(k):
        return device((z + k) % deep, x, y, c)

    barrier = pltpu.get_barrier_semaphore()
    everyone = [twin]
    everyone += [a_peer(k) for k in range(1, side)] + [b_peer(k) for k in range(1, side)]
    everyone += [z_peer(k) for k in range(1, deep)]
    for peer in everyone:
        pl.semaphore_signal(barrier, inc=1, device_id=peer, device_id_type=MESH)
    pl.semaphore_wait(barrier, len(everyone))

    def copy(source, target, send, recv, peer):
        return pltpu.make_async_remote_copy(
            src_ref=source, dst_ref=target, send_sem=send, recv_sem=recv,
            device_id=peer, device_id_type=MESH,
        )

    def t_copy(i):
        return copy(
            grads.at[(i // 2) % 2, i % 2, 1 - c], twin_in.at[i], t_send.at[i], t_recv.at[i], twin
        )

    def a_copy(i, k):
        return copy(
            twin_in.at[i, (a + k) % side], a_in.at[i, k - 1],
            a_send.at[i, k - 1], a_recv.at[i, k - 1], a_peer(k),
        )

    def b_copy(i, k):
        return copy(
            a_in.at[i, 0, (b + k) % side], b_in.at[i, k - 1],
            b_send.at[i, k - 1], b_recv.at[i, k - 1], b_peer(k),
        )

    def z_copy(i, k):
        return copy(
            b_in.at[i, 0, (z + k) % deep], z_in.at[i, k - 1],
            z_send.at[i, k - 1], z_recv.at[i, k - 1], z_peer(k),
        )

    def first(i):
        t_copy(i).start()

    def second_stage(i):
        t_copy(i).wait()
        twin_in[i] = twin_in[i] + grads[(i // 2) % 2, i % 2, c]
        for k in range(1, side):
            a_copy(i, k).start()

    def third(i):
        for k in range(1, side):
            a_copy(i, k).wait()
        found = twin_in[i, a]
        for k in range(1, side):
            found = found + a_in[i, k - 1]
        a_in[i, 0] = found
        for k in range(1, side):
            b_copy(i, k).start()

    def fourth(i):
        for k in range(1, side):
            b_copy(i, k).wait()
        found = a_in[i, 0, b]
        for k in range(1, side):
            found = found + b_in[i, k - 1]
        b_in[i, 0] = found
        for k in range(1, deep):
            z_copy(i, k).start()

    def fifth(i):
        for k in range(1, deep):
            z_copy(i, k).wait()
        found = b_in[i, 0, z].astype(jnp.float32)
        for k in range(1, deep):
            found = found + z_in[i, k - 1].astype(jnp.float32)
        owned[i] = found

    stages = (first, second_stage, third, fourth, fifth)

    lags = (0, 1, 3, 5, 7)

    def advance(step, low, high):
        for at in reversed(range(5)):
            i = step - lags[at]
            if isinstance(step, int):
                if low <= i < high:
                    stages[at](i)
            else:
                @pl.when((i >= low) & (i < high))
                def _(i=i, at=at):
                    stages[at](i)

    def fetch(source, target, at):
        return pltpu.make_async_copy(source, target, load.at[at])

    groups_up = hidden // width
    groups_in = qkv_hbm.shape[1] // width
    first_up = groups_in + 1
    first_down = first_up + groups_up
    dp_count = deep * across

    def down_load(j):
        moves = []
        for q in range(dp_count):
            owner, at = j * (dp_count // groups_up) + q // groups_up, q % groups_up
            moves.append(
                fetch(weights.at[first_down + at, pl.ds(2 * owner, 2)], right.at[pl.ds(2 * q, 2)], 2)
            )
        return moves

    def matrix():
        return right[...].reshape(width, width)

    def strips(rows, each, g):
        parts = []
        for f in range(fsdp):
            start = f * each + g * gw
            if not isinstance(start, int):
                start = pl.multiple_of(start, 128)
            parts.append(wide[rows, pl.ds(start, gw)])
        return jnp.concatenate(parts, axis=1)

    def band(ref, j):
        return ref.at[pl.ds(pl.multiple_of(j * width, width), width), :]

    def rows_at(m):
        return pl.ds(pl.multiple_of(m * block, block), block)

    def make_unit(slot, source, strip):
        @pl.loop(0, width // block)
        def _(m):
            lhs = left[rows_at(m), :]
            for f in range(fsdp):
                yy, cc = f // cores, f % cores
                found = matmul(lhs, source[:, pl.ds(strip(f), gw)], (1, 0)).astype(jnp.bfloat16)
                for q in range(block // piece):
                    owner = m * (block // rows_each) + q // 2
                    zz, xx = owner // across, owner % across
                    part = found[q * piece : (q + 1) * piece, :]
                    if cc == 0:
                        grads[slot, q % 2, 0, xx, yy, zz] = part
                    else:
                        grads[slot, q % 2, 1, yy, xx, zz] = part

    def columns(value):
        return jnp.sum(value, axis=0, keepdims=True)

    fetch(cot_hbm, cot, 0).start()
    fetch(band(act_hbm, 0), left, 1).start()
    for move in down_load(0):
        move.start()
    fetch(slope_hbm, wide, 3).start()
    fetch(unit_two, unit, 4).start()
    v_own[...] = jnp.zeros_like(v_own)
    total[...] = jnp.zeros_like(total)
    fetch(cot_hbm, cot, 0).wait()

    @pl.loop(0, 4)
    def _(j):
        fetch(band(act_hbm, j), left, 1).wait()
        make_unit(j % 2, cot, lambda f: f * gw)

        @pl.when(j < 3)
        def _():
            fetch(band(act_hbm, (j + 1) % 4), left, 1).start()

        @pl.when(j == 3)
        def _():
            fetch(two_hbm, left, 1).start()

        advance(2 * j, 0, 18)
        fetch(weights.at[0], right, 2).wait()

        @pl.when(j == 0)
        def _():
            fetch(slope_hbm, wide, 3).wait()

        span = pl.ds(pl.multiple_of(j * width, width), width)

        @pl.loop(0, steps)
        def _(m):
            found = matmul(cot[rows_at(m), :], matrix(), (1, 1))
            found = (found * wide[rows_at(m), span].astype(jnp.float32)).astype(jnp.bfloat16)
            wide[rows_at(m), span] = found
            v_own[pl.ds(8 + j, 1), :] += columns(found.astype(jnp.float32))

        @pl.when(j < 3)
        def _():
            for move in down_load((j + 1) % 4):
                move.start()

        @pl.when(j == 3)
        def _():
            fetch(weights.at[first_up], right, 2).start()

        advance(2 * j + 1, 0, 18)

    fetch(two_hbm, left, 1).wait()
    each_up = hidden // fsdp

    @pl.loop(0, 4)
    def _(j):
        make_unit(j % 2, wide, lambda f: pl.multiple_of(f * each_up + j * gw, 128))
        advance(8 + 2 * j, 0, 18)
        fetch(weights.at[first_up + j], right, 2).wait()

        @pl.loop(0, steps)
        def _(m):
            total[rows_at(m), :] += matmul(strips(rows_at(m), each_up, j), matrix(), (1, 1))

        @pl.when(j < 3)
        def _():
            fetch(weights.at[first_up + (j + 1) % 4], right, 2).start()

        @pl.when(j == 3)
        def _():
            fetch(weights.at[groups_in], right, 2).start()

        advance(9 + 2 * j, 0, 18)

    triple = qkv_hbm.shape[1]
    packed = wide.at[:, pl.ds(0, triple)]
    fetch(mixed_hbm, left, 1).start()
    fetch(qkv_hbm, packed, 3).start()
    fetch(unit_two, unit, 4).wait()

    def norm_back(rate, gain, finish):
        @pl.loop(0, steps)
        def _(m):
            grad = total[rows_at(m), :]
            normal = unit[rows_at(m), :].astype(jnp.float32)
            scaled = grad * gain
            mean = jnp.mean(scaled, axis=1, keepdims=True)
            tilt = jnp.mean(scaled * normal, axis=1, keepdims=True)
            finish(m, grad, normal, rate[rows_at(m), 0:1] * (scaled - mean - normal * tilt))

    def finish_two(m, grad, normal, moved):
        incoming = cot[rows_at(m), :].astype(jnp.float32)
        found = incoming + moved
        second[rows_at(m), :] = found
        low = found.astype(jnp.bfloat16)
        branch[rows_at(m), :] = low
        v_own[4:5, :] += columns(low.astype(jnp.float32))
        v_own[5:6, :] += columns(grad * normal)
        v_own[6:7, :] += columns(grad)
        v_own[7:8, :] += columns(incoming)

    norm_back(rate_two, gains[5:6, :], finish_two)
    fetch(unit_one, unit, 4).start()
    fetch(mixed_hbm, left, 1).wait()
    make_unit(0, branch, lambda f: f * gw)
    fetch(one_hbm, left, 1).start()
    advance(16, 0, 18)
    fetch(weights.at[groups_in], right, 2).wait()

    @pl.loop(0, steps)
    def _(m):
        found = matmul(branch[rows_at(m), :], matrix(), (1, 1))
        branch[rows_at(m), :] = found.astype(jnp.bfloat16)

    fetch(weights.at[0], right, 2).start()
    advance(17, 0, 18)
    fetch(qkv_hbm, packed, 3).wait()
    pairs = width // (2 * HEAD_DIM)
    scale = 1.0 / math.sqrt(HEAD_DIM)
    factor = scale * math.log2(math.e)
    lane = lax.broadcasted_iota(jnp.int32, (block, 2 * HEAD_DIM), 1)

    @pl.loop(0, pairs)
    def _(j):
        pair = 2 * HEAD_DIM
        at_q = pl.ds(pl.multiple_of(j * pair, pair), pair)
        at_k = pl.ds(pl.multiple_of(width + j * pair, pair), pair)
        at_v = pl.ds(pl.multiple_of(2 * width + j * pair, pair), pair)
        sum_q = jnp.zeros((1, pair), jnp.float32)
        for at in range(steps):
            rows = pl.ds(at * block, block)
            span = (at + 1) * block
            asked = wide[rows, at_q]
            given = branch[rows, at_q]
            seen = wide[pl.ds(0, span), at_k]
            held = wide[pl.ds(0, span), at_v]
            col = at * block + lax.broadcasted_iota(jnp.int32, (span, block), 1)
            row = lax.broadcasted_iota(jnp.int32, (span, block), 0)
            begin = at * block + lax.broadcasted_iota(jnp.int32, (1, block), 1)
            begin = begin - place[:, pl.ds(at * block, block)]
            allowed = (row <= col) & (row >= begin)
            grad_q = []
            grad_k = None
            grad_v = None
            for half in range(2):
                keep = (lane // HEAD_DIM) == half
                mine = jnp.where(keep, asked, jnp.zeros_like(asked))
                ours = jnp.where(keep, given, jnp.zeros_like(given))
                scores = matmul(seen, mine, (1, 1))
                scores = jnp.where(allowed, scores * factor, -1e30)
                probs = jnp.exp2(scores - jnp.max(scores, axis=0, keepdims=True))
                probs = probs * (1.0 / columns(probs))
                grad_p = matmul(held, ours, (1, 1))
                delta = columns(probs * grad_p)
                grad_s = (probs * (grad_p - delta)).astype(jnp.bfloat16)
                part_v = matmul(probs.astype(jnp.bfloat16), ours, (1, 0))
                part_k = matmul(grad_s, mine, (1, 0))
                grad_q.append(matmul(grad_s, seen, (0, 0)))
                grad_v = part_v if grad_v is None else grad_v + part_v
                grad_k = part_k if grad_k is None else grad_k + part_k
            found = jnp.where(lane < HEAD_DIM, grad_q[0], grad_q[1]) * scale
            found = found.astype(jnp.bfloat16)
            wide[rows, at_q] = found
            sum_q = sum_q + columns(found.astype(jnp.float32))
            if at:
                old = pl.ds(0, at * block)
                total[old, 0:pair] += grad_k[: at * block, :]
                total[old, pair : 2 * pair] += grad_v[: at * block, :]
            total[rows, 0:pair] = grad_k[at * block :, :]
            total[rows, pair : 2 * pair] = grad_v[at * block :, :]
        wide[:, at_k] = (total[:, 0:pair] * scale).astype(jnp.bfloat16)
        low = total[:, pair : 2 * pair].astype(jnp.bfloat16)
        wide[:, at_v] = low
        v_own[2:3, at_q] = sum_q
        v_own[3:4, at_q] = columns(low.astype(jnp.float32))
        advance(18 + j, 0, 18)

    total[...] = jnp.zeros_like(total)
    each_in = triple // fsdp
    fetch(one_hbm, left, 1).wait()
    for j in range(3):
        make_unit((9 + j) % 2, wide, lambda f: f * each_in + j * gw)
        advance(18 + 2 * j, 18, 24)
        advance(19 + 2 * j, 18, 24)
    fetch(unit_one, unit, 4).wait()
    for j in range(3):
        fetch(weights.at[j], right, 2).wait()

        @pl.loop(0, steps)
        def _(m):
            total[rows_at(m), :] += matmul(strips(rows_at(m), each_in, j), matrix(), (1, 1))

        if j < 2:
            fetch(weights.at[j + 1], right, 2).start()
        advance(24 + 2 * j, 18, 24)
        if j < 2:
            advance(25 + 2 * j, 18, 24)

    def finish_one(m, grad, normal, moved):
        branch[rows_at(m), :] = (second[rows_at(m), :] + moved).astype(jnp.bfloat16)
        v_own[0:1, :] += columns(grad * normal)
        v_own[1:2, :] += columns(grad)

    norm_back(rate_one, gains[0:1, :], finish_one)
    fetch(branch, result, 0).start()

    def small(source, target, at, peer):
        return copy(source, target, v_send.at[at], v_recv.at[at], peer)

    hops = [
        [(v_own, v_twin, 0, twin)],
        [(v_hold.at[0], v_a.at[k - 1], k, a_peer(k)) for k in range(1, side)],
        [(v_hold.at[1], v_b.at[k - 1], side + k - 1, b_peer(k)) for k in range(1, side)],
        [(v_hold.at[2], v_z.at[k - 1], 2 * side + k - 2, z_peer(k)) for k in range(1, deep)],
    ]
    lands = [
        lambda: [v_own[...], v_twin[...]],
        lambda: [v_hold[0]] + [v_a[k] for k in range(side - 1)],
        lambda: [v_hold[1]] + [v_b[k] for k in range(side - 1)],
        lambda: [v_hold[2]] + [v_z[k] for k in range(deep - 1)],
    ]
    for at in range(4):
        for hop in hops[at]:
            small(*hop).start()
        if at < 2:
            advance(29 + at, 18, 24)
        for hop in hops[at]:
            small(*hop).wait()
        found = lands[at]()
        whole = found[0]
        for item in found[1:]:
            whole = whole + item
        if at < 3:
            v_hold[at] = whole
        else:
            sums[...] = whole
    fetch(branch, result, 0).wait()


def backward(place, cot, act, slope, two, unit_two, rate_two, mixed, qkv, one, unit_one,
             rate_one, gains, weights):
    dp_count, fsdp_count = lax.axis_size("dp"), lax.axis_size("fsdp")
    dims = grid_of(dp_count, fsdp_count)
    deep, across, down, cores = dims
    assert across == down and cores == 2
    length, width = cot.shape
    hidden = slope.shape[1]
    piece = width // dp_count // 2
    gw = width // fsdp_count
    count = 2 * (2 * (hidden // width) + 1 + qkv.shape[1] // width)
    any_ = pl.BlockSpec(memory_space=pl.ANY)
    vmem = pl.BlockSpec(memory_space=pltpu.VMEM)
    bf16, f32 = jnp.bfloat16, jnp.float32
    hops = 2 * side_of(dims) + deep
    return pl.pallas_call(
        partial(backward_kernel, dims),
        out_shape=[
            jax.ShapeDtypeStruct((length, width), bf16),
            jax.ShapeDtypeStruct((count, piece, gw), f32),
            jax.ShapeDtypeStruct((16, width), f32),
        ],
        in_specs=[vmem, any_, any_, any_, any_, any_, vmem, any_, any_, any_, any_, vmem, vmem]
        + [any_],
        out_specs=[any_, vmem, vmem],
        scratch_shapes=[
            pltpu.VMEM((2, 2, 2, across, down, deep, piece, gw), bf16),
            pltpu.VMEM((count, across, down, deep, piece, gw), bf16),
            pltpu.VMEM((count, across - 1, down, deep, piece, gw), bf16),
            pltpu.VMEM((count, down - 1, deep, piece, gw), bf16),
            pltpu.VMEM((count, deep - 1, piece, gw), bf16),
            pltpu.VMEM((16, width), f32),
            pltpu.VMEM((3, 16, width), f32),
            pltpu.VMEM((16, width), f32),
            pltpu.VMEM((across - 1, 16, width), f32),
            pltpu.VMEM((down - 1, 16, width), f32),
            pltpu.VMEM((deep - 1, 16, width), f32),
            pltpu.VMEM((length, width), bf16),
            pltpu.VMEM((width, width), bf16),
            pltpu.VMEM((2 * dp_count, piece, width), bf16),
            pltpu.VMEM((length, width), bf16),
            pltpu.VMEM((length, hidden), bf16),
            pltpu.VMEM((length, width), f32),
            pltpu.VMEM((length, width), f32),
            pltpu.VMEM((length, width), bf16),
            pltpu.SemaphoreType.DMA((5,)),
            pltpu.SemaphoreType.DMA((count,)),
            pltpu.SemaphoreType.DMA((count,)),
            pltpu.SemaphoreType.DMA((count, across - 1)),
            pltpu.SemaphoreType.DMA((count, across - 1)),
            pltpu.SemaphoreType.DMA((count, down - 1)),
            pltpu.SemaphoreType.DMA((count, down - 1)),
            pltpu.SemaphoreType.DMA((count, deep - 1)),
            pltpu.SemaphoreType.DMA((count, deep - 1)),
            pltpu.SemaphoreType.DMA((hops,)),
            pltpu.SemaphoreType.DMA((hops,)),
        ],
        compiler_params=pltpu.CompilerParams(
            collective_id=1, has_side_effects=True, vmem_limit_bytes=67043328
        ),
        name="backward",
    )(place, cot, act, slope, two, unit_two, rate_two, mixed, qkv, one, unit_one, rate_one, gains,
      weights)


def side_of(dims):
    return dims[1]


def pick_grads(owned, sums, width, hidden):
    dp_count, fsdp_count = lax.axis_size("dp"), lax.axis_size("fsdp")
    devices = dp_count * fsdp_count
    at = lax.axis_index("dp") * fsdp_count + lax.axis_index("fsdp")
    count, piece, gw = owned.shape
    bands = hidden // width

    def beside(part):
        groups = part.shape[0] // 2
        part = part.reshape(groups, 2 * piece, gw).transpose(1, 0, 2)
        return part.reshape(2 * piece, groups * gw)

    down = owned[: 2 * bands].reshape(bands * 2 * piece, gw)
    up = beside(owned[2 * bands : 4 * bands])
    out = owned[4 * bands : 4 * bands + 2].reshape(2 * piece, gw)
    qkv = beside(owned[4 * bands + 2 :])
    each = width // devices
    small = lax.dynamic_slice(sums[:8], (0, at * each), (8, each))
    tall = sums[8 : 8 + bands].reshape(hidden)
    tall = lax.dynamic_slice(tall, (at * (hidden // devices),), (hidden // devices,))
    return small, tall, qkv, out, up, down


def body(
    frames,
    segment_ids,
    positions,
    cotangent,
    norm1_gain,
    norm1_shift,
    qkv_weight,
    query_bias,
    value_bias,
    out_weight,
    out_bias,
    norm2_gain,
    norm2_shift,
    up_weight,
    up_bias,
    down_weight,
    down_bias,
):
    length, width = frames.shape
    many = up_weight.shape[1] * lax.axis_size("fsdp")
    vectors = place_vectors(
        [
            norm1_gain,
            norm1_shift,
            query_bias,
            value_bias,
            out_bias,
            norm2_gain,
            norm2_shift,
            down_bias,
        ],
        up_bias,
    )
    (
        output, weights, act, slope, two, unit_two, rate_two, mixed, qkv, one, unit_one, rate_one,
        gains,
    ) = forward(
        positions[0][:, None], frames, vectors, (qkv_weight, out_weight, up_weight, down_weight)
    )
    units, deep, across, halves, piece, _ = weights.shape
    weights = weights.reshape(units, deep * across * halves, piece, width)
    frames_grad, owned, sums = backward(
        positions, cotangent, act, slope, two, unit_two, rate_two, mixed, qkv, one, unit_one,
        rate_one, gains, weights,
    )
    small, tall, qkv_grad, out_grad, up_grad, down_grad = pick_grads(owned, sums, width, many)
    return (
        output,
        frames_grad,
        small[0],
        small[1],
        qkv_grad,
        small[2],
        small[3],
        out_grad,
        small[4],
        small[5],
        small[6],
        up_grad,
        tall,
        down_grad,
        small[7],
    )


def solution(mesh):
    placed = (
        P(("dp", "fsdp"), None),
        P(("dp", "fsdp"), None),
        P(("dp", "fsdp"), None),
        P(("dp", "fsdp"), None),
        P(("dp", "fsdp")),
        P(("dp", "fsdp")),
        P("dp", "fsdp"),
        P(("dp", "fsdp")),
        P(("dp", "fsdp")),
        P("dp", "fsdp"),
        P(("dp", "fsdp")),
        P(("dp", "fsdp")),
        P(("dp", "fsdp")),
        P("dp", "fsdp"),
        P(("dp", "fsdp")),
        P("dp", "fsdp"),
        P(("dp", "fsdp")),
    )
    return jax.shard_map(
        body,
        mesh=mesh,
        in_specs=placed,
        out_specs=(
            P(("dp", "fsdp"), None),
            P(("dp", "fsdp"), None),
            P(("dp", "fsdp")),
            P(("dp", "fsdp")),
            P("dp", "fsdp"),
            P(("dp", "fsdp")),
            P(("dp", "fsdp")),
            P("dp", "fsdp"),
            P(("dp", "fsdp")),
            P(("dp", "fsdp")),
            P(("dp", "fsdp")),
            P("dp", "fsdp"),
            P(("dp", "fsdp")),
            P("dp", "fsdp"),
            P(("dp", "fsdp")),
        ),
        check_vma=False,
    )
```

```python
from functools import partial
import math

import jax
import jax.numpy as jnp
from jax import lax
from jax.experimental import pallas as pl
from jax.experimental.pallas import tpu as pltpu
from jax.sharding import PartitionSpec as P

MESH = pl.DeviceIdType.MESH

HEAD_DIM = 64


eps = 1e-05


def grid_of(dp_count, fsdp_count):
    across = 1
    while across * across * 8 <= dp_count:
        across *= 2
    while dp_count % across:
        across //= 2
    cores = 2 if fsdp_count % 2 == 0 else 1
    return dp_count // across, across, fsdp_count // cores, cores


def forward_kernel(dims, *refs):
    (
        place, frames, vector_shard, in_shard, out_shard, up_shard, down_shard,
        result, weights, act_hbm, slope_hbm, two_hbm, unit_two, rate_two, mixed_hbm, qkv_hbm,
        one_hbm, unit_one, rate_one, vectors,
        spread, tall, stream, normed, unit, qkv, mixed, act, slope, turned, loaded,
        load, save, local, z_send, z_recv, a_send, a_recv, b_send, b_recv, s_send, s_recv,
    ) = refs
    deep, across, down, cores = dims
    side = across
    fsdp = down * cores
    dp_count = deep * across
    devices = dp_count * fsdp
    length, width = stream.shape
    hidden = act.shape[1]
    triple = qkv.shape[1]
    piece = weights.shape[4]
    rows_each = 2 * piece
    gw = width // fsdp
    each_in, each_up = triple // fsdp, hidden // fsdp
    groups_in, groups_up = triple // width, hidden // width
    units = weights.shape[0]
    count = 2 * units
    extra = count
    first_up = groups_in + 1
    first_down = first_up + groups_up
    block = min(256, length)
    steps = length // block
    outer = lax.axis_index("dp")
    inner = lax.axis_index("fsdp")
    z, x, y, c = outer // across, outer % across, inner // cores, inner % cores
    a = (1 - c) * x + c * y
    b = (1 - c) * y + c * x

    def device(zz, xx, yy, cc):
        return (zz * across + xx, yy * cores + cc)

    twin = device(z, x, y, 1 - c)

    def a_peer(k):
        to = (a + k) % side
        return device(z, (1 - c) * to + c * x, (1 - c) * y + c * to, c)

    def b_peer(k):
        to = (b + k) % side
        return device(z, (1 - c) * x + c * to, (1 - c) * to + c * y, c)

    def z_peer(k):
        return device((z + k) % deep, x, y, c)

    barrier = pltpu.get_barrier_semaphore()
    everyone = [twin]
    everyone += [a_peer(k) for k in range(1, side)] + [b_peer(k) for k in range(1, side)]
    everyone += [z_peer(k) for k in range(1, deep)]
    for peer in everyone:
        pl.semaphore_signal(barrier, inc=1, device_id=peer, device_id_type=MESH)
    pl.semaphore_wait(barrier, len(everyone))

    def copy(source, target, send, recv, peer):
        return pltpu.make_async_remote_copy(
            src_ref=source, dst_ref=target, send_sem=send, recv_sem=recv,
            device_id=peer, device_id_type=MESH,
        )

    every = slice(None)

    def view(i, zz, xx, yy, cc):
        lane = yy * cores + cc
        if isinstance(i, int) and i == extra:
            return spread.at[zz, xx, :, pl.ds(pl.multiple_of(lane * 128, 128), 128)]
        return weights.at[
            i // 2, zz, xx, i % 2, :, pl.ds(pl.multiple_of(lane * gw, 128), gw)
        ]

    def own(i):
        if i == extra:
            return vector_shard
        unit_at, half = i // 2, i % 2
        rows = pl.ds(half * piece, piece)
        if unit_at < groups_in:
            return in_shard.at[rows, pl.ds(unit_at * gw, gw)]
        if unit_at < first_up:
            return out_shard.at[rows, :]
        if unit_at < first_down:
            return up_shard.at[rows, pl.ds((unit_at - first_up) * gw, gw)]
        return down_shard.at[pl.ds((unit_at - first_down) * rows_each + half * piece, piece), :]

    def begin(i):
        mine = view(i, z, x, y, c)
        pltpu.make_async_copy(own(i), mine, local.at[i]).start()
        for k in range(1, deep):
            copy(own(i), mine, z_send.at[i, k - 1], z_recv.at[i, k - 1], z_peer(k)).start()

    def first(i):
        mine = view(i, z, x, y, c)
        pltpu.make_async_copy(mine, mine, local.at[i]).wait()
        for k in range(1, deep):
            landed = view(i, (z + deep - k) % deep, x, y, c)
            copy(mine, landed, z_send.at[i, k - 1], z_recv.at[i, k - 1], z_peer(k)).wait()
        line = view(i, every, x, y, c)
        for k in range(1, side):
            copy(line, line, a_send.at[i, k - 1], a_recv.at[i, k - 1], a_peer(k)).start()

    def second(i):
        for k in range(1, side):
            xs = (1 - c) * ((x + side - k) % side) + c * x
            ys = (1 - c) * y + c * ((y + side - k) % side)
            landed = view(i, every, xs, ys, c)
            copy(landed, landed, a_send.at[i, k - 1], a_recv.at[i, k - 1], a_peer(k)).wait()
        for k in range(1, side):
            for s in range(side):
                line = view(i, every, (1 - c) * s + c * x, (1 - c) * y + c * s, c)
                at = (k - 1) * side + s
                copy(line, line, b_send.at[i, at], b_recv.at[i, at], b_peer(k)).start()

    def third(i):
        for k in range(1, side):
            for s in range(side):
                xs = (1 - c) * s + c * ((x + side - k) % side)
                ys = (1 - c) * ((y + side - k) % side) + c * s
                landed = view(i, every, xs, ys, c)
                at = (k - 1) * side + s
                copy(landed, landed, b_send.at[i, at], b_recv.at[i, at], b_peer(k)).wait()
        for s in range(side):
            sheet = view(i, every, every, s, c)
            copy(sheet, sheet, s_send.at[i, s], s_recv.at[i, s], twin).start()

    def fourth(i):
        for s in range(side):
            sheet = view(i, every, every, s, 1 - c)
            copy(sheet, sheet, s_send.at[i, s], s_recv.at[i, s], twin).wait()

    stages = (first, second, third, fourth)
    lag = 2
    last = 3 * lag

    def advance(step):
        for at in reversed(range(4)):
            i = step - lag * at
            if isinstance(step, int):
                if 0 <= i < count:
                    stages[at](i)
            else:
                @pl.when((i >= 0) & (i < count))
                def _(i=i, at=at):
                    stages[at](i)

    def rows_at(m):
        return pl.ds(pl.multiple_of(m * block, block), block)

    def lanes(start, size):
        return pl.ds(start if isinstance(start, int) else pl.multiple_of(start, 128), size)

    def unit_load(at, slot):
        return pltpu.make_async_copy(weights.at[at], loaded.at[slot], load.at[slot])

    def matrix(slot):
        return loaded[slot].reshape(width, width)

    begin(extra)
    for i in range(count):
        begin(i)

    even = lax.broadcasted_iota(jnp.int32, (1, width), 1)
    speed = jnp.exp((even // 2).astype(jnp.float32) * (-2.0 * math.log(10000.0) / width))
    phase = (even % 2).astype(jnp.float32) * (0.5 * math.pi)
    small = min(64, block)
    for at in range(4):
        @pl.loop(0, length // 4 // small)
        def _(s):
            rows = pl.ds(pl.multiple_of(at * (length // 4) + s * small, small), small)
            angle = place[rows, :].astype(jnp.float32) * speed + phase
            stream[rows, :] = frames[rows, :].astype(jnp.float32) + jnp.sin(angle)

        stages[at](extra)
        advance(at)

    group = 128 // (width // devices)
    for tile in range(width // 128):
        found = None
        for owner in range(tile * group, (tile + 1) * group):
            dp_at, f = owner // fsdp, owner % fsdp
            part = spread[dp_at // across, dp_at % across, 0:8, f * 128 : (f + 1) * 128]
            found = part if found is None else found + part
        vectors[:, tile * 128 : (tile + 1) * 128] = found
    group = 128 // (hidden // devices)
    for tile in range(hidden // 128):
        found = None
        for owner in range(tile * group, (tile + 1) * group):
            dp_at, f = owner // fsdp, owner % fsdp
            part = spread[dp_at // across, dp_at % across, 8:16, f * 128 : (f + 1) * 128]
            found = part if found is None else found + part
        tall[:, tile * 128 : (tile + 1) * 128] = found

    def normalize(m, value, row, rate_ref):
        mean = jnp.mean(value, axis=1, keepdims=True)
        centered = value - mean
        rate = lax.rsqrt(jnp.mean(centered * centered, axis=1, keepdims=True) + eps)
        normal = centered * rate
        rate_ref[rows_at(m), :] = jnp.broadcast_to(rate, (block, 128))
        unit[rows_at(m), :] = normal.astype(jnp.bfloat16)
        found = (normal * vectors[row : row + 1, :] + vectors[row + 1 : row + 2, :])
        found = found.astype(jnp.bfloat16)
        normed[rows_at(m), :] = found
        return found

    @pl.loop(0, steps)
    def _(m):
        found = normalize(m, stream[rows_at(m), :], 0, rate_one)
        turned[0, :, rows_at(m)] = found.T

    def keep(source, target, at):
        return pltpu.make_async_copy(source, target, save.at[at])

    keep(unit, unit_one, 0).start()
    keep(turned.at[0], one_hbm, 1).start()
    done = 4
    for g in range(groups_in):
        while done < 2 * g + 2 + last:
            advance(done)
            done += 1
        unit_load(g, g % 2).start()
        unit_load(g, g % 2).wait()

        @pl.loop(0, steps)
        def _(m):
            found = jnp.dot(
                normed[rows_at(m), :], matrix(g % 2), preferred_element_type=jnp.float32
            )
            for f in range(fsdp):
                start = f * each_in + g * gw
                part = found[:, f * gw : (f + 1) * gw]
                if start < width:
                    part = part + vectors[2:3, start : start + gw]
                elif start >= 2 * width:
                    at = start - 2 * width
                    part = part + vectors[3:4, at : at + gw]
                qkv[rows_at(m), start : start + gw] = part.astype(jnp.bfloat16)

    keep(qkv, qkv_hbm, 2).start()
    pairs = width // (2 * HEAD_DIM)
    base = done
    factor = math.log2(math.e) / math.sqrt(HEAD_DIM)
    lane = lax.broadcasted_iota(jnp.int32, (block, 2 * HEAD_DIM), 1)

    @pl.loop(0, pairs)
    def _(j):
        pair = 2 * HEAD_DIM
        at_q = lanes(j * pair, pair)
        at_k = lanes(width + j * pair, pair)
        at_v = lanes(2 * width + j * pair, pair)
        for at in range(steps):
            rows = pl.ds(at * block, block)
            span = (at + 1) * block
            asked = qkv[rows, at_q]
            seen = qkv[pl.ds(0, span), at_k]
            held = qkv[pl.ds(0, span), at_v]
            row = at * block + lax.broadcasted_iota(jnp.int32, (block, span), 0)
            col = lax.broadcasted_iota(jnp.int32, (block, span), 1)
            start = at * block + lax.broadcasted_iota(jnp.int32, (block, 1), 0) - place[rows, :]
            allowed = (col <= row) & (col >= start)
            found = []
            for half in range(2):
                mine = jnp.where((lane // HEAD_DIM) == half, asked, jnp.zeros_like(asked))
                scores = matmul(mine, seen, (1, 1))
                scores = jnp.where(allowed, scores * factor, -1e30)
                weight = jnp.exp2(scores - jnp.max(scores, axis=1, keepdims=True))
                whole = jnp.sum(weight, axis=1, keepdims=True)
                found.append(matmul(weight.astype(jnp.bfloat16), held, (1, 0)) / whole)
            part = jnp.where(lane < HEAD_DIM, found[0], found[1]).astype(jnp.bfloat16)
            mixed[rows, at_q] = part
            turned[1, lanes(j * pair, pair), rows] = part.T
        advance(base + j)

    keep(turned.at[1], mixed_hbm, 3).start()
    unit_load(groups_in, 0).start()
    base = base + pairs
    advance(base)
    keep(unit, unit_one, 0).wait()
    keep(turned.at[0], one_hbm, 1).wait()
    unit_load(groups_in, 0).wait()

    @pl.loop(0, steps)
    def _(m):
        found = jnp.dot(mixed[rows_at(m), :], matrix(0), preferred_element_type=jnp.float32)
        found = stream[rows_at(m), :] + found + vectors[4:5, :]
        stream[rows_at(m), :] = found
        found = normalize(m, found, 5, rate_two)
        turned[0, :, rows_at(m)] = found.T

    keep(unit, unit_two, 0).start()
    keep(turned.at[0], two_hbm, 1).start()
    advance(base + 1)
    base = base + 2

    def turned_rows(slot, g):
        moves = []
        for q in range(width // rows_each):
            f, rest = q * rows_each // gw, q * rows_each % gw
            at = f * each_up + g * gw + rest
            owner, band = at // (groups_up * rows_each), (at // rows_each) % groups_up
            target = pl.multiple_of(band * width + owner * rows_each, 16)
            moves.append(
                pltpu.make_async_copy(
                    turned.at[slot, pl.ds(q * rows_each, rows_each), :],
                    act_hbm.at[pl.ds(target, rows_each), :],
                    save.at[4 + slot],
                )
            )
        return moves

    def turned_done(slot):
        return pltpu.make_async_copy(
            turned.at[slot], act_hbm.at[pl.ds(0, width), :], save.at[4 + slot]
        )

    unit_load(first_up, 0).start()

    @pl.loop(0, groups_up)
    def _(g):
        slot = g % 2
        unit_load(first_up + g, slot).wait()

        @pl.when(g < groups_up - 1)
        def _():
            unit_load(first_up + g + 1, 1 - slot).start()

        @pl.when(g == 0)
        def _():
            keep(turned.at[0], two_hbm, 1).wait()

        @pl.when(g == 1)
        def _():
            keep(turned.at[1], mixed_hbm, 3).wait()

        @pl.when(g >= 2)
        def _():
            turned_done(slot).wait()

        @pl.loop(0, steps)
        def _(m):
            found = jnp.dot(
                normed[rows_at(m), :], matrix(slot), preferred_element_type=jnp.float32
            )
            for f in range(fsdp):
                at = lanes(f * each_up + g * gw, gw)
                pre = found[:, f * gw : (f + 1) * gw] + tall[0:1, at]
                half = 0.5 + 0.5 * lax.erf(pre * math.sqrt(0.5))
                low = (pre * half).astype(jnp.bfloat16)
                act[rows_at(m), at] = low
                bend = half + pre * jnp.exp(-0.5 * pre * pre) * (1.0 / math.sqrt(2.0 * math.pi))
                slope[rows_at(m), at] = bend.astype(jnp.bfloat16)
                turned[slot, pl.ds(f * gw, gw), rows_at(m)] = low.T

        for move in turned_rows(slot, g):
            move.start()
        advance(base + 2 * g)
        advance(base + 1 + 2 * g)

    keep(slope, slope_hbm, 6).start()
    for step in range(base + 2 * groups_up, count + last):
        advance(step)

    def band_load(k, slot):
        moves = []
        for q in range(dp_count):
            owner, at = k * (dp_count // groups_up) + q // groups_up, q % groups_up
            moves.append(
                pltpu.make_async_copy(
                    weights.at[first_down + at, owner // across, owner % across],
                    loaded.at[slot, q // across, q % across],
                    load.at[slot],
                )
            )
        return moves

    for move in band_load(0, 0):
        move.start()

    @pl.loop(0, groups_up)
    def _(k):
        slot = k % 2
        unit_load(0, slot).wait()

        @pl.when(k < groups_up - 1)
        def _():
            for move in band_load(k + 1, 1 - slot):
                move.start()

        @pl.loop(0, steps)
        def _(m):
            stream[rows_at(m), :] += jnp.dot(
                act[rows_at(m), lanes(k * width, width)], matrix(slot),
                preferred_element_type=jnp.float32,
            )

    @pl.loop(0, steps)
    def _(m):
        normed[rows_at(m), :] = (stream[rows_at(m), :] + vectors[7:8, :]).astype(jnp.bfloat16)

    keep(normed, result, 7).start()
    keep(unit, unit_two, 0).wait()
    keep(qkv, qkv_hbm, 2).wait()
    for slot in range(2):
        turned_done(slot).wait()
    keep(slope, slope_hbm, 6).wait()
    keep(normed, result, 7).wait()


def forward(place, frames, vectors, shards):
    dp_count, fsdp_count = lax.axis_size("dp"), lax.axis_size("fsdp")
    dims = grid_of(dp_count, fsdp_count)
    deep, across, down, cores = dims
    assert across == down and cores == 2
    length, width = frames.shape
    triple = shards[0].shape[1] * fsdp_count
    hidden = shards[2].shape[1] * fsdp_count
    piece = width // dp_count // 2
    units = 2 * (hidden // width) + 1 + triple // width
    count = 2 * units
    any_ = pl.BlockSpec(memory_space=pl.ANY)
    vmem = pl.BlockSpec(memory_space=pltpu.VMEM)
    bf16, f32 = jnp.bfloat16, jnp.float32

    def shape(*sizes, kind=bf16):
        return jax.ShapeDtypeStruct(sizes, kind)

    return pl.pallas_call(
        partial(forward_kernel, dims),
        out_shape=[
            shape(length, width),
            shape(units, deep, across, 2, piece, width),
            shape(hidden, length),
            shape(length, hidden),
            shape(width, length),
            shape(length, width),
            shape(length, 128, kind=f32),
            shape(width, length),
            shape(length, triple),
            shape(width, length),
            shape(length, width),
            shape(length, 128, kind=f32),
            shape(8, width, kind=f32),
        ],
        in_specs=[vmem] * 7,
        out_specs=[any_] * 6 + [vmem] + [any_] * 4 + [vmem] * 2,
        scratch_shapes=[
            pltpu.VMEM((deep, across, 16, fsdp_count * 128), f32),
            pltpu.VMEM((8, hidden), f32),
            pltpu.VMEM((length, width), f32),
            pltpu.VMEM((length, width), bf16),
            pltpu.VMEM((length, width), bf16),
            pltpu.VMEM((length, triple), bf16),
            pltpu.VMEM((length, width), bf16),
            pltpu.VMEM((length, hidden), bf16),
            pltpu.VMEM((length, hidden), bf16),
            pltpu.VMEM((2, width, length), bf16),
            pltpu.VMEM((2, deep, across, 2, piece, width), bf16),
            pltpu.SemaphoreType.DMA((2,)),
            pltpu.SemaphoreType.DMA((8,)),
            pltpu.SemaphoreType.DMA((count + 1,)),
            pltpu.SemaphoreType.DMA((count + 1, deep - 1)),
            pltpu.SemaphoreType.DMA((count + 1, deep - 1)),
            pltpu.SemaphoreType.DMA((count + 1, across - 1)),
            pltpu.SemaphoreType.DMA((count + 1, across - 1)),
            pltpu.SemaphoreType.DMA((count + 1, (across - 1) * across)),
            pltpu.SemaphoreType.DMA((count + 1, (across - 1) * across)),
            pltpu.SemaphoreType.DMA((count + 1, down)),
            pltpu.SemaphoreType.DMA((count + 1, down)),
        ],
        compiler_params=pltpu.CompilerParams(
            collective_id=0, has_side_effects=True, vmem_limit_bytes=67043328
        ),
        name="forward",
    )(place, frames, vectors, *shards)


def place_vectors(items, up_bias):
    devices = lax.axis_size("dp") * lax.axis_size("fsdp")
    at = lax.axis_index("dp") * lax.axis_size("fsdp") + lax.axis_index("fsdp")
    lane = jnp.arange(128)

    def placed(rows):
        size = rows.shape[1]
        repeated = jnp.tile(rows.astype(jnp.float32), (1, 128 // size))
        return jnp.where((lane // size == at % (128 // size))[None], repeated, 0.0)

    packed = jnp.stack(items)
    return jnp.concatenate(
        [placed(packed), placed(up_bias[None]), jnp.zeros((7, 128), jnp.float32)]
    )


def matmul(left, right, contract):
    return lax.dot_general(
        left, right, ((contract[:1], contract[1:]), ((), ())), preferred_element_type=jnp.float32
    )


def backward_kernel(dims, *refs):
    (
        place, cot_hbm, act_hbm, slope_hbm, two_hbm, unit_two, rate_two, mixed_hbm, qkv_hbm,
        one_hbm, unit_one, rate_one, gains, weights,
        result, owned, sums,
        grads, twin_in, a_in, b_in, z_in,
        v_own, v_hold, v_twin, v_a, v_b, v_z,
        cot, left, right, unit, wide, total, second, branch,
        load, t_send, t_recv, a_send, a_recv, b_send, b_recv, z_send, z_recv,
        v_send, v_recv,
    ) = refs
    deep, across, down, cores = dims
    side = across
    length, width = cot.shape
    hidden = wide.shape[1]
    piece, gw = owned.shape[1], owned.shape[2]
    fsdp = down * cores
    rows_each = 2 * piece
    outer = lax.axis_index("dp")
    inner = lax.axis_index("fsdp")
    z, x, y, c = outer // across, outer % across, inner // cores, inner % cores
    a = (1 - c) * x + c * y
    b = (1 - c) * y + c * x
    block = min(256, length)
    steps = length // block

    def device(zz, xx, yy, cc):
        return (zz * across + xx, yy * cores + cc)

    twin = device(z, x, y, 1 - c)

    def a_peer(k):
        to = (a + k) % side
        return device(z, (1 - c) * to + c * x, (1 - c) * y + c * to, c)

    def b_peer(k):
        to = (b + k) % side
        return device(z, (1 - c) * x + c * to, (1 - c) * to + c * y, c)

    def z_peer(k):
        return device((z + k) % deep, x, y, c)

    groups_up = hidden // width
    groups_in = qkv_hbm.shape[1] // width
    first_in = 2 * groups_up + 1
    first_up = groups_in + 1
    first_down = first_up + groups_up
    dp_count = deep * across
    barrier = pltpu.get_barrier_semaphore()
    everyone = [twin]
    everyone += [a_peer(k) for k in range(1, side)] + [b_peer(k) for k in range(1, side)]
    everyone += [z_peer(k) for k in range(1, deep)]
    for peer in everyone:
        pl.semaphore_signal(barrier, inc=1, device_id=peer, device_id_type=MESH)
    pl.semaphore_wait(barrier, len(everyone))

    def copy(source, target, send, recv, peer):
        return pltpu.make_async_remote_copy(
            src_ref=source, dst_ref=target, send_sem=send, recv_sem=recv,
            device_id=peer, device_id_type=MESH,
        )

    def t_copy(i):
        return copy(
            grads.at[(i // 2) % 2, i % 2, 1 - c], twin_in.at[i], t_send.at[i], t_recv.at[i], twin
        )

    def a_copy(i, k):
        return copy(
            twin_in.at[i, (a + k) % side], a_in.at[i, k - 1],
            a_send.at[i, k - 1], a_recv.at[i, k - 1], a_peer(k),
        )

    def b_copy(i, k):
        return copy(
            a_in.at[i, 0, (b + k) % side], b_in.at[i, k - 1],
            b_send.at[i, k - 1], b_recv.at[i, k - 1], b_peer(k),
        )

    def z_copy(i, k):
        return copy(
            b_in.at[i, 0, (z + k) % deep], z_in.at[i, k - 1],
            z_send.at[i, k - 1], z_recv.at[i, k - 1], z_peer(k),
        )

    def first(i):
        t_copy(i).start()

    def second_stage(i):
        t_copy(i).wait()
        twin_in[i] = twin_in[i] + grads[(i // 2) % 2, i % 2, c]
        for k in range(1, side):
            a_copy(i, k).start()

    def third(i):
        for k in range(1, side):
            a_copy(i, k).wait()
        found = twin_in[i, a]
        for k in range(1, side):
            found = found + a_in[i, k - 1]
        a_in[i, 0] = found
        for k in range(1, side):
            b_copy(i, k).start()

    def fourth(i):
        for k in range(1, side):
            b_copy(i, k).wait()
        found = a_in[i, 0, b]
        for k in range(1, side):
            found = found + b_in[i, k - 1]
        b_in[i, 0] = found
        for k in range(1, deep):
            z_copy(i, k).start()

    def fifth(i):
        for k in range(1, deep):
            z_copy(i, k).wait()
        found = b_in[i, 0, z].astype(jnp.float32)
        for k in range(1, deep):
            found = found + z_in[i, k - 1].astype(jnp.float32)
        g = i // 2 - first_in
        moved = 2 * ((g + inner) % groups_in - g)
        if isinstance(i, int):
            owned[i + (moved if g >= 0 else 0)] = found
        else:
            owned[i + (i // (2 * first_in)) * moved] = found

    def launch(u):
        for half in range(2):
            first(2 * u + half)

    def settle(u):
        for half in range(2):
            second_stage(2 * u + half)

    stages = (third, fourth, fifth)

    def advance(step, low, high):
        for at in reversed(range(3)):
            i = step - 2 * at
            if isinstance(step, int):
                if low <= i < high:
                    stages[at](i)
            else:
                @pl.when((i >= low) & (i < high))
                def _(i=i, at=at):
                    stages[at](i)

    def fetch(source, target, at):
        return pltpu.make_async_copy(source, target, load.at[at])

    def down_load(j):
        moves = []
        for q in range(dp_count):
            owner, at = j * (dp_count // groups_up) + q // groups_up, q % groups_up
            moves.append(
                fetch(weights.at[first_down + at, pl.ds(2 * owner, 2)], right.at[pl.ds(2 * q, 2)], 2)
            )
        return moves

    def matrix():
        return right[...].reshape(width, width)

    def strips(rows, each, g):
        parts = []
        for f in range(fsdp):
            start = f * each + g * gw
            if not isinstance(start, int):
                start = pl.multiple_of(start, 128)
            parts.append(wide[rows, pl.ds(start, gw)])
        return jnp.concatenate(parts, axis=1)

    def band(ref, j):
        return ref.at[pl.ds(pl.multiple_of(j * width, width), width), :]

    def rows_at(m):
        return pl.ds(pl.multiple_of(m * block, block), block)

    def make_unit(slot, source, strip):
        @pl.loop(0, width // block)
        def _(m):
            lhs = left[rows_at(m), :]
            for f in range(fsdp):
                yy, cc = f // cores, f % cores
                found = matmul(lhs, source[:, pl.ds(strip(f), gw)], (1, 0)).astype(jnp.bfloat16)
                for q in range(block // piece):
                    owner = m * (block // rows_each) + q // 2
                    zz, xx = owner // across, owner % across
                    part = found[q * piece : (q + 1) * piece, :]
                    if cc == 0:
                        grads[slot, q % 2, 0, xx, yy, zz] = part
                    else:
                        grads[slot, q % 2, 1, yy, xx, zz] = part

    def columns(value):
        return jnp.sum(value, axis=0, keepdims=True)

    fetch(cot_hbm, cot, 0).start()
    fetch(band(act_hbm, 0), left, 1).start()
    v_own[...] = jnp.zeros_like(v_own)
    total[...] = jnp.zeros_like(total)
    fetch(cot_hbm, cot, 0).wait()
    for move in down_load(0):
        move.start()
    fetch(slope_hbm, wide, 3).start()

    @pl.loop(0, 4)
    def _(j):
        fetch(band(act_hbm, j), left, 1).wait()
        make_unit(j % 2, cot, lambda f: f * gw)

        @pl.when(j < 3)
        def _():
            fetch(band(act_hbm, (j + 1) % 4), left, 1).start()

        @pl.when(j == 3)
        def _():
            fetch(two_hbm, left, 1).start()

        launch(j)
        fetch(weights.at[0], right, 2).wait()

        @pl.when(j == 0)
        def _():
            fetch(slope_hbm, wide, 3).wait()

        span = pl.ds(pl.multiple_of(j * width, width), width)

        @pl.loop(0, steps)
        def _(m):
            found = matmul(cot[rows_at(m), :], matrix(), (1, 1))
            found = (found * wide[rows_at(m), span].astype(jnp.float32)).astype(jnp.bfloat16)
            wide[rows_at(m), span] = found
            v_own[pl.ds(8 + j, 1), :] += columns(found.astype(jnp.float32))

        @pl.when(j < 3)
        def _():
            for move in down_load((j + 1) % 4):
                move.start()

        @pl.when(j == 3)
        def _():
            fetch(weights.at[first_up], right, 2).start()

        settle(j)
        advance(j - 1, 0, 24)

    fetch(two_hbm, left, 1).wait()
    fetch(unit_two, unit, 4).start()
    each_up = hidden // fsdp

    @pl.loop(0, 4)
    def _(j):
        make_unit(j % 2, wide, lambda f: pl.multiple_of(f * each_up + j * gw, 128))
        launch(4 + j)
        fetch(weights.at[first_up + j], right, 2).wait()

        @pl.loop(0, steps)
        def _(m):
            total[rows_at(m), :] += matmul(strips(rows_at(m), each_up, j), matrix(), (1, 1))

        @pl.when(j < 3)
        def _():
            fetch(weights.at[first_up + (j + 1) % 4], right, 2).start()

        @pl.when(j == 3)
        def _():
            fetch(weights.at[groups_in], right, 2).start()

        settle(4 + j)
        advance(3 + j, 0, 24)

    triple = qkv_hbm.shape[1]
    packed = wide.at[:, pl.ds(0, triple)]
    fetch(mixed_hbm, left, 1).start()
    fetch(qkv_hbm, packed, 3).start()
    fetch(unit_two, unit, 4).wait()

    def norm_back(rate, gain, finish):
        @pl.loop(0, steps)
        def _(m):
            grad = total[rows_at(m), :]
            normal = unit[rows_at(m), :].astype(jnp.float32)
            scaled = grad * gain
            mean = jnp.mean(scaled, axis=1, keepdims=True)
            tilt = jnp.mean(scaled * normal, axis=1, keepdims=True)
            finish(m, grad, normal, rate[rows_at(m), 0:1] * (scaled - mean - normal * tilt))

    def finish_two(m, grad, normal, moved):
        incoming = cot[rows_at(m), :].astype(jnp.float32)
        found = incoming + moved
        second[rows_at(m), :] = found
        low = found.astype(jnp.bfloat16)
        branch[rows_at(m), :] = low
        v_own[4:5, :] += columns(low.astype(jnp.float32))
        v_own[5:6, :] += columns(grad * normal)
        v_own[6:7, :] += columns(grad)
        v_own[7:8, :] += columns(incoming)

    norm_back(rate_two, gains[5:6, :], finish_two)
    advance(7, 0, 24)
    fetch(unit_one, unit, 4).start()
    fetch(mixed_hbm, left, 1).wait()
    make_unit(0, branch, lambda f: f * gw)
    fetch(one_hbm, left, 1).start()
    launch(8)
    fetch(weights.at[groups_in], right, 2).wait()

    @pl.loop(0, steps)
    def _(m):
        found = matmul(branch[rows_at(m), :], matrix(), (1, 1))
        branch[rows_at(m), :] = found.astype(jnp.bfloat16)

    fetch(weights.at[0], right, 2).start()
    settle(8)
    advance(8, 0, 24)
    fetch(qkv_hbm, packed, 3).wait()
    fetch(one_hbm, left, 1).wait()
    pairs = width // (2 * HEAD_DIM)
    each_in = triple // fsdp
    ready = [
        max((f * each_in + (g + f) % groups_in * gw) % width + gw for f in range(fsdp))
        // (2 * HEAD_DIM)
        - 1
        for g in range(groups_in)
    ]
    ready = [max(ready[: g + 1]) for g in range(groups_in)]
    late = ready[0] > 5 or ready[1] > 6
    scale = 1.0 / math.sqrt(HEAD_DIM)
    factor = scale * math.log2(math.e)
    lane = lax.broadcasted_iota(jnp.int32, (block, 2 * HEAD_DIM), 1)

    @pl.loop(0, pairs)
    def _(j):
        pair = 2 * HEAD_DIM
        at_q = pl.ds(pl.multiple_of(j * pair, pair), pair)
        at_k = pl.ds(pl.multiple_of(width + j * pair, pair), pair)
        at_v = pl.ds(pl.multiple_of(2 * width + j * pair, pair), pair)
        sum_q = jnp.zeros((1, pair), jnp.float32)
        for at in range(steps):
            rows = pl.ds(at * block, block)
            span = (at + 1) * block
            asked = wide[rows, at_q]
            given = branch[rows, at_q]
            seen = wide[pl.ds(0, span), at_k]
            held = wide[pl.ds(0, span), at_v]
            seen_t = seen.T
            col = at * block + lax.broadcasted_iota(jnp.int32, (span, block), 1)
            row = lax.broadcasted_iota(jnp.int32, (span, block), 0)
            begin = at * block + lax.broadcasted_iota(jnp.int32, (1, block), 1)
            begin = begin - place[:, pl.ds(at * block, block)]
            allowed = (row <= col) & (row >= begin)
            grad_q = []
            grad_k = None
            grad_v = None
            for half in range(2):
                keep = (lane // HEAD_DIM) == half
                mine = jnp.where(keep, asked, jnp.zeros_like(asked))
                ours = jnp.where(keep, given, jnp.zeros_like(given))
                scores = matmul(seen, mine, (1, 1))
                scores = jnp.where(allowed, scores * factor, -1e30)
                probs = jnp.exp2(scores - jnp.max(scores, axis=0, keepdims=True))
                probs = probs * (1.0 / columns(probs))
                grad_p = matmul(held, ours, (1, 1))
                delta = columns(probs * grad_p)
                grad_s = (probs * (grad_p - delta)).astype(jnp.bfloat16)
                part_v = matmul(probs.astype(jnp.bfloat16), ours, (1, 0))
                part_k = matmul(grad_s, mine, (1, 0))
                grad_q.append(matmul(seen_t[half * HEAD_DIM : (half + 1) * HEAD_DIM, :], grad_s, (1, 0)))
                grad_v = part_v if grad_v is None else grad_v + part_v
                grad_k = part_k if grad_k is None else grad_k + part_k
            found = (jnp.concatenate(grad_q, axis=0) * scale).T.astype(jnp.bfloat16)
            wide[rows, at_q] = found
            sum_q = sum_q + columns(found.astype(jnp.float32))
            if at:
                old = pl.ds(0, at * block)
                total[old, 0:pair] += grad_k[: at * block, :]
                total[old, pair : 2 * pair] += grad_v[: at * block, :]
            total[rows, 0:pair] = grad_k[at * block :, :]
            total[rows, pair : 2 * pair] = grad_v[at * block :, :]
        wide[:, at_k] = (total[:, 0:pair] * scale).astype(jnp.bfloat16)
        low = total[:, pair : 2 * pair].astype(jnp.bfloat16)
        wide[:, at_v] = low
        v_own[2:3, at_q] = sum_q
        v_own[3:4, at_q] = columns(low.astype(jnp.float32))
        for g in range(groups_in):
            tied = g > 0 and ready[g] == ready[g - 1]
            if g and not tied:
                @pl.when(j == ready[g - 1] + 1)
                def _(g=g):
                    settle(8 + g)

            @pl.when(j == ready[g])
            def _(g=g, tied=tied):
                if tied:
                    settle(8 + g)
                make_unit(
                    (9 + g) % 2, wide, lambda f: f * each_in + (g + f) % groups_in * gw
                )
                launch(9 + g)

        step = 9 + (3 * j) // 2
        if late:
            advance(step, 0, 18)
        else:
            advance(step, 0, 24)

        @pl.when(j % 2 == 1)
        def _():
            advance(step + 1, 0, 18 if late else 24)

    total[...] = jnp.zeros_like(total)
    settle(11)
    if late:
        for step in range(18, 21):
            advance(step, 18, 24)
    fetch(unit_one, unit, 4).wait()
    for j in range(3):
        fetch(weights.at[j], right, 2).wait()

        @pl.loop(0, steps)
        def _(m):
            total[rows_at(m), :] += matmul(strips(rows_at(m), each_in, j), matrix(), (1, 1))

        if j < 2:
            fetch(weights.at[j + 1], right, 2).start()
        advance(21 + j, 0, 24)

    def finish_one(m, grad, normal, moved):
        branch[rows_at(m), :] = (second[rows_at(m), :] + moved).astype(jnp.bfloat16)
        v_own[0:1, :] += columns(grad * normal)
        v_own[1:2, :] += columns(grad)

    norm_back(rate_one, gains[0:1, :], finish_one)
    fetch(branch, result, 0).start()

    def small(source, target, at, peer):
        return copy(source, target, v_send.at[at], v_recv.at[at], peer)

    hops = [
        [(v_own, v_twin, 0, twin)],
        [(v_hold.at[0], v_a.at[k - 1], k, a_peer(k)) for k in range(1, side)],
        [(v_hold.at[1], v_b.at[k - 1], side + k - 1, b_peer(k)) for k in range(1, side)],
        [(v_hold.at[2], v_z.at[k - 1], 2 * side + k - 2, z_peer(k)) for k in range(1, deep)],
    ]
    lands = [
        lambda: [v_own[...], v_twin[...]],
        lambda: [v_hold[0]] + [v_a[k] for k in range(side - 1)],
        lambda: [v_hold[1]] + [v_b[k] for k in range(side - 1)],
        lambda: [v_hold[2]] + [v_z[k] for k in range(deep - 1)],
    ]
    for at in range(4):
        for hop in hops[at]:
            small(*hop).start()
        advance(24 + at, 0, 24)
        for hop in hops[at]:
            small(*hop).wait()
        found = lands[at]()
        whole = found[0]
        for item in found[1:]:
            whole = whole + item
        if at < 3:
            v_hold[at] = whole
        else:
            sums[...] = whole
    fetch(branch, result, 0).wait()


def backward(place, cot, act, slope, two, unit_two, rate_two, mixed, qkv, one, unit_one,
             rate_one, gains, weights):
    dp_count, fsdp_count = lax.axis_size("dp"), lax.axis_size("fsdp")
    dims = grid_of(dp_count, fsdp_count)
    deep, across, down, cores = dims
    assert across == down and cores == 2
    length, width = cot.shape
    hidden = slope.shape[1]
    piece = width // dp_count // 2
    gw = width // fsdp_count
    count = 2 * (2 * (hidden // width) + 1 + qkv.shape[1] // width)
    any_ = pl.BlockSpec(memory_space=pl.ANY)
    vmem = pl.BlockSpec(memory_space=pltpu.VMEM)
    bf16, f32 = jnp.bfloat16, jnp.float32
    hops = 2 * side_of(dims) + deep
    return pl.pallas_call(
        partial(backward_kernel, dims),
        out_shape=[
            jax.ShapeDtypeStruct((length, width), bf16),
            jax.ShapeDtypeStruct((count, piece, gw), f32),
            jax.ShapeDtypeStruct((16, width), f32),
        ],
        in_specs=[vmem, any_, any_, any_, any_, any_, vmem, any_, any_, any_, any_, vmem, vmem]
        + [any_],
        out_specs=[any_, vmem, vmem],
        scratch_shapes=[
            pltpu.VMEM((2, 2, 2, across, down, deep, piece, gw), bf16),
            pltpu.VMEM((count, across, down, deep, piece, gw), bf16),
            pltpu.VMEM((count, across - 1, down, deep, piece, gw), bf16),
            pltpu.VMEM((count, down - 1, deep, piece, gw), bf16),
            pltpu.VMEM((count, deep - 1, piece, gw), bf16),
            pltpu.VMEM((16, width), f32),
            pltpu.VMEM((3, 16, width), f32),
            pltpu.VMEM((16, width), f32),
            pltpu.VMEM((across - 1, 16, width), f32),
            pltpu.VMEM((down - 1, 16, width), f32),
            pltpu.VMEM((deep - 1, 16, width), f32),
            pltpu.VMEM((length, width), bf16),
            pltpu.VMEM((width, width), bf16),
            pltpu.VMEM((2 * dp_count, piece, width), bf16),
            pltpu.VMEM((length, width), bf16),
            pltpu.VMEM((length, hidden), bf16),
            pltpu.VMEM((length, width), f32),
            pltpu.VMEM((length, width), f32),
            pltpu.VMEM((length, width), bf16),
            pltpu.SemaphoreType.DMA((5,)),
            pltpu.SemaphoreType.DMA((count,)),
            pltpu.SemaphoreType.DMA((count,)),
            pltpu.SemaphoreType.DMA((count, across - 1)),
            pltpu.SemaphoreType.DMA((count, across - 1)),
            pltpu.SemaphoreType.DMA((count, down - 1)),
            pltpu.SemaphoreType.DMA((count, down - 1)),
            pltpu.SemaphoreType.DMA((count, deep - 1)),
            pltpu.SemaphoreType.DMA((count, deep - 1)),
            pltpu.SemaphoreType.DMA((hops,)),
            pltpu.SemaphoreType.DMA((hops,)),
        ],
        compiler_params=pltpu.CompilerParams(
            collective_id=1, has_side_effects=True, vmem_limit_bytes=67043328
        ),
        name="backward",
    )(place, cot, act, slope, two, unit_two, rate_two, mixed, qkv, one, unit_one, rate_one, gains,
      weights)


def side_of(dims):
    return dims[1]


def pick_grads(owned, sums, width, hidden):
    dp_count, fsdp_count = lax.axis_size("dp"), lax.axis_size("fsdp")
    devices = dp_count * fsdp_count
    at = lax.axis_index("dp") * fsdp_count + lax.axis_index("fsdp")
    count, piece, gw = owned.shape
    bands = hidden // width

    def beside(part):
        groups = part.shape[0] // 2
        part = part.reshape(groups, 2 * piece, gw).transpose(1, 0, 2)
        return part.reshape(2 * piece, groups * gw)

    down = owned[: 2 * bands].reshape(bands * 2 * piece, gw)
    up = beside(owned[2 * bands : 4 * bands])
    out = owned[4 * bands : 4 * bands + 2].reshape(2 * piece, gw)
    qkv = beside(owned[4 * bands + 2 :])
    each = width // devices
    small = lax.dynamic_slice(sums[:8], (0, at * each), (8, each))
    tall = sums[8 : 8 + bands].reshape(hidden)
    tall = lax.dynamic_slice(tall, (at * (hidden // devices),), (hidden // devices,))
    return small, tall, qkv, out, up, down


def body(
    frames,
    segment_ids,
    positions,
    cotangent,
    norm1_gain,
    norm1_shift,
    qkv_weight,
    query_bias,
    value_bias,
    out_weight,
    out_bias,
    norm2_gain,
    norm2_shift,
    up_weight,
    up_bias,
    down_weight,
    down_bias,
):
    length, width = frames.shape
    many = up_weight.shape[1] * lax.axis_size("fsdp")
    vectors = place_vectors(
        [
            norm1_gain,
            norm1_shift,
            query_bias,
            value_bias,
            out_bias,
            norm2_gain,
            norm2_shift,
            down_bias,
        ],
        up_bias,
    )
    (
        output, weights, act, slope, two, unit_two, rate_two, mixed, qkv, one, unit_one, rate_one,
        gains,
    ) = forward(
        positions[0][:, None], frames, vectors, (qkv_weight, out_weight, up_weight, down_weight)
    )
    units, deep, across, halves, piece, _ = weights.shape
    weights = weights.reshape(units, deep * across * halves, piece, width)
    frames_grad, owned, sums = backward(
        positions, cotangent, act, slope, two, unit_two, rate_two, mixed, qkv, one, unit_one,
        rate_one, gains, weights,
    )
    small, tall, qkv_grad, out_grad, up_grad, down_grad = pick_grads(owned, sums, width, many)
    return (
        output,
        frames_grad,
        small[0],
        small[1],
        qkv_grad,
        small[2],
        small[3],
        out_grad,
        small[4],
        small[5],
        small[6],
        up_grad,
        tall,
        down_grad,
        small[7],
    )


def solution(mesh):
    placed = (
        P(("dp", "fsdp"), None),
        P(("dp", "fsdp"), None),
        P(("dp", "fsdp"), None),
        P(("dp", "fsdp"), None),
        P(("dp", "fsdp")),
        P(("dp", "fsdp")),
        P("dp", "fsdp"),
        P(("dp", "fsdp")),
        P(("dp", "fsdp")),
        P("dp", "fsdp"),
        P(("dp", "fsdp")),
        P(("dp", "fsdp")),
        P(("dp", "fsdp")),
        P("dp", "fsdp"),
        P(("dp", "fsdp")),
        P("dp", "fsdp"),
        P(("dp", "fsdp")),
    )
    return jax.shard_map(
        body,
        mesh=mesh,
        in_specs=placed,
        out_specs=(
            P(("dp", "fsdp"), None),
            P(("dp", "fsdp"), None),
            P(("dp", "fsdp")),
            P(("dp", "fsdp")),
            P("dp", "fsdp"),
            P(("dp", "fsdp")),
            P(("dp", "fsdp")),
            P("dp", "fsdp"),
            P(("dp", "fsdp")),
            P(("dp", "fsdp")),
            P(("dp", "fsdp")),
            P("dp", "fsdp"),
            P(("dp", "fsdp")),
            P("dp", "fsdp"),
            P(("dp", "fsdp")),
        ),
        check_vma=False,
    )
```

```python
from functools import partial
import math

import jax
import jax.numpy as jnp
from jax import lax
from jax.experimental import pallas as pl
from jax.experimental.pallas import tpu as pltpu
from jax.sharding import PartitionSpec as P

MESH = pl.DeviceIdType.MESH

HEAD_DIM = 64


eps = 1e-05


def grid_of(dp_count, fsdp_count):
    across = 1
    while across * across * 8 <= dp_count:
        across *= 2
    while dp_count % across:
        across //= 2
    cores = 2 if fsdp_count % 2 == 0 else 1
    return dp_count // across, across, fsdp_count // cores, cores


def forward_kernel(dims, *refs):
    (
        place, frames, vector_shard, in_shard, out_shard, up_shard, down_shard,
        result, weights, act_hbm, slope_hbm, two_hbm, unit_two, rate_two, mixed_hbm, qkv_hbm,
        one_hbm, unit_one, rate_one, vectors,
        spread, tall, stream, normed, unit, qkv, mixed, act, slope, turned, loaded,
        load, save, local, z_send, z_recv, a_send, a_recv, b_send, b_recv, s_send, s_recv,
    ) = refs
    deep, across, down, cores = dims
    side = across
    fsdp = down * cores
    dp_count = deep * across
    devices = dp_count * fsdp
    length, width = stream.shape
    hidden = act.shape[1]
    triple = qkv.shape[1]
    piece = weights.shape[4]
    rows_each = 2 * piece
    gw = width // fsdp
    each_in, each_up = triple // fsdp, hidden // fsdp
    groups_in, groups_up = triple // width, hidden // width
    units = weights.shape[0]
    count = 2 * units
    extra = count
    first_up = groups_in + 1
    first_down = first_up + groups_up
    block = min(256, length)
    steps = length // block
    outer = lax.axis_index("dp")
    inner = lax.axis_index("fsdp")
    z, x, y, c = outer // across, outer % across, inner // cores, inner % cores
    a = (1 - c) * x + c * y
    b = (1 - c) * y + c * x

    def device(zz, xx, yy, cc):
        return (zz * across + xx, yy * cores + cc)

    twin = device(z, x, y, 1 - c)

    def a_peer(k):
        to = (a + k) % side
        return device(z, (1 - c) * to + c * x, (1 - c) * y + c * to, c)

    def b_peer(k):
        to = (b + k) % side
        return device(z, (1 - c) * x + c * to, (1 - c) * to + c * y, c)

    def z_peer(k):
        return device((z + k) % deep, x, y, c)

    barrier = pltpu.get_barrier_semaphore()
    everyone = [twin]
    everyone += [a_peer(k) for k in range(1, side)] + [b_peer(k) for k in range(1, side)]
    everyone += [z_peer(k) for k in range(1, deep)]
    for peer in everyone:
        pl.semaphore_signal(barrier, inc=1, device_id=peer, device_id_type=MESH)
    pl.semaphore_wait(barrier, len(everyone))

    def copy(source, target, send, recv, peer):
        return pltpu.make_async_remote_copy(
            src_ref=source, dst_ref=target, send_sem=send, recv_sem=recv,
            device_id=peer, device_id_type=MESH,
        )

    every = slice(None)

    def view(i, zz, xx, yy, cc):
        lane = yy * cores + cc
        if isinstance(i, int) and i == extra:
            return spread.at[zz, xx, :, pl.ds(pl.multiple_of(lane * 128, 128), 128)]
        return weights.at[
            i // 2, zz, xx, i % 2, :, pl.ds(pl.multiple_of(lane * gw, 128), gw)
        ]

    def own(i):
        if i == extra:
            return vector_shard
        unit_at, half = i // 2, i % 2
        rows = pl.ds(half * piece, piece)
        if unit_at < groups_in:
            return in_shard.at[rows, pl.ds(unit_at * gw, gw)]
        if unit_at < first_up:
            return out_shard.at[rows, :]
        if unit_at < first_down:
            return up_shard.at[rows, pl.ds((unit_at - first_up) * gw, gw)]
        return down_shard.at[pl.ds((unit_at - first_down) * rows_each + half * piece, piece), :]

    def begin(i):
        mine = view(i, z, x, y, c)
        pltpu.make_async_copy(own(i), mine, local.at[i]).start()
        for k in range(1, deep):
            copy(own(i), mine, z_send.at[i, k - 1], z_recv.at[i, k - 1], z_peer(k)).start()

    def first(i):
        mine = view(i, z, x, y, c)
        pltpu.make_async_copy(mine, mine, local.at[i]).wait()
        for k in range(1, deep):
            landed = view(i, (z + deep - k) % deep, x, y, c)
            copy(mine, landed, z_send.at[i, k - 1], z_recv.at[i, k - 1], z_peer(k)).wait()
        line = view(i, every, x, y, c)
        for k in range(1, side):
            copy(line, line, a_send.at[i, k - 1], a_recv.at[i, k - 1], a_peer(k)).start()

    def second(i):
        for k in range(1, side):
            xs = (1 - c) * ((x + side - k) % side) + c * x
            ys = (1 - c) * y + c * ((y + side - k) % side)
            landed = view(i, every, xs, ys, c)
            copy(landed, landed, a_send.at[i, k - 1], a_recv.at[i, k - 1], a_peer(k)).wait()
        for k in range(1, side):
            for s in range(side):
                line = view(i, every, (1 - c) * s + c * x, (1 - c) * y + c * s, c)
                at = (k - 1) * side + s
                copy(line, line, b_send.at[i, at], b_recv.at[i, at], b_peer(k)).start()

    def third(i):
        for k in range(1, side):
            for s in range(side):
                xs = (1 - c) * s + c * ((x + side - k) % side)
                ys = (1 - c) * ((y + side - k) % side) + c * s
                landed = view(i, every, xs, ys, c)
                at = (k - 1) * side + s
                copy(landed, landed, b_send.at[i, at], b_recv.at[i, at], b_peer(k)).wait()
        for s in range(side):
            sheet = view(i, every, every, s, c)
            copy(sheet, sheet, s_send.at[i, s], s_recv.at[i, s], twin).start()

    def fourth(i):
        for s in range(side):
            sheet = view(i, every, every, s, 1 - c)
            copy(sheet, sheet, s_send.at[i, s], s_recv.at[i, s], twin).wait()

    stages = (first, second, third, fourth)
    lags = (0, 2, 5, 7)
    last = lags[3]

    def advance(step):
        for at in reversed(range(4)):
            i = step - lags[at]
            if isinstance(step, int):
                if 0 <= i < count:
                    stages[at](i)
            else:
                @pl.when((i >= 0) & (i < count))
                def _(i=i, at=at):
                    stages[at](i)

    def rows_at(m):
        return pl.ds(pl.multiple_of(m * block, block), block)

    def lanes(start, size):
        return pl.ds(start if isinstance(start, int) else pl.multiple_of(start, 128), size)

    def unit_load(at, slot):
        return pltpu.make_async_copy(weights.at[at], loaded.at[slot], load.at[slot])

    def matrix(slot):
        return loaded[slot].reshape(width, width)

    begin(extra)
    for i in range(count):
        begin(i)

    even = lax.broadcasted_iota(jnp.int32, (1, width), 1)
    speed = jnp.exp((even // 2).astype(jnp.float32) * (-2.0 * math.log(10000.0) / width))
    phase = (even % 2).astype(jnp.float32) * (0.5 * math.pi)
    small = min(64, block)
    for at in range(4):
        @pl.loop(0, length // 4 // small)
        def _(s):
            rows = pl.ds(pl.multiple_of(at * (length // 4) + s * small, small), small)
            angle = place[rows, :].astype(jnp.float32) * speed + phase
            stream[rows, :] = frames[rows, :].astype(jnp.float32) + jnp.sin(angle)

        stages[at](extra)
        advance(at)

    group = 128 // (width // devices)
    for tile in range(width // 128):
        found = None
        for owner in range(tile * group, (tile + 1) * group):
            dp_at, f = owner // fsdp, owner % fsdp
            part = spread[dp_at // across, dp_at % across, 0:8, f * 128 : (f + 1) * 128]
            found = part if found is None else found + part
        vectors[:, tile * 128 : (tile + 1) * 128] = found
    group = 128 // (hidden // devices)
    for tile in range(hidden // 128):
        found = None
        for owner in range(tile * group, (tile + 1) * group):
            dp_at, f = owner // fsdp, owner % fsdp
            part = spread[dp_at // across, dp_at % across, 8:16, f * 128 : (f + 1) * 128]
            found = part if found is None else found + part
        tall[:, tile * 128 : (tile + 1) * 128] = found

    def normalize(m, value, row, rate_ref):
        mean = jnp.mean(value, axis=1, keepdims=True)
        centered = value - mean
        rate = lax.rsqrt(jnp.mean(centered * centered, axis=1, keepdims=True) + eps)
        normal = centered * rate
        rate_ref[rows_at(m), :] = jnp.broadcast_to(rate, (block, 128))
        unit[rows_at(m), :] = normal.astype(jnp.bfloat16)
        found = (normal * vectors[row : row + 1, :] + vectors[row + 1 : row + 2, :])
        found = found.astype(jnp.bfloat16)
        normed[rows_at(m), :] = found
        return found

    @pl.loop(0, steps)
    def _(m):
        found = normalize(m, stream[rows_at(m), :], 0, rate_one)
        turned[0, :, rows_at(m)] = found.T

    def keep(source, target, at):
        return pltpu.make_async_copy(source, target, save.at[at])

    keep(unit, unit_one, 0).start()
    keep(turned.at[0], one_hbm, 1).start()
    done = 4
    for g in range(groups_in):
        while done < 2 * g + 2 + last:
            advance(done)
            done += 1
        unit_load(g, g % 2).start()
        unit_load(g, g % 2).wait()

        @pl.loop(0, steps)
        def _(m):
            found = jnp.dot(
                normed[rows_at(m), :], matrix(g % 2), preferred_element_type=jnp.float32
            )
            for f in range(fsdp):
                start = f * each_in + g * gw
                part = found[:, f * gw : (f + 1) * gw]
                if start < width:
                    part = part + vectors[2:3, start : start + gw]
                elif start >= 2 * width:
                    at = start - 2 * width
                    part = part + vectors[3:4, at : at + gw]
                qkv[rows_at(m), start : start + gw] = part.astype(jnp.bfloat16)

    keep(qkv, qkv_hbm, 2).start()
    pairs = width // (2 * HEAD_DIM)
    base = done
    factor = math.log2(math.e) / math.sqrt(HEAD_DIM)
    lane = lax.broadcasted_iota(jnp.int32, (block, 2 * HEAD_DIM), 1)

    @pl.loop(0, pairs)
    def _(j):
        pair = 2 * HEAD_DIM
        at_q = lanes(j * pair, pair)
        at_k = lanes(width + j * pair, pair)
        at_v = lanes(2 * width + j * pair, pair)
        for at in range(steps):
            rows = pl.ds(at * block, block)
            span = (at + 1) * block
            asked = qkv[rows, at_q]
            seen = qkv[pl.ds(0, span), at_k]
            held = qkv[pl.ds(0, span), at_v]
            row = at * block + lax.broadcasted_iota(jnp.int32, (block, span), 0)
            col = lax.broadcasted_iota(jnp.int32, (block, span), 1)
            start = at * block + lax.broadcasted_iota(jnp.int32, (block, 1), 0) - place[rows, :]
            allowed = (col <= row) & (col >= start)
            found = []
            for half in range(2):
                mine = jnp.where((lane // HEAD_DIM) == half, asked, jnp.zeros_like(asked))
                scores = matmul(mine, seen, (1, 1))
                scores = jnp.where(allowed, scores * factor, -1e30)
                weight = jnp.exp2(scores - jnp.max(scores, axis=1, keepdims=True))
                whole = jnp.sum(weight, axis=1, keepdims=True)
                found.append(matmul(weight.astype(jnp.bfloat16), held, (1, 0)) / whole)
            part = jnp.where(lane < HEAD_DIM, found[0], found[1]).astype(jnp.bfloat16)
            mixed[rows, at_q] = part
            turned[1, lanes(j * pair, pair), rows] = part.T
        advance(base + j)

    keep(turned.at[1], mixed_hbm, 3).start()
    unit_load(groups_in, 0).start()
    base = base + pairs
    advance(base)
    keep(unit, unit_one, 0).wait()
    keep(turned.at[0], one_hbm, 1).wait()
    unit_load(groups_in, 0).wait()

    @pl.loop(0, steps)
    def _(m):
        found = jnp.dot(mixed[rows_at(m), :], matrix(0), preferred_element_type=jnp.float32)
        found = stream[rows_at(m), :] + found + vectors[4:5, :]
        stream[rows_at(m), :] = found
        found = normalize(m, found, 5, rate_two)
        turned[0, :, rows_at(m)] = found.T

    keep(unit, unit_two, 0).start()
    keep(turned.at[0], two_hbm, 1).start()
    advance(base + 1)
    base = base + 2

    def turned_rows(slot, g):
        moves = []
        for q in range(width // rows_each):
            f, rest = q * rows_each // gw, q * rows_each % gw
            at = f * each_up + g * gw + rest
            owner, band = at // (groups_up * rows_each), (at // rows_each) % groups_up
            target = pl.multiple_of(band * width + owner * rows_each, 16)
            moves.append(
                pltpu.make_async_copy(
                    turned.at[slot, pl.ds(q * rows_each, rows_each), :],
                    act_hbm.at[pl.ds(target, rows_each), :],
                    save.at[4 + slot],
                )
            )
        return moves

    def turned_done(slot):
        return pltpu.make_async_copy(
            turned.at[slot], act_hbm.at[pl.ds(0, width), :], save.at[4 + slot]
        )

    unit_load(first_up, 0).start()

    @pl.loop(0, groups_up)
    def _(g):
        slot = g % 2
        unit_load(first_up + g, slot).wait()

        @pl.when(g < groups_up - 1)
        def _():
            unit_load(first_up + g + 1, 1 - slot).start()

        @pl.when(g == 0)
        def _():
            keep(turned.at[0], two_hbm, 1).wait()

        @pl.when(g == 1)
        def _():
            keep(turned.at[1], mixed_hbm, 3).wait()

        @pl.when(g >= 2)
        def _():
            turned_done(slot).wait()

        @pl.loop(0, steps)
        def _(m):
            found = jnp.dot(
                normed[rows_at(m), :], matrix(slot), preferred_element_type=jnp.float32
            )
            for f in range(fsdp):
                at = lanes(f * each_up + g * gw, gw)
                pre = found[:, f * gw : (f + 1) * gw] + tall[0:1, at]
                half = 0.5 + 0.5 * lax.erf(pre * math.sqrt(0.5))
                low = (pre * half).astype(jnp.bfloat16)
                act[rows_at(m), at] = low
                bend = half + pre * jnp.exp(-0.5 * pre * pre) * (1.0 / math.sqrt(2.0 * math.pi))
                slope[rows_at(m), at] = bend.astype(jnp.bfloat16)
                turned[slot, pl.ds(f * gw, gw), rows_at(m)] = low.T

        for move in turned_rows(slot, g):
            move.start()
        advance(base + 2 * g)
        advance(base + 1 + 2 * g)

    keep(slope, slope_hbm, 6).start()
    for step in range(base + 2 * groups_up, count + last):
        advance(step)

    def band_load(k, slot):
        moves = []
        for q in range(dp_count):
            owner, at = k * (dp_count // groups_up) + q // groups_up, q % groups_up
            moves.append(
                pltpu.make_async_copy(
                    weights.at[first_down + at, owner // across, owner % across],
                    loaded.at[slot, q // across, q % across],
                    load.at[slot],
                )
            )
        return moves

    for move in band_load(0, 0):
        move.start()

    @pl.loop(0, groups_up)
    def _(k):
        slot = k % 2
        unit_load(0, slot).wait()

        @pl.when(k < groups_up - 1)
        def _():
            for move in band_load(k + 1, 1 - slot):
                move.start()

        @pl.loop(0, steps)
        def _(m):
            stream[rows_at(m), :] += jnp.dot(
                act[rows_at(m), lanes(k * width, width)], matrix(slot),
                preferred_element_type=jnp.float32,
            )

    @pl.loop(0, steps)
    def _(m):
        normed[rows_at(m), :] = (stream[rows_at(m), :] + vectors[7:8, :]).astype(jnp.bfloat16)

    keep(normed, result, 7).start()
    keep(unit, unit_two, 0).wait()
    keep(qkv, qkv_hbm, 2).wait()
    for slot in range(2):
        turned_done(slot).wait()
    keep(slope, slope_hbm, 6).wait()
    keep(normed, result, 7).wait()


def forward(place, frames, vectors, shards):
    dp_count, fsdp_count = lax.axis_size("dp"), lax.axis_size("fsdp")
    dims = grid_of(dp_count, fsdp_count)
    deep, across, down, cores = dims
    assert across == down and cores == 2
    length, width = frames.shape
    triple = shards[0].shape[1] * fsdp_count
    hidden = shards[2].shape[1] * fsdp_count
    piece = width // dp_count // 2
    units = 2 * (hidden // width) + 1 + triple // width
    count = 2 * units
    any_ = pl.BlockSpec(memory_space=pl.ANY)
    vmem = pl.BlockSpec(memory_space=pltpu.VMEM)
    bf16, f32 = jnp.bfloat16, jnp.float32

    def shape(*sizes, kind=bf16):
        return jax.ShapeDtypeStruct(sizes, kind)

    return pl.pallas_call(
        partial(forward_kernel, dims),
        out_shape=[
            shape(length, width),
            shape(units, deep, across, 2, piece, width),
            shape(hidden, length),
            shape(length, hidden),
            shape(width, length),
            shape(length, width),
            shape(length, 128, kind=f32),
            shape(width, length),
            shape(length, triple),
            shape(width, length),
            shape(length, width),
            shape(length, 128, kind=f32),
            shape(8, width, kind=f32),
        ],
        in_specs=[vmem] * 7,
        out_specs=[any_] * 6 + [vmem] + [any_] * 4 + [vmem] * 2,
        scratch_shapes=[
            pltpu.VMEM((deep, across, 16, fsdp_count * 128), f32),
            pltpu.VMEM((8, hidden), f32),
            pltpu.VMEM((length, width), f32),
            pltpu.VMEM((length, width), bf16),
            pltpu.VMEM((length, width), bf16),
            pltpu.VMEM((length, triple), bf16),
            pltpu.VMEM((length, width), bf16),
            pltpu.VMEM((length, hidden), bf16),
            pltpu.VMEM((length, hidden), bf16),
            pltpu.VMEM((2, width, length), bf16),
            pltpu.VMEM((2, deep, across, 2, piece, width), bf16),
            pltpu.SemaphoreType.DMA((2,)),
            pltpu.SemaphoreType.DMA((8,)),
            pltpu.SemaphoreType.DMA((count + 1,)),
            pltpu.SemaphoreType.DMA((count + 1, deep - 1)),
            pltpu.SemaphoreType.DMA((count + 1, deep - 1)),
            pltpu.SemaphoreType.DMA((count + 1, across - 1)),
            pltpu.SemaphoreType.DMA((count + 1, across - 1)),
            pltpu.SemaphoreType.DMA((count + 1, (across - 1) * across)),
            pltpu.SemaphoreType.DMA((count + 1, (across - 1) * across)),
            pltpu.SemaphoreType.DMA((count + 1, down)),
            pltpu.SemaphoreType.DMA((count + 1, down)),
        ],
        compiler_params=pltpu.CompilerParams(
            collective_id=0, has_side_effects=True, vmem_limit_bytes=67043328
        ),
        name="forward",
    )(place, frames, vectors, *shards)


def place_vectors(items, up_bias):
    devices = lax.axis_size("dp") * lax.axis_size("fsdp")
    at = lax.axis_index("dp") * lax.axis_size("fsdp") + lax.axis_index("fsdp")
    lane = jnp.arange(128)

    def placed(rows):
        size = rows.shape[1]
        repeated = jnp.tile(rows.astype(jnp.float32), (1, 128 // size))
        return jnp.where((lane // size == at % (128 // size))[None], repeated, 0.0)

    packed = jnp.stack(items)
    return jnp.concatenate(
        [placed(packed), placed(up_bias[None]), jnp.zeros((7, 128), jnp.float32)]
    )


def matmul(left, right, contract):
    return lax.dot_general(
        left, right, ((contract[:1], contract[1:]), ((), ())), preferred_element_type=jnp.float32
    )


def backward_kernel(dims, *refs):
    (
        place, cot_hbm, act_hbm, slope_hbm, two_hbm, unit_two, rate_two, mixed_hbm, qkv_hbm,
        one_hbm, unit_one, rate_one, gains, weights,
        result, owned, sums,
        grads, twin_in, a_in, b_in, z_in,
        v_own, v_hold, v_twin, v_a, v_b, v_z,
        cot, left, right, unit, wide, total, second, branch,
        load, t_send, t_recv, a_send, a_recv, b_send, b_recv, z_send, z_recv,
        v_send, v_recv,
    ) = refs
    deep, across, down, cores = dims
    side = across
    length, width = cot.shape
    hidden = wide.shape[1]
    piece, gw = owned.shape[1], owned.shape[2]
    fsdp = down * cores
    rows_each = 2 * piece
    outer = lax.axis_index("dp")
    inner = lax.axis_index("fsdp")
    z, x, y, c = outer // across, outer % across, inner // cores, inner % cores
    a = (1 - c) * x + c * y
    b = (1 - c) * y + c * x
    block = min(256, length)
    steps = length // block

    def device(zz, xx, yy, cc):
        return (zz * across + xx, yy * cores + cc)

    twin = device(z, x, y, 1 - c)

    def a_peer(k):
        to = (a + k) % side
        return device(z, (1 - c) * to + c * x, (1 - c) * y + c * to, c)

    def b_peer(k):
        to = (b + k) % side
        return device(z, (1 - c) * x + c * to, (1 - c) * to + c * y, c)

    def z_peer(k):
        return device((z + k) % deep, x, y, c)

    groups_up = hidden // width
    groups_in = qkv_hbm.shape[1] // width
    first_in = 2 * groups_up + 1
    first_up = groups_in + 1
    first_down = first_up + groups_up
    dp_count = deep * across
    barrier = pltpu.get_barrier_semaphore()
    everyone = [twin]
    everyone += [a_peer(k) for k in range(1, side)] + [b_peer(k) for k in range(1, side)]
    everyone += [z_peer(k) for k in range(1, deep)]
    for peer in everyone:
        pl.semaphore_signal(barrier, inc=1, device_id=peer, device_id_type=MESH)
    pl.semaphore_wait(barrier, len(everyone))

    def copy(source, target, send, recv, peer):
        return pltpu.make_async_remote_copy(
            src_ref=source, dst_ref=target, send_sem=send, recv_sem=recv,
            device_id=peer, device_id_type=MESH,
        )

    def t_copy(i):
        return copy(
            grads.at[(i // 2) % 2, i % 2, 1 - c], twin_in.at[i], t_send.at[i], t_recv.at[i], twin
        )

    def a_copy(i, k):
        return copy(
            twin_in.at[i, (a + k) % side], a_in.at[i, k - 1],
            a_send.at[i, k - 1], a_recv.at[i, k - 1], a_peer(k),
        )

    def b_copy(i, k):
        return copy(
            a_in.at[i, 0, (b + k) % side], b_in.at[i, k - 1],
            b_send.at[i, k - 1], b_recv.at[i, k - 1], b_peer(k),
        )

    def z_copy(i, k):
        return copy(
            b_in.at[i, 0, (z + k) % deep], z_in.at[i, k - 1],
            z_send.at[i, k - 1], z_recv.at[i, k - 1], z_peer(k),
        )

    def first(i):
        t_copy(i).start()

    def second_stage(i):
        t_copy(i).wait()
        twin_in[i] = twin_in[i] + grads[(i // 2) % 2, i % 2, c]
        for k in range(1, side):
            a_copy(i, k).start()

    def third(i):
        for k in range(1, side):
            a_copy(i, k).wait()
        found = twin_in[i, a]
        for k in range(1, side):
            found = found + a_in[i, k - 1]
        a_in[i, 0] = found
        for k in range(1, side):
            b_copy(i, k).start()

    def fourth(i):
        for k in range(1, side):
            b_copy(i, k).wait()
        found = a_in[i, 0, b]
        for k in range(1, side):
            found = found + b_in[i, k - 1]
        b_in[i, 0] = found
        for k in range(1, deep):
            z_copy(i, k).start()

    def fifth(i):
        for k in range(1, deep):
            z_copy(i, k).wait()
        found = b_in[i, 0, z].astype(jnp.float32)
        for k in range(1, deep):
            found = found + z_in[i, k - 1].astype(jnp.float32)
        g = i // 2 - first_in
        moved = 2 * ((g + inner) % groups_in - g)
        if isinstance(i, int):
            owned[i + (moved if g >= 0 else 0)] = found
        else:
            owned[i + (i // (2 * first_in)) * moved] = found

    def launch(u):
        for half in range(2):
            first(2 * u + half)

    def settle(u):
        for half in range(2):
            second_stage(2 * u + half)

    stages = (third, fourth, fifth)

    def advance(step, low, high):
        for at in reversed(range(3)):
            i = step - 2 * at
            if isinstance(step, int):
                if low <= i < high:
                    stages[at](i)
            else:
                @pl.when((i >= low) & (i < high))
                def _(i=i, at=at):
                    stages[at](i)

    def fetch(source, target, at):
        return pltpu.make_async_copy(source, target, load.at[at])

    def down_load(j):
        moves = []
        for q in range(dp_count):
            owner, at = j * (dp_count // groups_up) + q // groups_up, q % groups_up
            moves.append(
                fetch(weights.at[first_down + at, pl.ds(2 * owner, 2)], right.at[pl.ds(2 * q, 2)], 2)
            )
        return moves

    def matrix():
        return right[...].reshape(width, width)

    def strips(rows, each, g):
        parts = []
        for f in range(fsdp):
            start = f * each + g * gw
            if not isinstance(start, int):
                start = pl.multiple_of(start, 128)
            parts.append(wide[rows, pl.ds(start, gw)])
        return jnp.concatenate(parts, axis=1)

    def band(ref, j):
        return ref.at[pl.ds(pl.multiple_of(j * width, width), width), :]

    def rows_at(m):
        return pl.ds(pl.multiple_of(m * block, block), block)

    def make_unit(slot, source, strip):
        @pl.loop(0, width // block)
        def _(m):
            lhs = left[rows_at(m), :]
            for f in range(fsdp):
                yy, cc = f // cores, f % cores
                found = matmul(lhs, source[:, pl.ds(strip(f), gw)], (1, 0)).astype(jnp.bfloat16)
                for q in range(block // piece):
                    owner = m * (block // rows_each) + q // 2
                    zz, xx = owner // across, owner % across
                    part = found[q * piece : (q + 1) * piece, :]
                    if cc == 0:
                        grads[slot, q % 2, 0, xx, yy, zz] = part
                    else:
                        grads[slot, q % 2, 1, yy, xx, zz] = part

    def columns(value):
        return jnp.sum(value, axis=0, keepdims=True)

    fetch(cot_hbm, cot, 0).start()
    fetch(band(act_hbm, 0), left, 1).start()
    v_own[...] = jnp.zeros_like(v_own)
    total[...] = jnp.zeros_like(total)
    fetch(cot_hbm, cot, 0).wait()
    for move in down_load(0):
        move.start()
    fetch(slope_hbm, wide, 3).start()

    @pl.loop(0, 4)
    def _(j):
        fetch(band(act_hbm, j), left, 1).wait()
        make_unit(j % 2, cot, lambda f: f * gw)

        @pl.when(j < 3)
        def _():
            fetch(band(act_hbm, (j + 1) % 4), left, 1).start()

        @pl.when(j == 3)
        def _():
            fetch(two_hbm, left, 1).start()

        launch(j)
        fetch(weights.at[0], right, 2).wait()

        @pl.when(j == 0)
        def _():
            fetch(slope_hbm, wide, 3).wait()

        span = pl.ds(pl.multiple_of(j * width, width), width)

        @pl.loop(0, steps)
        def _(m):
            found = matmul(cot[rows_at(m), :], matrix(), (1, 1))
            found = (found * wide[rows_at(m), span].astype(jnp.float32)).astype(jnp.bfloat16)
            wide[rows_at(m), span] = found
            v_own[pl.ds(8 + j, 1), :] += columns(found.astype(jnp.float32))

        @pl.when(j < 3)
        def _():
            for move in down_load((j + 1) % 4):
                move.start()

        @pl.when(j == 3)
        def _():
            fetch(weights.at[first_up], right, 2).start()

        settle(j)
        advance(j - 1, 0, 24)

    fetch(two_hbm, left, 1).wait()
    fetch(unit_two, unit, 4).start()
    each_up = hidden // fsdp

    @pl.loop(0, 4)
    def _(j):
        make_unit(j % 2, wide, lambda f: pl.multiple_of(f * each_up + j * gw, 128))
        launch(4 + j)
        fetch(weights.at[first_up + j], right, 2).wait()

        @pl.loop(0, steps)
        def _(m):
            total[rows_at(m), :] += matmul(strips(rows_at(m), each_up, j), matrix(), (1, 1))

        @pl.when(j < 3)
        def _():
            fetch(weights.at[first_up + (j + 1) % 4], right, 2).start()

        @pl.when(j == 3)
        def _():
            fetch(weights.at[groups_in], right, 2).start()

        settle(4 + j)
        advance(3 + j, 0, 24)

    triple = qkv_hbm.shape[1]
    packed = wide.at[:, pl.ds(0, triple)]
    fetch(mixed_hbm, left, 1).start()
    fetch(qkv_hbm, packed, 3).start()
    fetch(unit_two, unit, 4).wait()

    def norm_back(rate, gain, finish):
        @pl.loop(0, steps)
        def _(m):
            grad = total[rows_at(m), :]
            normal = unit[rows_at(m), :].astype(jnp.float32)
            scaled = grad * gain
            mean = jnp.mean(scaled, axis=1, keepdims=True)
            tilt = jnp.mean(scaled * normal, axis=1, keepdims=True)
            finish(m, grad, normal, rate[rows_at(m), 0:1] * (scaled - mean - normal * tilt))

    def finish_two(m, grad, normal, moved):
        incoming = cot[rows_at(m), :].astype(jnp.float32)
        found = incoming + moved
        second[rows_at(m), :] = found
        low = found.astype(jnp.bfloat16)
        branch[rows_at(m), :] = low
        v_own[4:5, :] += columns(low.astype(jnp.float32))
        v_own[5:6, :] += columns(grad * normal)
        v_own[6:7, :] += columns(grad)
        v_own[7:8, :] += columns(incoming)

    norm_back(rate_two, gains[5:6, :], finish_two)
    advance(7, 0, 24)
    fetch(unit_one, unit, 4).start()
    fetch(mixed_hbm, left, 1).wait()
    make_unit(0, branch, lambda f: f * gw)
    fetch(one_hbm, left, 1).start()
    launch(8)
    fetch(weights.at[groups_in], right, 2).wait()

    @pl.loop(0, steps)
    def _(m):
        found = matmul(branch[rows_at(m), :], matrix(), (1, 1))
        branch[rows_at(m), :] = found.astype(jnp.bfloat16)

    fetch(weights.at[0], right, 2).start()
    settle(8)
    advance(8, 0, 24)
    fetch(qkv_hbm, packed, 3).wait()
    fetch(one_hbm, left, 1).wait()
    pairs = width // (2 * HEAD_DIM)
    each_in = triple // fsdp
    ready = [
        max((f * each_in + (g + f) % groups_in * gw) % width + gw for f in range(fsdp))
        // (2 * HEAD_DIM)
        - 1
        for g in range(groups_in)
    ]
    ready = [max(ready[: g + 1]) for g in range(groups_in)]
    late = ready[0] > 5 or ready[1] > 6
    scale = 1.0 / math.sqrt(HEAD_DIM)
    factor = scale * math.log2(math.e)
    lane = lax.broadcasted_iota(jnp.int32, (block, 2 * HEAD_DIM), 1)

    @pl.loop(0, pairs)
    def _(j):
        pair = 2 * HEAD_DIM
        at_q = pl.ds(pl.multiple_of(j * pair, pair), pair)
        at_k = pl.ds(pl.multiple_of(width + j * pair, pair), pair)
        at_v = pl.ds(pl.multiple_of(2 * width + j * pair, pair), pair)
        sum_q = jnp.zeros((1, pair), jnp.float32)
        for at in range(steps):
            rows = pl.ds(at * block, block)
            span = (at + 1) * block
            asked = wide[rows, at_q]
            given = branch[rows, at_q]
            seen = wide[pl.ds(0, span), at_k]
            held = wide[pl.ds(0, span), at_v]
            seen_t = seen.T
            col = at * block + lax.broadcasted_iota(jnp.int32, (span, block), 1)
            row = lax.broadcasted_iota(jnp.int32, (span, block), 0)
            begin = at * block + lax.broadcasted_iota(jnp.int32, (1, block), 1)
            begin = begin - place[:, pl.ds(at * block, block)]
            allowed = (row <= col) & (row >= begin)
            grad_q = []
            grad_k = None
            grad_v = None
            for half in range(2):
                keep = (lane // HEAD_DIM) == half
                mine = jnp.where(keep, asked, jnp.zeros_like(asked))
                ours = jnp.where(keep, given, jnp.zeros_like(given))
                scores = matmul(seen, mine, (1, 1))
                scores = jnp.where(allowed, scores * factor, -1e30)
                probs = jnp.exp2(scores - jnp.max(scores, axis=0, keepdims=True))
                probs = probs * (1.0 / columns(probs))
                grad_p = matmul(held, ours, (1, 1))
                delta = columns(probs * grad_p)
                grad_s = (probs * (grad_p - delta)).astype(jnp.bfloat16)
                part_v = matmul(probs.astype(jnp.bfloat16), ours, (1, 0))
                part_k = matmul(grad_s, mine, (1, 0))
                grad_q.append(matmul(seen_t[half * HEAD_DIM : (half + 1) * HEAD_DIM, :], grad_s, (1, 0)))
                grad_v = part_v if grad_v is None else grad_v + part_v
                grad_k = part_k if grad_k is None else grad_k + part_k
            found = (jnp.concatenate(grad_q, axis=0) * scale).T.astype(jnp.bfloat16)
            wide[rows, at_q] = found
            sum_q = sum_q + columns(found.astype(jnp.float32))
            if at:
                old = pl.ds(0, at * block)
                total[old, 0:pair] += grad_k[: at * block, :]
                total[old, pair : 2 * pair] += grad_v[: at * block, :]
            total[rows, 0:pair] = grad_k[at * block :, :]
            total[rows, pair : 2 * pair] = grad_v[at * block :, :]
        wide[:, at_k] = (total[:, 0:pair] * scale).astype(jnp.bfloat16)
        low = total[:, pair : 2 * pair].astype(jnp.bfloat16)
        wide[:, at_v] = low
        v_own[2:3, at_q] = sum_q
        v_own[3:4, at_q] = columns(low.astype(jnp.float32))
        for g in range(groups_in):
            tied = g > 0 and ready[g] == ready[g - 1]
            if g and not tied:
                @pl.when(j == ready[g - 1] + 1)
                def _(g=g):
                    settle(8 + g)

            @pl.when(j == ready[g])
            def _(g=g, tied=tied):
                if tied:
                    settle(8 + g)
                make_unit(
                    (9 + g) % 2, wide, lambda f: f * each_in + (g + f) % groups_in * gw
                )
                launch(9 + g)

        step = 9 + (3 * j) // 2
        if late:
            advance(step, 0, 18)
        else:
            advance(step, 0, 24)

        @pl.when(j % 2 == 1)
        def _():
            advance(step + 1, 0, 18 if late else 24)

    total[...] = jnp.zeros_like(total)
    settle(11)
    if late:
        for step in range(18, 21):
            advance(step, 18, 24)
    fetch(unit_one, unit, 4).wait()
    for j in range(3):
        fetch(weights.at[j], right, 2).wait()

        @pl.loop(0, steps)
        def _(m):
            total[rows_at(m), :] += matmul(strips(rows_at(m), each_in, j), matrix(), (1, 1))

        if j < 2:
            fetch(weights.at[j + 1], right, 2).start()
        advance(21 + j, 0, 24)

    def finish_one(m, grad, normal, moved):
        branch[rows_at(m), :] = (second[rows_at(m), :] + moved).astype(jnp.bfloat16)
        v_own[0:1, :] += columns(grad * normal)
        v_own[1:2, :] += columns(grad)

    norm_back(rate_one, gains[0:1, :], finish_one)
    fetch(branch, result, 0).start()

    def small(source, target, at, peer):
        return copy(source, target, v_send.at[at], v_recv.at[at], peer)

    hops = [
        [(v_own, v_twin, 0, twin)],
        [(v_hold.at[0], v_a.at[k - 1], k, a_peer(k)) for k in range(1, side)],
        [(v_hold.at[1], v_b.at[k - 1], side + k - 1, b_peer(k)) for k in range(1, side)],
        [(v_hold.at[2], v_z.at[k - 1], 2 * side + k - 2, z_peer(k)) for k in range(1, deep)],
    ]
    lands = [
        lambda: [v_own[...], v_twin[...]],
        lambda: [v_hold[0]] + [v_a[k] for k in range(side - 1)],
        lambda: [v_hold[1]] + [v_b[k] for k in range(side - 1)],
        lambda: [v_hold[2]] + [v_z[k] for k in range(deep - 1)],
    ]
    for at in range(4):
        for hop in hops[at]:
            small(*hop).start()
        advance(24 + at, 0, 24)
        for hop in hops[at]:
            small(*hop).wait()
        found = lands[at]()
        whole = found[0]
        for item in found[1:]:
            whole = whole + item
        if at < 3:
            v_hold[at] = whole
        else:
            sums[...] = whole
    fetch(branch, result, 0).wait()


def backward(place, cot, act, slope, two, unit_two, rate_two, mixed, qkv, one, unit_one,
             rate_one, gains, weights):
    dp_count, fsdp_count = lax.axis_size("dp"), lax.axis_size("fsdp")
    dims = grid_of(dp_count, fsdp_count)
    deep, across, down, cores = dims
    assert across == down and cores == 2
    length, width = cot.shape
    hidden = slope.shape[1]
    piece = width // dp_count // 2
    gw = width // fsdp_count
    count = 2 * (2 * (hidden // width) + 1 + qkv.shape[1] // width)
    any_ = pl.BlockSpec(memory_space=pl.ANY)
    vmem = pl.BlockSpec(memory_space=pltpu.VMEM)
    bf16, f32 = jnp.bfloat16, jnp.float32
    hops = 2 * side_of(dims) + deep
    return pl.pallas_call(
        partial(backward_kernel, dims),
        out_shape=[
            jax.ShapeDtypeStruct((length, width), bf16),
            jax.ShapeDtypeStruct((count, piece, gw), f32),
            jax.ShapeDtypeStruct((16, width), f32),
        ],
        in_specs=[vmem, any_, any_, any_, any_, any_, vmem, any_, any_, any_, any_, vmem, vmem]
        + [any_],
        out_specs=[any_, vmem, vmem],
        scratch_shapes=[
            pltpu.VMEM((2, 2, 2, across, down, deep, piece, gw), bf16),
            pltpu.VMEM((count, across, down, deep, piece, gw), bf16),
            pltpu.VMEM((count, across - 1, down, deep, piece, gw), bf16),
            pltpu.VMEM((count, down - 1, deep, piece, gw), bf16),
            pltpu.VMEM((count, deep - 1, piece, gw), bf16),
            pltpu.VMEM((16, width), f32),
            pltpu.VMEM((3, 16, width), f32),
            pltpu.VMEM((16, width), f32),
            pltpu.VMEM((across - 1, 16, width), f32),
            pltpu.VMEM((down - 1, 16, width), f32),
            pltpu.VMEM((deep - 1, 16, width), f32),
            pltpu.VMEM((length, width), bf16),
            pltpu.VMEM((width, width), bf16),
            pltpu.VMEM((2 * dp_count, piece, width), bf16),
            pltpu.VMEM((length, width), bf16),
            pltpu.VMEM((length, hidden), bf16),
            pltpu.VMEM((length, width), f32),
            pltpu.VMEM((length, width), f32),
            pltpu.VMEM((length, width), bf16),
            pltpu.SemaphoreType.DMA((5,)),
            pltpu.SemaphoreType.DMA((count,)),
            pltpu.SemaphoreType.DMA((count,)),
            pltpu.SemaphoreType.DMA((count, across - 1)),
            pltpu.SemaphoreType.DMA((count, across - 1)),
            pltpu.SemaphoreType.DMA((count, down - 1)),
            pltpu.SemaphoreType.DMA((count, down - 1)),
            pltpu.SemaphoreType.DMA((count, deep - 1)),
            pltpu.SemaphoreType.DMA((count, deep - 1)),
            pltpu.SemaphoreType.DMA((hops,)),
            pltpu.SemaphoreType.DMA((hops,)),
        ],
        compiler_params=pltpu.CompilerParams(
            collective_id=1, has_side_effects=True, vmem_limit_bytes=67043328
        ),
        name="backward",
    )(place, cot, act, slope, two, unit_two, rate_two, mixed, qkv, one, unit_one, rate_one, gains,
      weights)


def side_of(dims):
    return dims[1]


def pick_grads(owned, sums, width, hidden):
    dp_count, fsdp_count = lax.axis_size("dp"), lax.axis_size("fsdp")
    devices = dp_count * fsdp_count
    at = lax.axis_index("dp") * fsdp_count + lax.axis_index("fsdp")
    count, piece, gw = owned.shape
    bands = hidden // width

    def beside(part):
        groups = part.shape[0] // 2
        part = part.reshape(groups, 2 * piece, gw).transpose(1, 0, 2)
        return part.reshape(2 * piece, groups * gw)

    down = owned[: 2 * bands].reshape(bands * 2 * piece, gw)
    up = beside(owned[2 * bands : 4 * bands])
    out = owned[4 * bands : 4 * bands + 2].reshape(2 * piece, gw)
    qkv = beside(owned[4 * bands + 2 :])
    each = width // devices
    small = lax.dynamic_slice(sums[:8], (0, at * each), (8, each))
    tall = sums[8 : 8 + bands].reshape(hidden)
    tall = lax.dynamic_slice(tall, (at * (hidden // devices),), (hidden // devices,))
    return small, tall, qkv, out, up, down


def body(
    frames,
    segment_ids,
    positions,
    cotangent,
    norm1_gain,
    norm1_shift,
    qkv_weight,
    query_bias,
    value_bias,
    out_weight,
    out_bias,
    norm2_gain,
    norm2_shift,
    up_weight,
    up_bias,
    down_weight,
    down_bias,
):
    length, width = frames.shape
    many = up_weight.shape[1] * lax.axis_size("fsdp")
    vectors = place_vectors(
        [
            norm1_gain,
            norm1_shift,
            query_bias,
            value_bias,
            out_bias,
            norm2_gain,
            norm2_shift,
            down_bias,
        ],
        up_bias,
    )
    (
        output, weights, act, slope, two, unit_two, rate_two, mixed, qkv, one, unit_one, rate_one,
        gains,
    ) = forward(
        positions[0][:, None], frames, vectors, (qkv_weight, out_weight, up_weight, down_weight)
    )
    units, deep, across, halves, piece, _ = weights.shape
    weights = weights.reshape(units, deep * across * halves, piece, width)
    frames_grad, owned, sums = backward(
        positions, cotangent, act, slope, two, unit_two, rate_two, mixed, qkv, one, unit_one,
        rate_one, gains, weights,
    )
    small, tall, qkv_grad, out_grad, up_grad, down_grad = pick_grads(owned, sums, width, many)
    return (
        output,
        frames_grad,
        small[0],
        small[1],
        qkv_grad,
        small[2],
        small[3],
        out_grad,
        small[4],
        small[5],
        small[6],
        up_grad,
        tall,
        down_grad,
        small[7],
    )


def solution(mesh):
    placed = (
        P(("dp", "fsdp"), None),
        P(("dp", "fsdp"), None),
        P(("dp", "fsdp"), None),
        P(("dp", "fsdp"), None),
        P(("dp", "fsdp")),
        P(("dp", "fsdp")),
        P("dp", "fsdp"),
        P(("dp", "fsdp")),
        P(("dp", "fsdp")),
        P("dp", "fsdp"),
        P(("dp", "fsdp")),
        P(("dp", "fsdp")),
        P(("dp", "fsdp")),
        P("dp", "fsdp"),
        P(("dp", "fsdp")),
        P("dp", "fsdp"),
        P(("dp", "fsdp")),
    )
    return jax.shard_map(
        body,
        mesh=mesh,
        in_specs=placed,
        out_specs=(
            P(("dp", "fsdp"), None),
            P(("dp", "fsdp"), None),
            P(("dp", "fsdp")),
            P(("dp", "fsdp")),
            P("dp", "fsdp"),
            P(("dp", "fsdp")),
            P(("dp", "fsdp")),
            P("dp", "fsdp"),
            P(("dp", "fsdp")),
            P(("dp", "fsdp")),
            P(("dp", "fsdp")),
            P("dp", "fsdp"),
            P(("dp", "fsdp")),
            P("dp", "fsdp"),
            P(("dp", "fsdp")),
        ),
        check_vma=False,
    )
```
